32 devices in a mesh: group: 2 (over y), tm: 4 (over z), height: 2 (over x), width: 2 (over core).
Axes of the slice: x: 2, y: 2, z: 4, core: 2. Of those that a mesh axis runs over, the one named last changes fastest.
Arguments:
- queries: bfloat16 [8, 16, 32, 1120], P(('group', 'tm'), 'height', 'width'), parts along dimension 0, may hold values from -5 to 5
- attn_keys: bfloat16 [8, 16, 32, 1120], P(('group', 'tm'), 'height', 'width'), parts along dimension 0, may hold values from -40 to 40
- attn_values: bfloat16 [8, 16, 32, 1120], P(('group', 'tm'), 'height', 'width'), parts along dimension 0, may hold values from -7 to 7
- attn_cotangent: bfloat16 [8, 16, 32, 1120], P(('group', 'tm'), 'height', 'width'), parts along dimension 0, may hold values from -7 to 7
- clip_ids: int32 [8], P('group'), parts along dimension 0, may hold values from 0 to 1, as said below
- hidden_pre: bfloat16 [8, 16, 32, 5632], P(('group', 'tm'), 'height', 'width'), parts along dimension 0, may hold values from -6 to 6
- conv_weight: float32 [9, 5632], replicated, may hold values from -2 to 2
Outputs:
- query_grad: bfloat16 [8, 16, 32, 1120], P(('group', 'tm'), 'height', 'width'), parts along dimension 0
- key_grad: bfloat16 [8, 16, 32, 1120], P(('group', 'tm'), 'height', 'width'), parts along dimension 0
- value_gradient: bfloat16 [8, 16, 32, 1120], P(('group', 'tm'), 'height', 'width'), parts along dimension 0
- hidden_grad: bfloat16 [8, 16, 32, 5632], P(('group', 'tm'), 'height', 'width'), parts along dimension 0
The draws below stay inside these ranges and needn't reach their ends.
There are 2 independent parts, one for each index of `group`. The reference program is written for one: setup_inputs(seed, part) draws one part's arguments, and reference() takes and returns one part's arrays. A program takes and returns all parts, laid end to end along the dimension named above; an argument that names none is the same for every part. Nothing has to cross between parts.
Inputs may be any that keep to these rules, and one draw needn't show every extreme that they name: clip_ids never falls; the 4 frames form two clips, 0 then 1, each of 1 to 3 frames.
All inputs are finite; a program needn't handle non-finite values.
Results may differ from the reference program's by a relative error of at most 0.001.
Values may be sent and summed in bfloat16 or wider, within the bound.
No kernel may reach another device: no remote copies, remote signals or barrier semaphores. Data moves between devices by JAX's collectives and lax.ppermute only.
A program may use at most 64 MiB of HBM per device.

```python
import math
from functools import reduce
import jax
import jax.numpy as jnp
from jax import lax

HEAD_DIM = 112
HEADS = 10
FH = 2816
FRAMES = 4
HT = 16
WD = 32


def framed(key):
    channels = HEADS * HEAD_DIM
    key_offset, key_noise = jax.random.split(key)
    offset = jnp.clip(jax.random.normal(key_offset, (FRAMES, 1, 1, channels), jnp.float32), -3.0, 3.0)
    noise = jnp.clip(jax.random.normal(key_noise, (FRAMES, HT, WD, channels), jnp.float32), -4.0, 4.0)
    return offset + noise


def draw_attn_values(key, part):
    return framed(jax.random.fold_in(key, 11)).astype(jnp.bfloat16)


def draw_attn_cotangent(key, part):
    return framed(jax.random.fold_in(key, 23)).astype(jnp.bfloat16)


def draw_attn_keys(key, part):
    key_scale, key_noise = jax.random.split(jax.random.fold_in(key, 37))
    scales = jnp.exp(jax.random.uniform(key_scale, (FRAMES, 1, 1, HEADS, 1), jnp.float32, 0.0, math.log(10.0)))
    noise = jnp.clip(jax.random.normal(key_noise, (FRAMES, HT, WD, HEADS, HEAD_DIM), jnp.float32), -4.0, 4.0)
    return (noise * scales).reshape(FRAMES, HT, WD, HEADS * HEAD_DIM).astype(jnp.bfloat16)


def draw_clip_ids(key, part):
    lowest = FRAMES // 4
    spread_count = FRAMES - 2 * lowest + 1
    parity = jnp.asarray(part, jnp.int32) % 2
    choices_here = (spread_count - parity + 1) // 2
    picked = jax.random.randint(jax.random.fold_in(key, 53), (), 0, 1 << 20, jnp.int32) % choices_here
    boundary = lowest + parity + 2 * picked
    return (jnp.arange(FRAMES, dtype=jnp.int32) >= boundary).astype(jnp.int32)


def block_levels(own_key, extent, shards, smallest, top_value):
    gain, own = 1.0, jax.random.fold_in(own_key, 6)
    for axis_at, shards_of in shards:
        draws = jnp.exp(jax.random.uniform(jax.random.fold_in(own, axis_at), (shards_of,), jnp.float32, smallest / len(shards), top_value / len(shards)))
        gain = gain * jnp.repeat(draws, extent[axis_at] // shards_of).reshape([-1 if axis == axis_at else 1 for axis in range(len(extent))])
    return gain


def scatter_about(stream_key, extent, scale, limit, cuts=(), kind=jnp.bfloat16):
    entries = scale * jax.random.normal(stream_key, extent, jnp.float32)
    if cuts:
        entries = entries * block_levels(stream_key, extent, cuts, -0.22, 0.18)
    return jnp.clip(entries, -limit, limit).astype(kind)


def setup_inputs(seed: int = 0, part: int = 0) -> dict:
    key_list = jax.random.split(jax.random.key(seed), 8)
    own_keys = jax.random.split(jax.random.fold_in(key_list[7], part), 8)
    queries = scatter_about(own_keys[0], (FRAMES, HT, WD, HEADS * HEAD_DIM), 1.0, 5.0, ((0, 4), (1, 2), (2, 2)))
    attn_keys = draw_attn_keys(jax.random.fold_in(jax.random.fold_in(key_list[7], part), 71), part)
    attn_values = draw_attn_values(jax.random.fold_in(jax.random.fold_in(key_list[7], part), 71), part)
    attn_cotangent = draw_attn_cotangent(jax.random.fold_in(jax.random.fold_in(key_list[7], part), 71), part)
    clip_ids = draw_clip_ids(jax.random.fold_in(jax.random.fold_in(key_list[7], part), 71), part)
    hidden_pre = scatter_about(own_keys[5], (FRAMES, HT, WD, 2 * FH), 1.0, 6.0, ((0, 4), (1, 2), (2, 2)))
    conv_weight = scatter_about(key_list[6], (9, 2 * FH), 9 ** -0.5, 2.0, (), jnp.float32)
    return {"queries": queries, "attn_keys": attn_keys, "attn_values": attn_values, "attn_cotangent": attn_cotangent, "clip_ids": clip_ids, "hidden_pre": hidden_pre, "conv_weight": conv_weight}


EPSILON = 1e-06
TOP_PRECISION = lax.Precision.HIGHEST

def frame_terms(inputs):
    key_frame, value_frame = inputs
    feature_keys = jnp.maximum(key_frame.astype(jnp.float32), 0.0).reshape(-1, HEADS, HEAD_DIM)
    value_row_block = value_frame.astype(jnp.float32).reshape(-1, HEADS, HEAD_DIM)
    frame_key_value = jnp.einsum('jrf,jrx->rfx', feature_keys, value_row_block, precision=TOP_PRECISION)
    return (frame_key_value, lax.optimization_barrier(jnp.sum(feature_keys, axis=0)))

def query_side(inputs):
    query_frame, cotangent_frame, state_key_value, state_norm = inputs
    feature_query = jnp.maximum(query_frame.astype(jnp.float32), 0.0).reshape(-1, HEADS, HEAD_DIM)
    cotangent = cotangent_frame.astype(jnp.float32).reshape(-1, HEADS, HEAD_DIM)
    ratio_numerator = jnp.einsum('cob,obq->coq', feature_query, state_key_value, precision=TOP_PRECISION)
    denominator = jnp.einsum('thk,hk->th', feature_query, state_norm, precision=TOP_PRECISION) + EPSILON
    attended = ratio_numerator / denominator[..., None]
    scaled_gradient = cotangent / denominator[..., None]
    denominator_grad = -lax.optimization_barrier(jnp.sum(cotangent * attended, axis=-1)) / denominator
    feature_gradient = jnp.einsum('dla,lja->dlj', scaled_gradient, state_key_value, precision=TOP_PRECISION)
    feature_gradient = feature_gradient + state_norm[None] * denominator_grad[..., None]
    query_grad = jnp.where(feature_query > 0.0, feature_gradient, 0.0).reshape(query_frame.shape).astype(jnp.bfloat16)
    gradient_key_value = jnp.einsum('jrf,jrx->rfx', feature_query, scaled_gradient, precision=TOP_PRECISION)
    grad_norm = jnp.einsum('thk,th->hk', feature_query, denominator_grad, precision=TOP_PRECISION)
    return (query_grad, gradient_key_value, grad_norm)

def key_side(inputs):
    key_frame, value_frame, total_key_value, norm_total = inputs
    feature_keys = jnp.maximum(key_frame.astype(jnp.float32), 0.0).reshape(-1, HEADS, HEAD_DIM)
    value_row_block = value_frame.astype(jnp.float32).reshape(-1, HEADS, HEAD_DIM)
    feature_gradient = jnp.einsum('dla,lja->dlj', value_row_block, total_key_value, precision=TOP_PRECISION) + norm_total[None]
    key_grad = jnp.where(feature_keys > 0.0, feature_gradient, 0.0).reshape(key_frame.shape).astype(jnp.bfloat16)
    value_gradient = jnp.einsum('cob,obq->coq', feature_keys, total_key_value, precision=TOP_PRECISION)
    return (key_grad, value_gradient.reshape(value_frame.shape).astype(jnp.bfloat16))

def glu_grad(conv_out, split_at):
    value_part = conv_out[..., :split_at]
    gate_part = conv_out[..., split_at:]
    squash = jax.nn.sigmoid(gate_part)
    glu = value_part * gate_part * squash
    value_gradient = glu * gate_part * squash
    gate_grad = glu * value_part * squash * (1.0 + gate_part * (1.0 - squash))
    return jnp.concatenate([value_gradient, gate_grad], axis=-1)

def depthwise(source, weights, start, sign, height_out, width_out):
    terms = []
    for offset_row in (-1, 0, 1):
        for offset_col in (-1, 0, 1):
            tap_index = (offset_row + 1) * 3 + offset_col + 1
            row_start = start + sign * offset_row
            col_start = start + sign * offset_col
            window = source[row_start:row_start + height_out, col_start:col_start + width_out].astype(jnp.float32)
            terms.append(weights[tap_index] * window)
    return reduce(lambda first, second: first + second, terms)

def reference(queries, attn_keys, attn_values, attn_cotangent, clip_ids, hidden_pre, conv_weight):
    changes = (clip_ids[1:] != clip_ids[:-1]).astype(jnp.float32)
    starts = jnp.concatenate([jnp.ones((1,), jnp.float32), changes])
    ends = jnp.concatenate([changes, jnp.ones((1,), jnp.float32)])
    frame_key_value, frame_norm = lax.map(frame_terms, (attn_keys, attn_values))

    def forward_step(carried, inputs):
        kv_here, norm_here, start_here = inputs
        kv_now = kv_here + (1.0 - start_here) * carried[0]
        norm_now = norm_here + (1.0 - start_here) * carried[1]
        return ((kv_now, norm_now), (kv_now, norm_now))
    initial = (jnp.zeros_like(frame_key_value[0]), jnp.zeros_like(frame_norm[0]))
    ignored, states = lax.scan(forward_step, initial, (frame_key_value, frame_norm, starts))
    query_grad, gradient_key_value, grad_norm = lax.map(query_side, (queries, attn_cotangent, states[0], states[1]))

    def reverse_step(carried, inputs):
        kv_here, norm_here, end_here = inputs
        kv_now = kv_here + (1.0 - end_here) * carried[0]
        norm_now = norm_here + (1.0 - end_here) * carried[1]
        return ((kv_now, norm_now), (kv_now, norm_now))
    ignored, totals = lax.scan(reverse_step, initial, (gradient_key_value, grad_norm, ends), reverse=True)
    key_grad, value_gradient = lax.map(key_side, (attn_keys, attn_values, totals[0], totals[1]))
    weights = conv_weight.astype(jnp.float32)

    def conv_frame(hidden_frame):
        padded = jnp.pad(hidden_frame, ((1, 1), (1, 1), (0, 0)))
        conv_out = depthwise(padded, weights, 1, 1, HT, WD)
        conv_grad = glu_grad(conv_out, FH)
        grad_padded = jnp.pad(conv_grad, ((1, 1), (1, 1), (0, 0)))
        return depthwise(grad_padded, weights, 1, -1, HT, WD).astype(jnp.bfloat16)
    hidden_grad = lax.map(conv_frame, hidden_pre)
    return (query_grad, key_grad, value_gradient, hidden_grad)
```

```python
import functools
from functools import reduce

import jax
import jax.numpy as jnp
from jax import lax
from jax.experimental import pallas as pl
from jax.experimental.pallas import tpu as pltpu
from jax.sharding import PartitionSpec as P

HEAD_DIM = 112
HEADS = 10


EPSILON = 1e-06
TOP_PRECISION = lax.Precision.HIGHEST


def entering(value, axis, join, neutral, backward):
    count, mine = (lax.axis_size(axis), lax.axis_index(axis))
    pieces = jax.tree.map(lambda part: lax.all_gather(part, axis), value)
    if backward:
        pieces = jax.tree.map(lambda part: part[::-1], pieces)
        mine = count - 1 - mine
    so_far = jax.tree.map(
        lambda part, zero: jnp.full_like(part, 0) + jnp.asarray(zero, part.dtype), value, neutral
    )

    def turn(position, so_far):
        longer = join(so_far, jax.tree.map(lambda part: part[position], pieces))
        return jax.tree.map(lambda new, old: jnp.where(position < mine, new, old), longer, so_far)

    return lax.fori_loop(0, count - 1, turn, so_far)


def padded(block, sides, width):
    for axis, dim in sides:
        count = lax.axis_size(axis)
        forward = [(i, i + 1) for i in range(count - 1)]
        backward = [(target, source) for source, target in forward]
        low = lax.ppermute(
            lax.slice_in_dim(block, block.shape[dim] - width, None, axis=dim), axis, forward
        )
        high = lax.ppermute(lax.slice_in_dim(block, 0, width, axis=dim), axis, backward)
        block = jnp.concatenate([low, block, high], axis=dim)
    return block


def carry_on(earlier, later):
    keeping = 1.0 - later[0]
    return (
        jnp.maximum(earlier[0], later[0]),
        later[1] + keeping * earlier[1],
        later[2] + keeping * earlier[2],
    )


def clip_flags(clip_ids):
    frame = lax.axis_index("tm")
    frame_count = lax.axis_size("tm")
    current = lax.dynamic_index_in_dim(clip_ids, frame, 0, keepdims=False)
    before = lax.dynamic_index_in_dim(clip_ids, jnp.maximum(frame - 1, 0), 0, keepdims=False)
    after = lax.dynamic_index_in_dim(
        clip_ids, jnp.minimum(frame + 1, frame_count - 1), 0, keepdims=False
    )
    starts = jnp.where((frame == 0) | (current != before), 1.0, 0.0).astype(jnp.float32)
    ends = jnp.where((frame == frame_count - 1) | (current != after), 1.0, 0.0).astype(jnp.float32)
    return (starts, ends)


def glu_grad(conv_out, split_at):
    value_part = conv_out[..., :split_at]
    gate_part = conv_out[..., split_at:]
    squash = jax.nn.sigmoid(gate_part)
    glu = value_part * gate_part * squash
    value_gradient = glu * gate_part * squash
    gate_grad = glu * value_part * squash * (1.0 + gate_part * (1.0 - squash))
    return jnp.concatenate([value_gradient, gate_grad], axis=-1)


def depthwise(source, weights, start, sign, height_out, width_out):
    terms = []
    for offset_row in (-1, 0, 1):
        for offset_col in (-1, 0, 1):
            tap_index = (offset_row + 1) * 3 + offset_col + 1
            row_start = start + sign * offset_row
            col_start = start + sign * offset_col
            window = source[
                row_start : row_start + height_out, col_start : col_start + width_out
            ].astype(jnp.float32)
            terms.append(weights[tap_index] * window)
    return reduce(lambda first, second: first + second, terms)


def general_attention(queries, attn_keys, attn_values, attn_cotangent, clip_ids):
    token_count = queries.shape[1] * queries.shape[2]
    flat_width = HEADS * HEAD_DIM
    starts, ends = clip_flags(clip_ids)
    zero_flag = jnp.zeros((), jnp.float32)
    feature_keys = jnp.maximum(attn_keys, 0).reshape(token_count, HEADS, HEAD_DIM)
    value_row_block = attn_values.reshape(token_count, HEADS, HEAD_DIM)
    local_kv = jnp.einsum(
        "jrf,jrx->rfx", feature_keys, value_row_block, preferred_element_type=jnp.float32
    ).reshape(flat_width, HEAD_DIM)
    local_norm = jnp.sum(feature_keys.astype(jnp.float32), axis=0).reshape(flat_width)
    share_kv, share_norm = (
        lax.psum_scatter(local_kv, ("height", "width"), scatter_dimension=0, tiled=True),
        lax.psum_scatter(local_norm, ("height", "width"), scatter_dimension=0, tiled=True),
    )
    earlier = entering(
        (starts, share_kv, share_norm),
        "tm",
        carry_on,
        (zero_flag, jnp.zeros_like(share_kv), jnp.zeros_like(share_norm)),
        False,
    )
    part_kv = share_kv + (1.0 - starts) * earlier[1]
    part_norm = share_norm + (1.0 - starts) * earlier[2]
    state_key_value, state_norm = (
        lax.all_gather(part_kv, ("height", "width"), axis=0, tiled=True),
        lax.all_gather(part_norm, ("height", "width"), axis=0, tiled=True),
    )
    state_key_value = state_key_value.reshape(HEADS, HEAD_DIM, HEAD_DIM)
    state_norm = state_norm.reshape(HEADS, HEAD_DIM)
    feature_query = (
        jnp.maximum(queries, 0).reshape(token_count, HEADS, HEAD_DIM).astype(jnp.float32)
    )
    cotangent = attn_cotangent.reshape(token_count, HEADS, HEAD_DIM).astype(jnp.float32)
    ratio_numerator = jnp.einsum(
        "cob,obq->coq", feature_query, state_key_value, precision=TOP_PRECISION
    )
    denominator = (
        jnp.einsum("thk,hk->th", feature_query, state_norm, precision=TOP_PRECISION) + EPSILON
    )
    attended = ratio_numerator / denominator[..., None]
    scaled_gradient = cotangent / denominator[..., None]
    denominator_grad = -jnp.sum(cotangent * attended, axis=-1) / denominator
    query_feature_gradient = jnp.einsum(
        "dla,lja->dlj", scaled_gradient, state_key_value, precision=TOP_PRECISION
    )
    query_feature_gradient = query_feature_gradient + state_norm[None] * denominator_grad[..., None]
    query_grad = (
        jnp.where(feature_query > 0.0, query_feature_gradient, 0.0)
        .reshape(queries.shape)
        .astype(jnp.bfloat16)
    )
    gradient_key_value = jnp.einsum(
        "jrf,jrx->rfx", feature_query, scaled_gradient, precision=TOP_PRECISION
    ).reshape(flat_width, HEAD_DIM)
    grad_norm = jnp.einsum(
        "thk,th->hk", feature_query, denominator_grad, precision=TOP_PRECISION
    ).reshape(flat_width)
    share_grad_kv, share_grad_norm = (
        lax.psum_scatter(gradient_key_value, ("height", "width"), scatter_dimension=0, tiled=True),
        lax.psum_scatter(grad_norm, ("height", "width"), scatter_dimension=0, tiled=True),
    )
    later = entering(
        (ends, share_grad_kv, share_grad_norm),
        "tm",
        carry_on,
        (zero_flag, jnp.zeros_like(share_grad_kv), jnp.zeros_like(share_grad_norm)),
        True,
    )
    part_grad_kv = share_grad_kv + (1.0 - ends) * later[1]
    part_grad_norm = share_grad_norm + (1.0 - ends) * later[2]
    total_key_value, norm_total = (
        lax.all_gather(part_grad_kv, ("height", "width"), axis=0, tiled=True),
        lax.all_gather(part_grad_norm, ("height", "width"), axis=0, tiled=True),
    )
    total_key_value = total_key_value.reshape(HEADS, HEAD_DIM, HEAD_DIM)
    norm_total = norm_total.reshape(HEADS, HEAD_DIM)
    key_feat_grad = (
        jnp.einsum(
            "dla,lja->dlj",
            value_row_block.astype(jnp.float32),
            total_key_value,
            precision=TOP_PRECISION,
        )
        + norm_total[None]
    )
    key_grad = (
        jnp.where(feature_keys > 0, key_feat_grad, 0.0)
        .reshape(attn_keys.shape)
        .astype(jnp.bfloat16)
    )
    value_gradient = jnp.einsum(
        "cob,obq->coq", feature_keys.astype(jnp.float32), total_key_value, precision=TOP_PRECISION
    )
    value_gradient = value_gradient.reshape(attn_values.shape).astype(jnp.bfloat16)
    return (query_grad, key_grad, value_gradient)


LANES = 128


def split_terms(value):
    high = value.astype(jnp.bfloat16)
    low = (value - high.astype(jnp.float32)).astype(jnp.bfloat16)
    return high, low


def dot_tokens(left, right):
    return lax.dot_general(left, right, (((0,), (0,)), ((), ())), preferred_element_type=jnp.float32)


def dot_rows(left, right):
    return lax.dot_general(left, right, (((1,), (0,)), ((), ())), preferred_element_type=jnp.float32)


def dot_columns(left, right):
    return lax.dot_general(left, right, (((1,), (1,)), ((), ())), preferred_element_type=jnp.float32)


def head_slice(ref, head):
    return ref[:, head * HEAD_DIM : (head + 1) * HEAD_DIM]


def tail_block(rows, first):
    column = lax.broadcasted_iota(jnp.int32, (rows, LANES - HEAD_DIM), 1)
    return jnp.where(column == 0, first, 0.0).astype(jnp.bfloat16)


def vmem_call(kernel, out_shape, scratch=(), smem_first=False, n_in=0, flops=0, bytes_accessed=0, aliases=None):
    vmem = pl.BlockSpec(memory_space=pltpu.VMEM)
    in_specs = [vmem] * n_in
    if smem_first:
        in_specs[0] = pl.BlockSpec(memory_space=pltpu.SMEM)
    return pl.pallas_call(
        kernel,
        out_shape=out_shape,
        in_specs=in_specs,
        out_specs=jax.tree.map(lambda _: vmem, out_shape),
        scratch_shapes=list(scratch),
        cost_estimate=pl.CostEstimate(flops=flops, bytes_accessed=bytes_accessed, transcendentals=0),
    )


def state_kernel(key_ref, value_ref, keep_ref, send_ref, halves):
    tokens = key_ref.shape[0]
    one = tail_block(tokens, 1.0)
    half = halves.shape[2]
    per_group = HEADS // 2
    column = lax.axis_index("width")
    for group in range(2):
        for place in range(per_group):
            head = group * per_group + place
            feature = jnp.maximum(head_slice(key_ref, head), 0)
            wide = jnp.concatenate([head_slice(value_ref, head), one], axis=1)
            store_rows(halves, group, place * HEAD_DIM, dot_tokens(feature, wide), half)
    keep_ref[...] = halves[column]
    send_ref[...] = halves[1 - column]


def store_rows(halves, group, first, block, half):
    cut = min(max(half - first, 0), HEAD_DIM)
    if cut:
        index = (0, group) if group is not None else (0,)
        halves[(*index, slice(first, first + cut))] = block[:cut]
    if cut < HEAD_DIM:
        index = (1, group) if group is not None else (1,)
        start = first + cut - half
        halves[(*index, slice(start, start + HEAD_DIM - cut))] = block[cut:]


def pick_kernel(keep_ref, came_ref, mine_ref, other_ref):
    row = lax.axis_index("height")
    mine_ref[...] = keep_ref[row] + came_ref[row]
    other_ref[...] = keep_ref[1 - row] + came_ref[1 - row]


def heads_kernel(query_ref, cotangent_ref, mine_ref, other_ref, groups):
    none = tail_block(query_ref.shape[0], 0.0)
    per_group = HEADS // 2
    row = lax.axis_index("height")
    for head in range(HEADS):
        group, place = divmod(head, per_group)
        feature = jnp.maximum(head_slice(query_ref, head), 0)
        groups[group, 0, place] = jnp.concatenate([feature, none], axis=1)
        groups[group, 1, place] = jnp.concatenate([head_slice(cotangent_ref, head), none], axis=1)
    mine_ref[...] = groups[row]
    other_ref[...] = groups[1 - row]


def chain_kernel(step, clip_ref, own_ref, near_ref, far_ref, out_ref):
    frame = lax.axis_index("tm")
    last = lax.axis_size("tm") - 1
    here = clip_ref[frame]
    first = jnp.clip(frame - step, 0, last)
    second = jnp.clip(frame - 2 * step, 0, last)
    near = jnp.where((clip_ref[first] == here) & (first != frame), 1.0, 0.0)
    far = jnp.where((clip_ref[second] == here) & (second != first), 1.0, 0.0)
    out_ref[...] = own_ref[...] + near * near_ref[...] + far * far_ref[...]


def query_kernel(state_ref, came_ref, mine_ref, other_ref, keep_ref, send_ref, own_out, other_out, state, halves):
    column = lax.axis_index("width")
    half = state_ref.shape[0]
    per_group = HEADS // 2
    tokens = mine_ref.shape[2]
    state[column] = state_ref[...]
    state[1 - column] = came_ref[...]
    lane = lax.broadcasted_iota(jnp.int32, (2 * tokens, LANES), 1)
    for place in range(per_group):
        feature = jnp.concatenate([mine_ref[0, place], other_ref[0, place]], axis=0)
        cotangent = jnp.concatenate([mine_ref[1, place], other_ref[1, place]], axis=0).astype(jnp.float32)
        high, low = split_terms(load_rows(state, place * HEAD_DIM, half))
        narrow = feature[:, :HEAD_DIM]
        product = dot_rows(narrow, high) + dot_rows(narrow, low)
        inverse = 1.0 / (product[:, HEAD_DIM : HEAD_DIM + 1] + EPSILON)
        against = jnp.sum(cotangent * product, axis=1, keepdims=True)
        norm_grad = -(against * inverse) * inverse
        scaled = jnp.where(lane == HEAD_DIM, norm_grad, cotangent * inverse)
        scaled_high, scaled_low = split_terms(scaled)
        grad = dot_tokens(narrow, scaled_high) + dot_tokens(narrow, scaled_low)
        store_rows(halves, None, place * HEAD_DIM, grad, half)
        back = dot_columns(scaled_high, high) + dot_columns(scaled_high, low) + dot_columns(scaled_low, high)
        back = jnp.where(narrow > 0, back, 0.0).astype(jnp.bfloat16)
        own_out[place, :, :HEAD_DIM] = back[:tokens]
        other_out[place, :, :HEAD_DIM] = back[tokens:]
    keep_ref[...] = halves[column]
    send_ref[...] = halves[1 - column]


def load_rows(state, first, half):
    cut = min(max(half - first, 0), HEAD_DIM)
    parts = []
    if cut:
        parts.append(state[0, first : first + cut])
    if cut < HEAD_DIM:
        start = first + cut - half
        parts.append(state[1, start : start + HEAD_DIM - cut])
    return parts[0] if len(parts) == 1 else jnp.concatenate(parts, axis=0)


def key_kernel(key_ref, value_ref, near_ref, near_came_ref, far_ref, far_came_ref, key_out, value_out, total):
    column, row = lax.axis_index("width"), lax.axis_index("height")
    half = near_ref.shape[0]
    per_group = HEADS // 2
    total[row, column] = near_ref[...]
    total[row, 1 - column] = near_came_ref[...]
    total[1 - row, column] = far_ref[...]
    total[1 - row, 1 - column] = far_came_ref[...]
    one = tail_block(key_ref.shape[0], 1.0)
    for head in range(HEADS):
        group, place = divmod(head, per_group)
        feature = jnp.maximum(head_slice(key_ref, head), 0)
        wide = jnp.concatenate([head_slice(value_ref, head), one], axis=1)
        high, low = split_terms(load_rows(total.at[group], place * HEAD_DIM, half))
        grad = dot_columns(wide, high) + dot_columns(wide, low)
        lanes = slice(head * HEAD_DIM, (head + 1) * HEAD_DIM)
        key_out[:, lanes] = jnp.where(feature > 0, grad, 0.0).astype(jnp.bfloat16)
        product = dot_rows(feature, high) + dot_rows(feature, low)
        value_out[:, lanes] = product[:, :HEAD_DIM].astype(jnp.bfloat16)


def join_kernel(mine_ref, came_ref, out_ref):
    row = lax.axis_index("height")
    per_group = HEADS // 2
    for place in range(per_group):
        mine, came = mine_ref[place, :, :HEAD_DIM], came_ref[place, :, :HEAD_DIM]
        first = jnp.where(row == 0, mine, came)
        second = jnp.where(row == 0, came, mine)
        out_ref[:, place * HEAD_DIM : (place + 1) * HEAD_DIM] = first
        at = (per_group + place) * HEAD_DIM
        out_ref[:, at : at + HEAD_DIM] = second


def struct(shape, dtype=jnp.float32):
    return jax.ShapeDtypeStruct(shape, dtype)


SWAP = [(0, 1), (1, 0)]


def paired_attention(queries, attn_keys, attn_values, attn_cotangent, clip_ids):
    tokens = queries.shape[1] * queries.shape[2]
    flat = HEADS * HEAD_DIM
    per_group = HEADS // 2
    half = per_group * HEAD_DIM // 2
    frames = lax.axis_size("tm")
    query, key, value, cotangent = (
        part.reshape(tokens, flat) for part in (queries, attn_keys, attn_values, attn_cotangent)
    )
    share = struct((half, LANES))
    pair = struct((2, half, LANES))

    keep, send = vmem_call(
        state_kernel, (pair, pair), [pltpu.VMEM((2, 2, half, LANES), jnp.float32)], n_in=2,
        flops=2 * tokens * flat * LANES, bytes_accessed=4 * tokens * flat + 8 * half * LANES * 2,
    )(key, value)
    came = lax.ppermute(send, "width", SWAP)
    mine, other = vmem_call(pick_kernel, (share, share), n_in=2, bytes_accessed=24 * half * LANES)(keep, came)
    came = lax.ppermute(other, "height", SWAP)

    packed = struct((2, per_group, tokens, LANES), jnp.bfloat16)
    heads_mine, heads_other = vmem_call(
        heads_kernel, (packed, packed), [pltpu.VMEM((2, 2, per_group, tokens, LANES), jnp.bfloat16)], n_in=2,
        bytes_accessed=12 * tokens * flat,
    )(query, cotangent)
    own = mine + came
    heads_other, own = lax.optimization_barrier((heads_other, own))
    heads_came = lax.ppermute(heads_other, "height", SWAP)

    def along_frames(own, step):
        moves = [[(at, at + step * hop) for at in range(frames) if 0 <= at + step * hop < frames] for hop in (1, 2)]
        near = lax.ppermute(own, "tm", moves[0])
        far = lax.ppermute(own, "tm", moves[1])
        return vmem_call(
            functools.partial(chain_kernel, step), share, smem_first=True, n_in=4, bytes_accessed=16 * half * LANES
        )(clip_ids, own, near, far)

    state = along_frames(own, 1)
    came = lax.ppermute(state, "width", SWAP)
    back = struct((per_group, tokens, LANES), jnp.bfloat16)
    keep, send, back_mine, back_other = vmem_call(
        query_kernel, (share, share, back, back),
        [pltpu.VMEM((2, half, LANES), jnp.float32), pltpu.VMEM((2, half, LANES), jnp.float32)], n_in=4,
        flops=14 * tokens * flat * LANES, bytes_accessed=8 * tokens * flat,
    )(state, came, heads_mine, heads_came)
    came = lax.ppermute(send, "width", SWAP)
    own = keep + came
    back_other, own = lax.optimization_barrier((back_other, own))
    total = along_frames(own, -1)
    back_came = lax.ppermute(back_other, "height", SWAP)
    query_grad = vmem_call(
        join_kernel, struct((tokens, flat), jnp.bfloat16), n_in=2, bytes_accessed=4 * tokens * flat
    )(back_mine, back_came)
    far = lax.ppermute(total, "height", SWAP)
    near_came = lax.ppermute(total, "width", SWAP)
    far_came = lax.ppermute(far, "width", SWAP)
    out = struct((tokens, flat), jnp.bfloat16)
    key_grad, value_gradient = vmem_call(
        key_kernel, (out, out), [pltpu.VMEM((2, 2, half, LANES), jnp.float32)], n_in=6,
        flops=8 * tokens * flat * LANES, bytes_accessed=8 * tokens * flat,
    )(key, value, total, near_came, far, far_came)
    return tuple(part.reshape(queries.shape) for part in (query_grad, key_grad, value_gradient))


def mixed_ffn(hidden_pre, conv_weight):
    row_count = hidden_pre.shape[1]
    col_count = hidden_pre.shape[2]
    split_at = hidden_pre.shape[3] // 2
    widened = padded(hidden_pre, (("height", 1), ("width", 2)), 2)[0]
    conv_out = depthwise(widened, conv_weight, 1, 1, row_count + 2, col_count + 2)
    row_global = lax.axis_index("height") * row_count + jnp.arange(row_count + 2) - 1
    col_global = lax.axis_index("width") * col_count + jnp.arange(col_count + 2) - 1
    row_inside = (row_global >= 0) & (row_global < row_count * lax.axis_size("height"))
    col_inside = (col_global >= 0) & (col_global < col_count * lax.axis_size("width"))
    inside = (row_inside[:, None] & col_inside[None, :]).astype(jnp.float32)
    conv_grad = glu_grad(conv_out, split_at) * inside[:, :, None]
    hidden_grad = depthwise(conv_grad, conv_weight, 1, -1, row_count, col_count)
    hidden_grad = hidden_grad[None].astype(jnp.bfloat16)
    return hidden_grad


def per_device(queries, attn_keys, attn_values, attn_cotangent, clip_ids, hidden_pre, conv_weight):
    paired = (
        lax.axis_size("height") == 2
        and lax.axis_size("width") == 2
        and 3 <= lax.axis_size("tm") <= 4
        and HEADS % 2 == 0
        and queries.shape[0] == 1
    )
    attention = paired_attention if paired else general_attention
    grads = attention(queries, attn_keys, attn_values, attn_cotangent, clip_ids)
    return (*grads, mixed_ffn(hidden_pre, conv_weight))


def solution(mesh):
    return jax.shard_map(
        per_device,
        mesh=mesh,
        in_specs=(
            P(("group", "tm"), "height", "width", None),
            P(("group", "tm"), "height", "width", None),
            P(("group", "tm"), "height", "width", None),
            P(("group", "tm"), "height", "width", None),
            P("group"),
            P(("group", "tm"), "height", "width", None),
            P(),
        ),
        out_specs=(
            P(("group", "tm"), "height", "width", None),
            P(("group", "tm"), "height", "width", None),
            P(("group", "tm"), "height", "width", None),
            P(("group", "tm"), "height", "width", None),
        ),
        check_vma=False,
    )
```

```python
import functools
from functools import reduce

import jax
import jax.numpy as jnp
from jax import lax
from jax.experimental import pallas as pl
from jax.experimental.pallas import tpu as pltpu
from jax.sharding import PartitionSpec as P

HEAD_DIM = 112
HEADS = 10


EPSILON = 1e-06
TOP_PRECISION = lax.Precision.HIGHEST


def entering(value, axis, join, neutral, backward):
    count, mine = (lax.axis_size(axis), lax.axis_index(axis))
    pieces = jax.tree.map(lambda part: lax.all_gather(part, axis), value)
    if backward:
        pieces = jax.tree.map(lambda part: part[::-1], pieces)
        mine = count - 1 - mine
    so_far = jax.tree.map(
        lambda part, zero: jnp.full_like(part, 0) + jnp.asarray(zero, part.dtype), value, neutral
    )

    def turn(position, so_far):
        longer = join(so_far, jax.tree.map(lambda part: part[position], pieces))
        return jax.tree.map(lambda new, old: jnp.where(position < mine, new, old), longer, so_far)

    return lax.fori_loop(0, count - 1, turn, so_far)


def padded(block, sides, width):
    for axis, dim in sides:
        count = lax.axis_size(axis)
        forward = [(i, i + 1) for i in range(count - 1)]
        backward = [(target, source) for source, target in forward]
        low = lax.ppermute(
            lax.slice_in_dim(block, block.shape[dim] - width, None, axis=dim), axis, forward
        )
        high = lax.ppermute(lax.slice_in_dim(block, 0, width, axis=dim), axis, backward)
        block = jnp.concatenate([low, block, high], axis=dim)
    return block


def carry_on(earlier, later):
    keeping = 1.0 - later[0]
    return (
        jnp.maximum(earlier[0], later[0]),
        later[1] + keeping * earlier[1],
        later[2] + keeping * earlier[2],
    )


def clip_flags(clip_ids):
    frame = lax.axis_index("tm")
    frame_count = lax.axis_size("tm")
    current = lax.dynamic_index_in_dim(clip_ids, frame, 0, keepdims=False)
    before = lax.dynamic_index_in_dim(clip_ids, jnp.maximum(frame - 1, 0), 0, keepdims=False)
    after = lax.dynamic_index_in_dim(
        clip_ids, jnp.minimum(frame + 1, frame_count - 1), 0, keepdims=False
    )
    starts = jnp.where((frame == 0) | (current != before), 1.0, 0.0).astype(jnp.float32)
    ends = jnp.where((frame == frame_count - 1) | (current != after), 1.0, 0.0).astype(jnp.float32)
    return (starts, ends)


def glu_grad(conv_out, split_at):
    value_part = conv_out[..., :split_at]
    gate_part = conv_out[..., split_at:]
    squash = jax.nn.sigmoid(gate_part)
    glu = value_part * gate_part * squash
    value_gradient = glu * gate_part * squash
    gate_grad = glu * value_part * squash * (1.0 + gate_part * (1.0 - squash))
    return jnp.concatenate([value_gradient, gate_grad], axis=-1)


def depthwise(source, weights, start, sign, height_out, width_out):
    terms = []
    for offset_row in (-1, 0, 1):
        for offset_col in (-1, 0, 1):
            tap_index = (offset_row + 1) * 3 + offset_col + 1
            row_start = start + sign * offset_row
            col_start = start + sign * offset_col
            window = source[
                row_start : row_start + height_out, col_start : col_start + width_out
            ].astype(jnp.float32)
            terms.append(weights[tap_index] * window)
    return reduce(lambda first, second: first + second, terms)


def general_attention(queries, attn_keys, attn_values, attn_cotangent, clip_ids):
    token_count = queries.shape[1] * queries.shape[2]
    flat_width = HEADS * HEAD_DIM
    starts, ends = clip_flags(clip_ids)
    zero_flag = jnp.zeros((), jnp.float32)
    feature_keys = jnp.maximum(attn_keys, 0).reshape(token_count, HEADS, HEAD_DIM)
    value_row_block = attn_values.reshape(token_count, HEADS, HEAD_DIM)
    local_kv = jnp.einsum(
        "jrf,jrx->rfx", feature_keys, value_row_block, preferred_element_type=jnp.float32
    ).reshape(flat_width, HEAD_DIM)
    local_norm = jnp.sum(feature_keys.astype(jnp.float32), axis=0).reshape(flat_width)
    share_kv, share_norm = (
        lax.psum_scatter(local_kv, ("height", "width"), scatter_dimension=0, tiled=True),
        lax.psum_scatter(local_norm, ("height", "width"), scatter_dimension=0, tiled=True),
    )
    earlier = entering(
        (starts, share_kv, share_norm),
        "tm",
        carry_on,
        (zero_flag, jnp.zeros_like(share_kv), jnp.zeros_like(share_norm)),
        False,
    )
    part_kv = share_kv + (1.0 - starts) * earlier[1]
    part_norm = share_norm + (1.0 - starts) * earlier[2]
    state_key_value, state_norm = (
        lax.all_gather(part_kv, ("height", "width"), axis=0, tiled=True),
        lax.all_gather(part_norm, ("height", "width"), axis=0, tiled=True),
    )
    state_key_value = state_key_value.reshape(HEADS, HEAD_DIM, HEAD_DIM)
    state_norm = state_norm.reshape(HEADS, HEAD_DIM)
    feature_query = (
        jnp.maximum(queries, 0).reshape(token_count, HEADS, HEAD_DIM).astype(jnp.float32)
    )
    cotangent = attn_cotangent.reshape(token_count, HEADS, HEAD_DIM).astype(jnp.float32)
    ratio_numerator = jnp.einsum(
        "cob,obq->coq", feature_query, state_key_value, precision=TOP_PRECISION
    )
    denominator = (
        jnp.einsum("thk,hk->th", feature_query, state_norm, precision=TOP_PRECISION) + EPSILON
    )
    attended = ratio_numerator / denominator[..., None]
    scaled_gradient = cotangent / denominator[..., None]
    denominator_grad = -jnp.sum(cotangent * attended, axis=-1) / denominator
    query_feature_gradient = jnp.einsum(
        "dla,lja->dlj", scaled_gradient, state_key_value, precision=TOP_PRECISION
    )
    query_feature_gradient = query_feature_gradient + state_norm[None] * denominator_grad[..., None]
    query_grad = (
        jnp.where(feature_query > 0.0, query_feature_gradient, 0.0)
        .reshape(queries.shape)
        .astype(jnp.bfloat16)
    )
    gradient_key_value = jnp.einsum(
        "jrf,jrx->rfx", feature_query, scaled_gradient, precision=TOP_PRECISION
    ).reshape(flat_width, HEAD_DIM)
    grad_norm = jnp.einsum(
        "thk,th->hk", feature_query, denominator_grad, precision=TOP_PRECISION
    ).reshape(flat_width)
    share_grad_kv, share_grad_norm = (
        lax.psum_scatter(gradient_key_value, ("height", "width"), scatter_dimension=0, tiled=True),
        lax.psum_scatter(grad_norm, ("height", "width"), scatter_dimension=0, tiled=True),
    )
    later = entering(
        (ends, share_grad_kv, share_grad_norm),
        "tm",
        carry_on,
        (zero_flag, jnp.zeros_like(share_grad_kv), jnp.zeros_like(share_grad_norm)),
        True,
    )
    part_grad_kv = share_grad_kv + (1.0 - ends) * later[1]
    part_grad_norm = share_grad_norm + (1.0 - ends) * later[2]
    total_key_value, norm_total = (
        lax.all_gather(part_grad_kv, ("height", "width"), axis=0, tiled=True),
        lax.all_gather(part_grad_norm, ("height", "width"), axis=0, tiled=True),
    )
    total_key_value = total_key_value.reshape(HEADS, HEAD_DIM, HEAD_DIM)
    norm_total = norm_total.reshape(HEADS, HEAD_DIM)
    key_feat_grad = (
        jnp.einsum(
            "dla,lja->dlj",
            value_row_block.astype(jnp.float32),
            total_key_value,
            precision=TOP_PRECISION,
        )
        + norm_total[None]
    )
    key_grad = (
        jnp.where(feature_keys > 0, key_feat_grad, 0.0)
        .reshape(attn_keys.shape)
        .astype(jnp.bfloat16)
    )
    value_gradient = jnp.einsum(
        "cob,obq->coq", feature_keys.astype(jnp.float32), total_key_value, precision=TOP_PRECISION
    )
    value_gradient = value_gradient.reshape(attn_values.shape).astype(jnp.bfloat16)
    return (query_grad, key_grad, value_gradient)


LANES = 128


def split_terms(value):
    high = value.astype(jnp.bfloat16)
    low = (value - high.astype(jnp.float32)).astype(jnp.bfloat16)
    return high, low


def dot_tokens(left, right):
    return lax.dot_general(left, right, (((0,), (0,)), ((), ())), preferred_element_type=jnp.float32)


def dot_rows(left, right):
    return lax.dot_general(left, right, (((1,), (0,)), ((), ())), preferred_element_type=jnp.float32)


def dot_columns(left, right):
    return lax.dot_general(left, right, (((1,), (1,)), ((), ())), preferred_element_type=jnp.float32)


def head_slice(ref, head):
    return ref[:, head * HEAD_DIM : (head + 1) * HEAD_DIM]


def tail_block(rows, first):
    column = lax.broadcasted_iota(jnp.int32, (rows, LANES - HEAD_DIM), 1)
    return jnp.where(column == 0, first, 0.0).astype(jnp.bfloat16)


def vmem_call(kernel, out_shape, scratch=(), smem_first=False, n_in=0, flops=0, bytes_accessed=0, vmem_mib=8):
    vmem = pl.BlockSpec(memory_space=pltpu.VMEM)
    in_specs = [vmem] * n_in
    if smem_first:
        in_specs[0] = pl.BlockSpec(memory_space=pltpu.SMEM)
    return pl.pallas_call(
        kernel,
        out_shape=out_shape,
        in_specs=in_specs,
        out_specs=jax.tree.map(lambda _: vmem, out_shape),
        scratch_shapes=list(scratch),
        cost_estimate=pl.CostEstimate(flops=flops, bytes_accessed=bytes_accessed, transcendentals=0),
        compiler_params=pltpu.CompilerParams(vmem_limit_bytes=vmem_mib << 20),
    )


def state_kernel(key_ref, value_ref, keep_ref, send_ref, halves):
    tokens = key_ref.shape[0]
    one = tail_block(tokens, 1.0)
    half = halves.shape[2]
    per_group = HEADS // 2
    column = lax.axis_index("width")
    for group in range(2):
        for place in range(per_group):
            head = group * per_group + place
            feature = jnp.maximum(head_slice(key_ref, head), 0)
            wide = jnp.concatenate([head_slice(value_ref, head), one], axis=1)
            store_rows(halves, group, place * HEAD_DIM, dot_tokens(feature, wide), half)
    keep_ref[...] = halves[column]
    send_ref[...] = halves[1 - column]


def store_rows(halves, group, first, block, half):
    cut = min(max(half - first, 0), HEAD_DIM)
    if cut:
        index = (0, group) if group is not None else (0,)
        halves[(*index, slice(first, first + cut))] = block[:cut]
    if cut < HEAD_DIM:
        index = (1, group) if group is not None else (1,)
        start = first + cut - half
        halves[(*index, slice(start, start + HEAD_DIM - cut))] = block[cut:]


def pick_kernel(keep_ref, came_ref, mine_ref, other_ref):
    row = lax.axis_index("height")
    mine_ref[...] = keep_ref[row] + came_ref[row]
    other_ref[...] = keep_ref[1 - row] + came_ref[1 - row]


def heads_kernel(query_ref, cotangent_ref, mine_ref, other_ref, groups):
    none = tail_block(query_ref.shape[0], 0.0)
    per_group = HEADS // 2
    row = lax.axis_index("height")
    for head in range(HEADS):
        group, place = divmod(head, per_group)
        feature = jnp.maximum(head_slice(query_ref, head), 0)
        groups[group, 0, place] = jnp.concatenate([feature, none], axis=1)
        groups[group, 1, place] = jnp.concatenate([head_slice(cotangent_ref, head), none], axis=1)
    mine_ref[...] = groups[row]
    other_ref[...] = groups[1 - row]


def chain_kernel(step, clip_ref, own_ref, near_ref, far_ref, out_ref):
    frame = lax.axis_index("tm")
    last = lax.axis_size("tm") - 1
    here = clip_ref[frame]
    first = jnp.clip(frame - step, 0, last)
    second = jnp.clip(frame - 2 * step, 0, last)
    near = jnp.where((clip_ref[first] == here) & (first != frame), 1.0, 0.0)
    far = jnp.where((clip_ref[second] == here) & (second != first), 1.0, 0.0)
    out_ref[...] = own_ref[...] + near * near_ref[...] + far * far_ref[...]


def query_kernel(state_ref, came_ref, mine_ref, other_ref, keep_ref, send_ref, own_out, other_out, state, halves):
    column = lax.axis_index("width")
    half = state_ref.shape[0]
    per_group = HEADS // 2
    tokens = mine_ref.shape[2]
    state[column] = state_ref[...]
    state[1 - column] = came_ref[...]
    lane = lax.broadcasted_iota(jnp.int32, (2 * tokens, LANES), 1)
    for place in range(per_group):
        feature = jnp.concatenate([mine_ref[0, place], other_ref[0, place]], axis=0)
        cotangent = jnp.concatenate([mine_ref[1, place], other_ref[1, place]], axis=0).astype(jnp.float32)
        high, low = split_terms(load_rows(state, place * HEAD_DIM, half))
        narrow = feature[:, :HEAD_DIM]
        product = dot_rows(narrow, high) + dot_rows(narrow, low)
        inverse = 1.0 / (product[:, HEAD_DIM : HEAD_DIM + 1] + EPSILON)
        against = jnp.sum(cotangent * product, axis=1, keepdims=True)
        norm_grad = -(against * inverse) * inverse
        scaled = jnp.where(lane == HEAD_DIM, norm_grad, cotangent * inverse)
        scaled_high, scaled_low = split_terms(scaled)
        grad = dot_tokens(narrow, scaled_high) + dot_tokens(narrow, scaled_low)
        store_rows(halves, None, place * HEAD_DIM, grad, half)
        back = dot_columns(scaled_high, high) + dot_columns(scaled_high, low) + dot_columns(scaled_low, high)
        back = jnp.where(narrow > 0, back, 0.0).astype(jnp.bfloat16)
        own_out[place, :, :HEAD_DIM] = back[:tokens]
        other_out[place, :, :HEAD_DIM] = back[tokens:]
    keep_ref[...] = halves[column]
    send_ref[...] = halves[1 - column]


def load_rows(state, first, half):
    cut = min(max(half - first, 0), HEAD_DIM)
    parts = []
    if cut:
        parts.append(state[0, first : first + cut])
    if cut < HEAD_DIM:
        start = first + cut - half
        parts.append(state[1, start : start + HEAD_DIM - cut])
    return parts[0] if len(parts) == 1 else jnp.concatenate(parts, axis=0)


def key_kernel(key_ref, value_ref, near_ref, near_came_ref, far_ref, far_came_ref, key_out, value_out, total):
    column, row = lax.axis_index("width"), lax.axis_index("height")
    half = near_ref.shape[0]
    per_group = HEADS // 2
    total[row, column] = near_ref[...]
    total[row, 1 - column] = near_came_ref[...]
    total[1 - row, column] = far_ref[...]
    total[1 - row, 1 - column] = far_came_ref[...]
    one = tail_block(key_ref.shape[0], 1.0)
    for head in range(HEADS):
        group, place = divmod(head, per_group)
        feature = jnp.maximum(head_slice(key_ref, head), 0)
        wide = jnp.concatenate([head_slice(value_ref, head), one], axis=1)
        high, low = split_terms(load_rows(total.at[group], place * HEAD_DIM, half))
        grad = dot_columns(wide, high) + dot_columns(wide, low)
        lanes = slice(head * HEAD_DIM, (head + 1) * HEAD_DIM)
        key_out[:, lanes] = jnp.where(feature > 0, grad, 0.0).astype(jnp.bfloat16)
        product = dot_rows(feature, high) + dot_rows(feature, low)
        value_out[:, lanes] = product[:, :HEAD_DIM].astype(jnp.bfloat16)


def join_kernel(mine_ref, came_ref, out_ref):
    row = lax.axis_index("height")
    per_group = HEADS // 2
    for place in range(per_group):
        mine, came = mine_ref[place, :, :HEAD_DIM], came_ref[place, :, :HEAD_DIM]
        first = jnp.where(row == 0, mine, came)
        second = jnp.where(row == 0, came, mine)
        out_ref[:, place * HEAD_DIM : (place + 1) * HEAD_DIM] = first
        at = (per_group + place) * HEAD_DIM
        out_ref[:, at : at + HEAD_DIM] = second


def struct(shape, dtype=jnp.float32):
    return jax.ShapeDtypeStruct(shape, dtype)


SWAP = [(0, 1), (1, 0)]


def paired_attention(queries, attn_keys, attn_values, attn_cotangent, clip_ids):
    tokens = queries.shape[1] * queries.shape[2]
    flat = HEADS * HEAD_DIM
    per_group = HEADS // 2
    half = per_group * HEAD_DIM // 2
    frames = lax.axis_size("tm")
    query, key, value, cotangent = (
        part.reshape(tokens, flat) for part in (queries, attn_keys, attn_values, attn_cotangent)
    )
    share = struct((half, LANES))
    pair = struct((2, half, LANES))

    keep, send = vmem_call(
        state_kernel, (pair, pair), [pltpu.VMEM((2, 2, half, LANES), jnp.float32)], n_in=2,
        flops=2 * tokens * flat * LANES, bytes_accessed=4 * tokens * flat + 8 * half * LANES * 2,
    )(key, value)
    came = lax.ppermute(send, "width", SWAP)
    mine, other = vmem_call(pick_kernel, (share, share), n_in=2, bytes_accessed=24 * half * LANES)(keep, came)
    came = lax.ppermute(other, "height", SWAP)

    packed = struct((2, per_group, tokens, LANES), jnp.bfloat16)
    heads_mine, heads_other = vmem_call(
        heads_kernel, (packed, packed), [pltpu.VMEM((2, 2, per_group, tokens, LANES), jnp.bfloat16)], n_in=2,
        bytes_accessed=12 * tokens * flat,
    )(query, cotangent)
    own = mine + came
    heads_other, own = lax.optimization_barrier((heads_other, own))
    heads_came = lax.ppermute(heads_other, "height", SWAP)

    def along_frames(own, step):
        moves = [[(at, at + step * hop) for at in range(frames) if 0 <= at + step * hop < frames] for hop in (1, 2)]
        near = lax.ppermute(own, "tm", moves[0])
        far = lax.ppermute(own, "tm", moves[1])
        return vmem_call(
            functools.partial(chain_kernel, step), share, smem_first=True, n_in=4, bytes_accessed=16 * half * LANES
        )(clip_ids, own, near, far)

    state = along_frames(own, 1)
    came = lax.ppermute(state, "width", SWAP)
    back = struct((per_group, tokens, LANES), jnp.bfloat16)
    keep, send, back_mine, back_other = vmem_call(
        query_kernel, (share, share, back, back),
        [pltpu.VMEM((2, half, LANES), jnp.float32), pltpu.VMEM((2, half, LANES), jnp.float32)], n_in=4,
        flops=14 * tokens * flat * LANES, bytes_accessed=8 * tokens * flat,
    )(state, came, heads_mine, heads_came)
    came = lax.ppermute(send, "width", SWAP)
    own = keep + came
    back_other, own = lax.optimization_barrier((back_other, own))
    total = along_frames(own, -1)
    back_came = lax.ppermute(back_other, "height", SWAP)
    query_grad = vmem_call(
        join_kernel, struct((tokens, flat), jnp.bfloat16), n_in=2, bytes_accessed=4 * tokens * flat
    )(back_mine, back_came)
    far = lax.ppermute(total, "height", SWAP)
    near_came = lax.ppermute(total, "width", SWAP)
    far_came = lax.ppermute(far, "width", SWAP)
    out = struct((tokens, flat), jnp.bfloat16)
    key_grad, value_gradient = vmem_call(
        key_kernel, (out, out), [pltpu.VMEM((2, 2, half, LANES), jnp.float32)], n_in=6,
        flops=8 * tokens * flat * LANES, bytes_accessed=8 * tokens * flat,
    )(key, value, total, near_came, far, far_came)
    return tuple(part.reshape(queries.shape) for part in (query_grad, key_grad, value_gradient))


def mixed_ffn(hidden_pre, conv_weight):
    row_count = hidden_pre.shape[1]
    col_count = hidden_pre.shape[2]
    split_at = hidden_pre.shape[3] // 2
    widened = padded(hidden_pre, (("height", 1), ("width", 2)), 2)[0]
    conv_out = depthwise(widened, conv_weight, 1, 1, row_count + 2, col_count + 2)
    row_global = lax.axis_index("height") * row_count + jnp.arange(row_count + 2) - 1
    col_global = lax.axis_index("width") * col_count + jnp.arange(col_count + 2) - 1
    row_inside = (row_global >= 0) & (row_global < row_count * lax.axis_size("height"))
    col_inside = (col_global >= 0) & (col_global < col_count * lax.axis_size("width"))
    inside = (row_inside[:, None] & col_inside[None, :]).astype(jnp.float32)
    conv_grad = glu_grad(conv_out, split_at) * inside[:, :, None]
    hidden_grad = depthwise(conv_grad, conv_weight, 1, -1, row_count, col_count)
    hidden_grad = hidden_grad[None].astype(jnp.bfloat16)
    return hidden_grad


TILES = 8
REACH = 2


def conv_kernel(rows_per_frame, row_refs, *refs):
    halo_rows, refs = refs[:row_refs], refs[row_refs:]
    side_ref, refs = refs[0], refs[1:]
    corners, refs = refs[:row_refs], refs[row_refs:]
    block_ref, weight_ref, out_ref, taps, value_in, gate_in, value_grad, gate_grad, value_out, gate_out = refs
    rows, cols, channels = block_ref.shape
    lane_tiles = channels // LANES // 2
    pitch = -(-lane_tiles // TILES) * TILES
    row, column = lax.axis_index("height"), lax.axis_index("width")
    first_row, last_row = row == 0, row == lax.axis_size("height") - 1
    wide, tall = cols + 2 * REACH, rows + 2 * REACH
    grad_wide = wide - 2

    for tile in range(2 * lane_tiles):
        place = tile if tile < lane_tiles else pitch + tile - lane_tiles
        taps[pl.ds(place, 9, stride=2 * pitch), :] = weight_ref[:, tile * LANES : (tile + 1) * LANES]

    def source_at(at_row, at_col):
        return pl.multiple_of((at_row * wide + at_col) * TILES, TILES)

    def grad_at(at_row, at_col):
        return pl.multiple_of((at_row * grad_wide + at_col) * TILES, TILES)

    zero = jnp.zeros((TILES, LANES), jnp.float32)
    low_border = jnp.where(first_row, 0, rows + REACH)
    outer_col = jnp.where(column == 0, 0, cols + REACH)
    side_col = jnp.where(column == 0, cols + REACH, 0)
    grad_outer_col = jnp.where(column == 0, 0, grad_wide - 1)
    start_col = jnp.where(column == 0, REACH, REACH - 1)
    low, high = jnp.where(first_row, REACH, REACH - 1), jnp.where(last_row, rows + REACH, rows + REACH + 1)

    for ref in (value_in, gate_in):
        @pl.loop(0, tall)
        def _(at):
            for extra in range(REACH):
                ref[pl.ds(source_at(at, outer_col + extra), TILES), :] = zero

    for ref in (value_grad, gate_grad):
        @pl.loop(0, rows + 2)
        def _(at):
            ref[pl.ds(grad_at(at, grad_outer_col), TILES), :] = zero

        for edge, at in ((first_row, 0), (last_row, rows + 1)):
            @pl.when(edge)
            def _():
                for col in range(grad_wide):
                    ref[pl.ds(grad_at(at, col), TILES), :] = zero

    for base in range(0, lane_tiles, TILES):
        count = min(TILES, lane_tiles - base)

        def spread(load, at_row, at_col, length):
            for ref, offset in ((value_in, base), (gate_in, lane_tiles + base)):
                for tile in range(count):
                    part = load(slice((offset + tile) * LANES, (offset + tile + 1) * LANES)).astype(jnp.float32)
                    ref[pl.ds(source_at(at_row, at_col) + tile, length, stride=TILES), :] = part

        @pl.loop(0, rows)
        def _(at):
            spread(lambda lanes: block_ref[at, :, lanes], at + REACH, REACH, cols)
            spread(lambda lanes: side_ref[at, :, lanes], at + REACH, side_col, REACH)

        for edge, at, which in ((first_row, 0, 0), (last_row, rows + REACH, row_refs - 1)):
            rows_ref, corner_ref = halo_rows[which], corners[which]
            for extra in range(REACH):
                @pl.when(jnp.logical_not(edge))
                def _():
                    spread(lambda lanes: rows_ref[extra, :, lanes], at + extra, REACH, cols)
                    spread(lambda lanes: corner_ref[extra, :, lanes], at + extra, side_col, REACH)

                @pl.when(edge)
                def _():
                    for ref in (value_in, gate_in):
                        for col in range(wide):
                            ref[pl.ds(source_at(at + extra, col), TILES), :] = zero

        def weights(offset):
            return [taps[2 * pitch * tap + offset + base : 2 * pitch * tap + offset + base + TILES, :] for tap in range(9)]

        value_taps, gate_taps = weights(0), weights(pitch)

        @pl.loop(low, high)
        def _(at):
            cache = {}

            def read(ref, a, col):
                if (id(ref), a, col) not in cache:
                    cache[id(ref), a, col] = ref[pl.ds(source_at(at + a, start_col + col), TILES), :]
                return cache[id(ref), a, col]

            for col in range(cols + 1):
                def conv(ref, kernel):
                    total = None
                    for a in (-1, 0, 1):
                        for b in (-1, 0, 1):
                            term = kernel[3 * (a + 1) + b + 1] * read(ref, a, col + b)
                            total = term if total is None else total + term
                    return total

                value, gate = conv(value_in, value_taps), conv(gate_in, gate_taps)
                squash = jax.nn.sigmoid(gate)
                gated = gate * squash
                glu = value * gated
                place = pl.ds(grad_at(at - 1, start_col + col - 1), TILES)
                value_grad[place, :] = glu * gated
                gate_grad[place, :] = glu * value * (squash + gated * (1.0 - squash))

        @pl.loop(0, rows)
        def _(at):
            for ref, kernel, result in ((value_grad, value_taps, value_out), (gate_grad, gate_taps, gate_out)):
                cache = {}

                def read(a, col):
                    if (a, col) not in cache:
                        cache[a, col] = ref[pl.ds(grad_at(at + a, col), TILES), :]
                    return cache[a, col]

                for col in range(cols):
                    total = None
                    for a in (-1, 0, 1):
                        for b in (-1, 0, 1):
                            term = kernel[3 * (a + 1) + b + 1] * read(1 - a, col + 1 - b)
                            total = term if total is None else total + term
                    result[col * TILES : (col + 1) * TILES, :] = total
            for result, offset in ((value_out, base), (gate_out, lane_tiles + base)):
                for tile in range(count):
                    lanes = slice((offset + tile) * LANES, (offset + tile + 1) * LANES)
                    out_ref[at, :, lanes] = result[pl.ds(tile, cols, stride=TILES), :].astype(jnp.bfloat16)


def edge_slice(block, axis_name, dim, low_side):
    start = jnp.where(low_side, 0, block.shape[dim] - REACH)
    return lax.dynamic_slice_in_dim(block, start, REACH, axis=dim)


def halo_arrays(hidden_pre):
    block = hidden_pre[0]
    height = lax.axis_size("height")
    column = lax.axis_index("width")
    if height == 2:
        edge = edge_slice(block, "height", 0, lax.axis_index("height") == 1)
        halo_rows = [lax.ppermute(edge, "height", SWAP)]
    else:
        up = [(at, at + 1) for at in range(height - 1)]
        down = [(at + 1, at) for at in range(height - 1)]
        halo_rows = [
            lax.ppermute(block[block.shape[0] - REACH :], "height", up),
            lax.ppermute(block[:REACH], "height", down),
        ]
    side = lax.ppermute(edge_slice(block, "width", 1, column == 1), "width", SWAP)
    corners = [lax.ppermute(edge_slice(part, "width", 1, column == 1), "width", SWAP) for part in halo_rows]
    return halo_rows, side, corners


def paired_ffn(hidden_pre, conv_weight):
    halo_rows, side, corners = halo_arrays(hidden_pre)
    block = hidden_pre[0]
    rows, cols, channels = block.shape
    lane_tiles = channels // LANES // 2
    pitch = -(-lane_tiles // TILES) * TILES
    source = pltpu.VMEM(((rows + 2 * REACH) * (cols + 2 * REACH) * TILES, LANES), jnp.float32)
    grad = pltpu.VMEM(((rows + 2) * (cols + 2) * TILES, LANES), jnp.float32)
    result = pltpu.VMEM((cols * TILES, LANES), jnp.float32)
    size = rows * cols * channels
    hidden_grad = vmem_call(
        functools.partial(conv_kernel, rows, len(halo_rows)),
        struct((rows, cols, channels), jnp.bfloat16),
        [pltpu.VMEM((9 * 2 * pitch, LANES), jnp.float32), source, source, grad, grad, result, result],
        n_in=2 * len(halo_rows) + 3, flops=60 * size, bytes_accessed=6 * size,
    )(*halo_rows, side, *corners, block, conv_weight)
    return hidden_grad[None]


def per_device(queries, attn_keys, attn_values, attn_cotangent, clip_ids, hidden_pre, conv_weight):
    paired = (
        lax.axis_size("height") == 2
        and lax.axis_size("width") == 2
        and 3 <= lax.axis_size("tm") <= 4
        and HEADS % 2 == 0
        and queries.shape[0] == 1
    )
    attention = paired_attention if paired else general_attention
    grads = attention(queries, attn_keys, attn_values, attn_cotangent, clip_ids)
    hidden_grad = paired_ffn(hidden_pre, conv_weight) if lax.axis_size("width") == 2 and hidden_pre.shape[0] == 1 and hidden_pre.shape[3] % (2 * LANES) == 0 else mixed_ffn(hidden_pre, conv_weight)
    return (*grads, hidden_grad)


def solution(mesh):
    return jax.shard_map(
        per_device,
        mesh=mesh,
        in_specs=(
            P(("group", "tm"), "height", "width", None),
            P(("group", "tm"), "height", "width", None),
            P(("group", "tm"), "height", "width", None),
            P(("group", "tm"), "height", "width", None),
            P("group"),
            P(("group", "tm"), "height", "width", None),
            P(),
        ),
        out_specs=(
            P(("group", "tm"), "height", "width", None),
            P(("group", "tm"), "height", "width", None),
            P(("group", "tm"), "height", "width", None),
            P(("group", "tm"), "height", "width", None),
        ),
        check_vma=False,
    )
```

```python
import functools
from functools import reduce

import jax
import jax.numpy as jnp
from jax import lax
from jax.experimental import pallas as pl
from jax.experimental.pallas import tpu as pltpu
from jax.sharding import PartitionSpec as P

HEAD_DIM = 112
HEADS = 10


EPSILON = 1e-06
TOP_PRECISION = lax.Precision.HIGHEST


def entering(value, axis, join, neutral, backward):
    count, mine = (lax.axis_size(axis), lax.axis_index(axis))
    pieces = jax.tree.map(lambda part: lax.all_gather(part, axis), value)
    if backward:
        pieces = jax.tree.map(lambda part: part[::-1], pieces)
        mine = count - 1 - mine
    so_far = jax.tree.map(
        lambda part, zero: jnp.full_like(part, 0) + jnp.asarray(zero, part.dtype), value, neutral
    )

    def turn(position, so_far):
        longer = join(so_far, jax.tree.map(lambda part: part[position], pieces))
        return jax.tree.map(lambda new, old: jnp.where(position < mine, new, old), longer, so_far)

    return lax.fori_loop(0, count - 1, turn, so_far)


def padded(block, sides, width):
    for axis, dim in sides:
        count = lax.axis_size(axis)
        forward = [(i, i + 1) for i in range(count - 1)]
        backward = [(target, source) for source, target in forward]
        low = lax.ppermute(
            lax.slice_in_dim(block, block.shape[dim] - width, None, axis=dim), axis, forward
        )
        high = lax.ppermute(lax.slice_in_dim(block, 0, width, axis=dim), axis, backward)
        block = jnp.concatenate([low, block, high], axis=dim)
    return block


def carry_on(earlier, later):
    keeping = 1.0 - later[0]
    return (
        jnp.maximum(earlier[0], later[0]),
        later[1] + keeping * earlier[1],
        later[2] + keeping * earlier[2],
    )


def clip_flags(clip_ids):
    frame = lax.axis_index("tm")
    frame_count = lax.axis_size("tm")
    current = lax.dynamic_index_in_dim(clip_ids, frame, 0, keepdims=False)
    before = lax.dynamic_index_in_dim(clip_ids, jnp.maximum(frame - 1, 0), 0, keepdims=False)
    after = lax.dynamic_index_in_dim(
        clip_ids, jnp.minimum(frame + 1, frame_count - 1), 0, keepdims=False
    )
    starts = jnp.where((frame == 0) | (current != before), 1.0, 0.0).astype(jnp.float32)
    ends = jnp.where((frame == frame_count - 1) | (current != after), 1.0, 0.0).astype(jnp.float32)
    return (starts, ends)


def glu_grad(conv_out, split_at):
    value_part = conv_out[..., :split_at]
    gate_part = conv_out[..., split_at:]
    squash = jax.nn.sigmoid(gate_part)
    glu = value_part * gate_part * squash
    value_gradient = glu * gate_part * squash
    gate_grad = glu * value_part * squash * (1.0 + gate_part * (1.0 - squash))
    return jnp.concatenate([value_gradient, gate_grad], axis=-1)


def depthwise(source, weights, start, sign, height_out, width_out):
    terms = []
    for offset_row in (-1, 0, 1):
        for offset_col in (-1, 0, 1):
            tap_index = (offset_row + 1) * 3 + offset_col + 1
            row_start = start + sign * offset_row
            col_start = start + sign * offset_col
            window = source[
                row_start : row_start + height_out, col_start : col_start + width_out
            ].astype(jnp.float32)
            terms.append(weights[tap_index] * window)
    return reduce(lambda first, second: first + second, terms)


def general_attention(queries, attn_keys, attn_values, attn_cotangent, clip_ids):
    token_count = queries.shape[1] * queries.shape[2]
    flat_width = HEADS * HEAD_DIM
    starts, ends = clip_flags(clip_ids)
    zero_flag = jnp.zeros((), jnp.float32)
    feature_keys = jnp.maximum(attn_keys, 0).reshape(token_count, HEADS, HEAD_DIM)
    value_row_block = attn_values.reshape(token_count, HEADS, HEAD_DIM)
    local_kv = jnp.einsum(
        "jrf,jrx->rfx", feature_keys, value_row_block, preferred_element_type=jnp.float32
    ).reshape(flat_width, HEAD_DIM)
    local_norm = jnp.sum(feature_keys.astype(jnp.float32), axis=0).reshape(flat_width)
    share_kv, share_norm = (
        lax.psum_scatter(local_kv, ("height", "width"), scatter_dimension=0, tiled=True),
        lax.psum_scatter(local_norm, ("height", "width"), scatter_dimension=0, tiled=True),
    )
    earlier = entering(
        (starts, share_kv, share_norm),
        "tm",
        carry_on,
        (zero_flag, jnp.zeros_like(share_kv), jnp.zeros_like(share_norm)),
        False,
    )
    part_kv = share_kv + (1.0 - starts) * earlier[1]
    part_norm = share_norm + (1.0 - starts) * earlier[2]
    state_key_value, state_norm = (
        lax.all_gather(part_kv, ("height", "width"), axis=0, tiled=True),
        lax.all_gather(part_norm, ("height", "width"), axis=0, tiled=True),
    )
    state_key_value = state_key_value.reshape(HEADS, HEAD_DIM, HEAD_DIM)
    state_norm = state_norm.reshape(HEADS, HEAD_DIM)
    feature_query = (
        jnp.maximum(queries, 0).reshape(token_count, HEADS, HEAD_DIM).astype(jnp.float32)
    )
    cotangent = attn_cotangent.reshape(token_count, HEADS, HEAD_DIM).astype(jnp.float32)
    ratio_numerator = jnp.einsum(
        "cob,obq->coq", feature_query, state_key_value, precision=TOP_PRECISION
    )
    denominator = (
        jnp.einsum("thk,hk->th", feature_query, state_norm, precision=TOP_PRECISION) + EPSILON
    )
    attended = ratio_numerator / denominator[..., None]
    scaled_gradient = cotangent / denominator[..., None]
    denominator_grad = -jnp.sum(cotangent * attended, axis=-1) / denominator
    query_feature_gradient = jnp.einsum(
        "dla,lja->dlj", scaled_gradient, state_key_value, precision=TOP_PRECISION
    )
    query_feature_gradient = query_feature_gradient + state_norm[None] * denominator_grad[..., None]
    query_grad = (
        jnp.where(feature_query > 0.0, query_feature_gradient, 0.0)
        .reshape(queries.shape)
        .astype(jnp.bfloat16)
    )
    gradient_key_value = jnp.einsum(
        "jrf,jrx->rfx", feature_query, scaled_gradient, precision=TOP_PRECISION
    ).reshape(flat_width, HEAD_DIM)
    grad_norm = jnp.einsum(
        "thk,th->hk", feature_query, denominator_grad, precision=TOP_PRECISION
    ).reshape(flat_width)
    share_grad_kv, share_grad_norm = (
        lax.psum_scatter(gradient_key_value, ("height", "width"), scatter_dimension=0, tiled=True),
        lax.psum_scatter(grad_norm, ("height", "width"), scatter_dimension=0, tiled=True),
    )
    later = entering(
        (ends, share_grad_kv, share_grad_norm),
        "tm",
        carry_on,
        (zero_flag, jnp.zeros_like(share_grad_kv), jnp.zeros_like(share_grad_norm)),
        True,
    )
    part_grad_kv = share_grad_kv + (1.0 - ends) * later[1]
    part_grad_norm = share_grad_norm + (1.0 - ends) * later[2]
    total_key_value, norm_total = (
        lax.all_gather(part_grad_kv, ("height", "width"), axis=0, tiled=True),
        lax.all_gather(part_grad_norm, ("height", "width"), axis=0, tiled=True),
    )
    total_key_value = total_key_value.reshape(HEADS, HEAD_DIM, HEAD_DIM)
    norm_total = norm_total.reshape(HEADS, HEAD_DIM)
    key_feat_grad = (
        jnp.einsum(
            "dla,lja->dlj",
            value_row_block.astype(jnp.float32),
            total_key_value,
            precision=TOP_PRECISION,
        )
        + norm_total[None]
    )
    key_grad = (
        jnp.where(feature_keys > 0, key_feat_grad, 0.0)
        .reshape(attn_keys.shape)
        .astype(jnp.bfloat16)
    )
    value_gradient = jnp.einsum(
        "cob,obq->coq", feature_keys.astype(jnp.float32), total_key_value, precision=TOP_PRECISION
    )
    value_gradient = value_gradient.reshape(attn_values.shape).astype(jnp.bfloat16)
    return (query_grad, key_grad, value_gradient)


LANES = 128


def split_terms(value):
    high = value.astype(jnp.bfloat16)
    low = (value - high.astype(jnp.float32)).astype(jnp.bfloat16)
    return high, low


def dot_tokens(left, right):
    return lax.dot_general(left, right, (((0,), (0,)), ((), ())), preferred_element_type=jnp.float32)


def dot_rows(left, right):
    return lax.dot_general(left, right, (((1,), (0,)), ((), ())), preferred_element_type=jnp.float32)


def dot_columns(left, right):
    return lax.dot_general(left, right, (((1,), (1,)), ((), ())), preferred_element_type=jnp.float32)


def head_slice(ref, head):
    return ref[:, head * HEAD_DIM : (head + 1) * HEAD_DIM]


def tail_block(rows, first):
    column = lax.broadcasted_iota(jnp.int32, (rows, LANES - HEAD_DIM), 1)
    return jnp.where(column == 0, first, 0.0).astype(jnp.bfloat16)


def vmem_call(kernel, out_shape, scratch=(), smem_first=False, n_in=0, flops=0, bytes_accessed=0, vmem_mib=8, in_hbm=False, out_hbm=False):
    vmem = pl.BlockSpec(memory_space=pltpu.VMEM)
    in_specs = [pl.BlockSpec(memory_space=pltpu.HBM) if in_hbm else vmem] * n_in
    if smem_first:
        in_specs[0] = pl.BlockSpec(memory_space=pltpu.SMEM)
    return pl.pallas_call(
        kernel,
        out_shape=out_shape,
        in_specs=in_specs,
        out_specs=jax.tree.map(lambda _: pl.BlockSpec(memory_space=pltpu.HBM) if out_hbm else vmem, out_shape),
        scratch_shapes=list(scratch),
        cost_estimate=pl.CostEstimate(flops=flops, bytes_accessed=bytes_accessed, transcendentals=0),
        compiler_params=pltpu.CompilerParams(vmem_limit_bytes=vmem_mib << 20),
    )


PARTS = 4


def stage(sources, targets, sems):
    copies = []
    for at, (source, target) in enumerate(zip(sources, targets)):
        rows = source.shape[0] // PARTS
        for part in range(PARTS):
            span = pl.ds(part * rows, rows)
            copies.append(pltpu.make_async_copy(source.at[span], target.at[span], sems.at[at, part]))
    for copy in copies:
        copy.start()
    for copy in copies:
        copy.wait()


def state_kernel(key_hbm, value_hbm, keep_ref, send_ref, halves, key_ref, value_ref, sems):
    stage((key_hbm, value_hbm), (key_ref, value_ref), sems)
    tokens = key_ref.shape[0]
    one = tail_block(tokens, 1.0)
    half = halves.shape[2]
    per_group = HEADS // 2
    column = lax.axis_index("width")
    for group in range(2):
        for place in range(per_group):
            head = group * per_group + place
            feature = jnp.maximum(head_slice(key_ref, head), 0)
            wide = jnp.concatenate([head_slice(value_ref, head), one], axis=1)
            store_rows(halves, group, place * HEAD_DIM, dot_tokens(feature, wide), half)
    keep_ref[...] = halves[column]
    send_ref[...] = halves[1 - column]


def store_rows(halves, group, first, block, half):
    cut = min(max(half - first, 0), HEAD_DIM)
    if cut:
        index = (0, group) if group is not None else (0,)
        halves[(*index, slice(first, first + cut))] = block[:cut]
    if cut < HEAD_DIM:
        index = (1, group) if group is not None else (1,)
        start = first + cut - half
        halves[(*index, slice(start, start + HEAD_DIM - cut))] = block[cut:]


def pick_kernel(keep_ref, came_ref, mine_ref, other_ref):
    row = lax.axis_index("height")
    mine_ref[...] = keep_ref[row] + came_ref[row]
    other_ref[...] = keep_ref[1 - row] + came_ref[1 - row]


def heads_kernel(query_hbm, cotangent_hbm, mine_ref, other_ref, groups, query_ref, cotangent_ref, sems):
    stage((query_hbm, cotangent_hbm), (query_ref, cotangent_ref), sems)
    none = tail_block(query_ref.shape[0], 0.0)
    per_group = HEADS // 2
    row = lax.axis_index("height")
    for head in range(HEADS):
        group, place = divmod(head, per_group)
        feature = jnp.maximum(head_slice(query_ref, head), 0)
        groups[group, 0, place] = jnp.concatenate([feature, none], axis=1)
        groups[group, 1, place] = jnp.concatenate([head_slice(cotangent_ref, head), none], axis=1)
    mine_ref[...] = groups[row]
    other_ref[...] = groups[1 - row]


def mask_kernel(clip_ref, out_ref):
    frame = lax.axis_index("tm")
    last = lax.axis_size("tm") - 1
    here = clip_ref[frame]
    line = lax.broadcasted_iota(jnp.int32, out_ref.shape, 0)
    masks = jnp.zeros(out_ref.shape, jnp.float32)
    for at, (step, hop) in enumerate(((1, 1), (1, 2), (-1, 1), (-1, 2))):
        other = frame - step * hop
        inside = (other >= 0) & (other <= last)
        same = inside & (clip_ref[jnp.clip(other, 0, last)] == here)
        masks = jnp.where(line == at, jnp.where(same, 1.0, 0.0), masks)
    out_ref[...] = masks


def query_kernel(state_ref, came_ref, mine_ref, other_ref, keep_ref, send_ref, own_out, other_out, state, halves):
    column = lax.axis_index("width")
    half = state_ref.shape[0]
    per_group = HEADS // 2
    tokens = mine_ref.shape[2]
    state[column] = state_ref[...]
    state[1 - column] = came_ref[...]
    lane = lax.broadcasted_iota(jnp.int32, (2 * tokens, LANES), 1)
    for place in range(per_group):
        feature = jnp.concatenate([mine_ref[0, place], other_ref[0, place]], axis=0)
        cotangent = jnp.concatenate([mine_ref[1, place], other_ref[1, place]], axis=0).astype(jnp.float32)
        high, low = split_terms(load_rows(state, place * HEAD_DIM, half))
        narrow = feature[:, :HEAD_DIM]
        product = dot_rows(narrow, high) + dot_rows(narrow, low)
        inverse = 1.0 / (product[:, HEAD_DIM : HEAD_DIM + 1] + EPSILON)
        against = jnp.sum(cotangent * product, axis=1, keepdims=True)
        norm_grad = -(against * inverse) * inverse
        scaled = jnp.where(lane == HEAD_DIM, norm_grad, cotangent * inverse)
        scaled_high, scaled_low = split_terms(scaled)
        grad = dot_tokens(narrow, scaled_high) + dot_tokens(narrow, scaled_low)
        store_rows(halves, None, place * HEAD_DIM, grad, half)
        back = dot_columns(scaled_high, high) + dot_columns(scaled_high, low) + dot_columns(scaled_low, high)
        back = jnp.where(narrow > 0, back, 0.0).astype(jnp.bfloat16)
        own_out[place, :, :HEAD_DIM] = back[:tokens]
        other_out[place, :, :HEAD_DIM] = back[tokens:]
    keep_ref[...] = halves[column]
    send_ref[...] = halves[1 - column]


def load_rows(state, first, half):
    cut = min(max(half - first, 0), HEAD_DIM)
    parts = []
    if cut:
        parts.append(state[0, first : first + cut])
    if cut < HEAD_DIM:
        start = first + cut - half
        parts.append(state[1, start : start + HEAD_DIM - cut])
    return parts[0] if len(parts) == 1 else jnp.concatenate(parts, axis=0)


def key_heads(key_ref, value_ref, total, half, group, place, one):
    head = group * (HEADS // 2) + place
    feature = jnp.maximum(head_slice(key_ref, head), 0)
    wide = jnp.concatenate([head_slice(value_ref, head), one], axis=1)
    high, low = split_terms(load_rows(total, place * HEAD_DIM, half))
    grad = dot_columns(wide, high) + dot_columns(wide, low)
    product = dot_rows(feature, high) + dot_rows(feature, low)
    return jnp.where(feature > 0, grad, 0.0).astype(jnp.bfloat16), product[:, :HEAD_DIM].astype(jnp.bfloat16)


def key_kernel(mine, key_ref, value_ref, here_ref, came_ref, *refs):
    column, row = lax.axis_index("width"), lax.axis_index("height")
    half = here_ref.shape[0]
    given, (key_out, value_out, total) = refs[:-3], refs[-3:]
    total[column] = here_ref[...]
    total[1 - column] = came_ref[...]
    one = tail_block(key_ref.shape[0], 1.0)
    for group in range(2):
        @pl.when(row == (group if mine else 1 - group))
        def _():
            for place in range(HEADS // 2):
                grads = key_heads(key_ref, value_ref, total, half, group, place, one)
                for at, out in enumerate((key_out, value_out)):
                    if mine:
                        out[place, :, :HEAD_DIM] = grads[at]
                        continue
                    for which, part in ((group, grads[at]), (1 - group, given[at][place, :, :HEAD_DIM])):
                        first = (which * (HEADS // 2) + place) * HEAD_DIM
                        out[:, first : first + HEAD_DIM] = part


def join_kernel(mine_ref, came_ref, out_ref):
    row = lax.axis_index("height")
    per_group = HEADS // 2
    for place in range(per_group):
        mine, came = mine_ref[place, :, :HEAD_DIM], came_ref[place, :, :HEAD_DIM]
        first = jnp.where(row == 0, mine, came)
        second = jnp.where(row == 0, came, mine)
        out_ref[:, place * HEAD_DIM : (place + 1) * HEAD_DIM] = first
        at = (per_group + place) * HEAD_DIM
        out_ref[:, at : at + HEAD_DIM] = second


def struct(shape, dtype=jnp.float32):
    return jax.ShapeDtypeStruct(shape, dtype)


SWAP = [(0, 1), (1, 0)]


def paired(queries, attn_keys, attn_values, attn_cotangent, clip_ids, hidden_pre, conv_weight):
    tokens = queries.shape[1] * queries.shape[2]
    flat = HEADS * HEAD_DIM
    per_group = HEADS // 2
    half = per_group * HEAD_DIM // 2
    frames = lax.axis_size("tm")
    query, key, value, cotangent = (
        part.reshape(tokens, flat) for part in (queries, attn_keys, attn_values, attn_cotangent)
    )
    share = struct((half, LANES))
    pair = struct((2, half, LANES))

    masks = vmem_call(mask_kernel, struct((8, LANES)), smem_first=True, n_in=1, bytes_accessed=4096)(
        pltpu.with_memory_space_constraint(clip_ids, pltpu.HBM)
    )
    key_hbm, value_hbm = (
        pltpu.with_memory_space_constraint(part, pltpu.HBM) for part in (key, value)
    )
    staged = [pltpu.VMEM((tokens, flat), jnp.bfloat16)] * 2 + [pltpu.SemaphoreType.DMA((2, PARTS))]
    keep, send = vmem_call(
        state_kernel, (pair, pair), [pltpu.VMEM((2, 2, half, LANES), jnp.float32), *staged], n_in=2, in_hbm=True,
        flops=2 * tokens * flat * LANES, bytes_accessed=4 * tokens * flat + 8 * half * LANES * 2,
    )(key_hbm, value_hbm)
    came = lax.ppermute(send, "width", SWAP)
    mine, other = vmem_call(pick_kernel, (share, share), n_in=2, bytes_accessed=24 * half * LANES)(keep, came)
    came = lax.ppermute(other, "height", SWAP)

    packed = struct((2, per_group, tokens, LANES), jnp.bfloat16)
    query, cotangent, mine = lax.optimization_barrier((query, cotangent, mine))
    heads_mine, heads_other = vmem_call(
        heads_kernel, (packed, packed), [pltpu.VMEM((2, 2, per_group, tokens, LANES), jnp.bfloat16), *staged], n_in=2, in_hbm=True,
        bytes_accessed=12 * tokens * flat,
    )(*(pltpu.with_memory_space_constraint(part, pltpu.HBM) for part in (query, cotangent)))
    _, own = lax.optimization_barrier((heads_other, mine + came))
    heads_sent = lax.ppermute(heads_other, "height", SWAP)

    def along_frames(own, step, beside):
        moves = [[(at, at + step * hop) for at in range(frames) if 0 <= at + step * hop < frames] for hop in (1, 2)]
        near = lax.ppermute(own, "tm", moves[0])
        far = lax.ppermute(own, "tm", moves[1])
        near, far, beside = beside(own, near, far)
        at = 0 if step > 0 else 2
        return own + masks[at : at + 1] * near + masks[at + 1 : at + 2] * far, beside

    def fetch(own, near, far):
        block, _ = lax.optimization_barrier((hidden_pre, own))
        near, far, arrived = lax.optimization_barrier((near, far, heads_sent))
        return near, far, (halo_arrays(block), arrived)

    state, (halo, heads_came) = along_frames(own, 1, fetch)
    came = lax.ppermute(state, "width", SWAP)
    back = struct((per_group, tokens, LANES), jnp.bfloat16)
    keep, send, back_mine, back_other = vmem_call(
        query_kernel, (share, share, back, back),
        [pltpu.VMEM((2, half, LANES), jnp.float32), pltpu.VMEM((2, half, LANES), jnp.float32)], n_in=4,
        flops=14 * tokens * flat * LANES, bytes_accessed=8 * tokens * flat,
    )(state, came, heads_mine, heads_came)
    came = lax.ppermute(send, "width", SWAP)
    own = keep + came

    def convolve(own, near, far):
        other, _ = lax.optimization_barrier((back_other, own))
        back_came = lax.ppermute(other, "height", SWAP)
        hidden_grad = ffn(hidden_pre, conv_weight, halo)
        query_grad = vmem_call(
            join_kernel, struct((tokens, flat), jnp.bfloat16), n_in=2, bytes_accessed=4 * tokens * flat
        )(back_mine, back_came)
        near, far, grads = lax.optimization_barrier((near, far, (query_grad, hidden_grad)))
        return near, far, grads

    total, (query_grad, hidden_grad) = along_frames(own, -1, convolve)
    far = lax.ppermute(total, "height", SWAP)
    near_came = lax.ppermute(total, "width", SWAP)
    state = [pltpu.VMEM((2, half, LANES), jnp.float32)]
    cost = {"flops": 4 * tokens * flat * LANES, "bytes_accessed": 4 * tokens * flat}
    near_grads = vmem_call(functools.partial(key_kernel, True), (back, back), state, n_in=4, **cost)(
        key, value, total, near_came
    )
    far_came = lax.ppermute(far, "width", SWAP)
    out = struct((tokens, flat), jnp.bfloat16)
    key_grad, value_gradient = vmem_call(functools.partial(key_kernel, False), (out, out), state, n_in=6, **cost)(
        key, value, far, far_came, *near_grads
    )
    grads = tuple(part.reshape(queries.shape) for part in (query_grad, key_grad, value_gradient))
    return (*grads, hidden_grad)


def mixed_ffn(hidden_pre, conv_weight):
    row_count = hidden_pre.shape[1]
    col_count = hidden_pre.shape[2]
    split_at = hidden_pre.shape[3] // 2
    widened = padded(hidden_pre, (("height", 1), ("width", 2)), 2)[0]
    conv_out = depthwise(widened, conv_weight, 1, 1, row_count + 2, col_count + 2)
    row_global = lax.axis_index("height") * row_count + jnp.arange(row_count + 2) - 1
    col_global = lax.axis_index("width") * col_count + jnp.arange(col_count + 2) - 1
    row_inside = (row_global >= 0) & (row_global < row_count * lax.axis_size("height"))
    col_inside = (col_global >= 0) & (col_global < col_count * lax.axis_size("width"))
    inside = (row_inside[:, None] & col_inside[None, :]).astype(jnp.float32)
    conv_grad = glu_grad(conv_out, split_at) * inside[:, :, None]
    hidden_grad = depthwise(conv_grad, conv_weight, 1, -1, row_count, col_count)
    hidden_grad = hidden_grad[None].astype(jnp.bfloat16)
    return hidden_grad


TILES = 8
REACH = 2


def conv_kernel(rows_per_frame, row_refs, *refs):
    halo_rows, refs = refs[:row_refs], refs[row_refs:]
    side_ref, refs = refs[0], refs[1:]
    corners, refs = refs[:row_refs], refs[row_refs:]
    block_ref, weight_ref, out_hbm, taps, value_in, gate_in, value_grad, gate_grad, value_out, gate_out, out_ref, sems = refs
    rows, cols, channels = block_ref.shape
    lane_tiles = channels // LANES // 2
    pitch = -(-lane_tiles // TILES) * TILES
    row, column = lax.axis_index("height"), lax.axis_index("width")
    first_row, last_row = row == 0, row == lax.axis_size("height") - 1
    wide, tall = cols + 2 * REACH, rows + 2 * REACH
    grad_wide = wide - 2

    for tile in range(2 * lane_tiles):
        place = tile if tile < lane_tiles else pitch + tile - lane_tiles
        taps[pl.ds(place, 9, stride=2 * pitch), :] = weight_ref[:, tile * LANES : (tile + 1) * LANES]

    def source_at(at_row, at_col):
        return pl.multiple_of((at_row * wide + at_col) * TILES, TILES)

    def grad_at(at_row, at_col):
        return pl.multiple_of((at_row * grad_wide + at_col) * TILES, TILES)

    zero = jnp.zeros((TILES, LANES), jnp.float32)
    low_border = jnp.where(first_row, 0, rows + REACH)
    outer_col = jnp.where(column == 0, 0, cols + REACH)
    side_col = jnp.where(column == 0, cols + REACH, 0)
    grad_outer_col = jnp.where(column == 0, 0, grad_wide - 1)
    start_col = jnp.where(column == 0, REACH, REACH - 1)
    low, high = jnp.where(first_row, REACH, REACH - 1), jnp.where(last_row, rows + REACH, rows + REACH + 1)

    for ref in (value_in, gate_in):
        @pl.loop(0, tall)
        def _(at):
            for extra in range(REACH):
                ref[pl.ds(source_at(at, outer_col + extra), TILES), :] = zero

    for ref in (value_grad, gate_grad):
        @pl.loop(0, rows + 2)
        def _(at):
            ref[pl.ds(grad_at(at, grad_outer_col), TILES), :] = zero

        for edge, at in ((first_row, 0), (last_row, rows + 1)):
            @pl.when(edge)
            def _():
                for col in range(grad_wide):
                    ref[pl.ds(grad_at(at, col), TILES), :] = zero

    copies = []
    for base in range(0, lane_tiles, TILES):
        count = min(TILES, lane_tiles - base)

        def spread(load, at_row, at_col, length):
            for ref, offset in ((value_in, base), (gate_in, lane_tiles + base)):
                for tile in range(count):
                    part = load(slice((offset + tile) * LANES, (offset + tile + 1) * LANES)).astype(jnp.float32)
                    ref[pl.ds(source_at(at_row, at_col) + tile, length, stride=TILES), :] = part

        @pl.loop(0, rows)
        def _(at):
            spread(lambda lanes: block_ref[at, :, lanes], at + REACH, REACH, cols)
            spread(lambda lanes: side_ref[at, :, lanes], at + REACH, side_col, REACH)

        for edge, at, which in ((first_row, 0, 0), (last_row, rows + REACH, row_refs - 1)):
            rows_ref, corner_ref = halo_rows[which], corners[which]
            for extra in range(REACH):
                @pl.when(jnp.logical_not(edge))
                def _():
                    spread(lambda lanes: rows_ref[extra, :, lanes], at + extra, REACH, cols)
                    spread(lambda lanes: corner_ref[extra, :, lanes], at + extra, side_col, REACH)

                @pl.when(edge)
                def _():
                    for ref in (value_in, gate_in):
                        for col in range(wide):
                            ref[pl.ds(source_at(at + extra, col), TILES), :] = zero

        def weights(offset):
            return [taps[2 * pitch * tap + offset + base : 2 * pitch * tap + offset + base + TILES, :] for tap in range(9)]

        value_taps, gate_taps = weights(0), weights(pitch)

        @pl.loop(low, high)
        def _(at):
            cache = {}

            def read(ref, a, col):
                if (id(ref), a, col) not in cache:
                    cache[id(ref), a, col] = ref[pl.ds(source_at(at + a, start_col + col), TILES), :]
                return cache[id(ref), a, col]

            for col in range(cols + 1):
                def conv(ref, kernel):
                    total = None
                    for a in (-1, 0, 1):
                        for b in (-1, 0, 1):
                            term = kernel[3 * (a + 1) + b + 1] * read(ref, a, col + b)
                            total = term if total is None else total + term
                    return total

                value, gate = conv(value_in, value_taps), conv(gate_in, gate_taps)
                squash = jax.nn.sigmoid(gate)
                gated = gate * squash
                glu = value * gated
                place = pl.ds(grad_at(at - 1, start_col + col - 1), TILES)
                value_grad[place, :] = glu * gated
                gate_grad[place, :] = glu * value * (squash + gated * (1.0 - squash))

        @pl.loop(0, rows)
        def _(at):
            for ref, kernel, result in ((value_grad, value_taps, value_out), (gate_grad, gate_taps, gate_out)):
                cache = {}

                def read(a, col):
                    if (a, col) not in cache:
                        cache[a, col] = ref[pl.ds(grad_at(at + a, col), TILES), :]
                    return cache[a, col]

                for col in range(cols):
                    total = None
                    for a in (-1, 0, 1):
                        for b in (-1, 0, 1):
                            term = kernel[3 * (a + 1) + b + 1] * read(1 - a, col + 1 - b)
                            total = term if total is None else total + term
                    result[col * TILES : (col + 1) * TILES, :] = total
            for result, offset in ((value_out, base), (gate_out, lane_tiles + base)):
                for tile in range(count):
                    lanes = slice((offset + tile) * LANES, (offset + tile + 1) * LANES)
                    out_ref[at, :, lanes] = result[pl.ds(tile, cols, stride=TILES), :].astype(jnp.bfloat16)

        for at, offset in enumerate((base, lane_tiles + base)):
            lanes = pl.ds(offset * LANES, count * LANES)
            copy = pltpu.make_async_copy(out_ref.at[:, :, lanes], out_hbm.at[:, :, lanes], sems.at[at, base // TILES])
            copy.start()
            copies.append(copy)
    for copy in copies:
        copy.wait()


def edge_slice(block, axis_name, dim, low_side):
    start = jnp.where(low_side, 0, block.shape[dim] - REACH)
    return lax.dynamic_slice_in_dim(block, start, REACH, axis=dim)


def halo_arrays(hidden_pre):
    block = hidden_pre[0]
    height = lax.axis_size("height")
    column = lax.axis_index("width")
    if height == 2:
        edge = edge_slice(block, "height", 0, lax.axis_index("height") == 1)
        halo_rows = [lax.ppermute(edge, "height", SWAP)]
    else:
        up = [(at, at + 1) for at in range(height - 1)]
        down = [(at + 1, at) for at in range(height - 1)]
        halo_rows = [
            lax.ppermute(block[block.shape[0] - REACH :], "height", up),
            lax.ppermute(block[:REACH], "height", down),
        ]
    side = lax.ppermute(edge_slice(block, "width", 1, column == 1), "width", SWAP)
    corners = [lax.ppermute(edge_slice(part, "width", 1, column == 1), "width", SWAP) for part in halo_rows]
    return halo_rows, side, corners


def ffn(hidden_pre, conv_weight, halo):
    halo_rows, side, corners = halo
    block = hidden_pre[0]
    rows, cols, channels = block.shape
    lane_tiles = channels // LANES // 2
    pitch = -(-lane_tiles // TILES) * TILES
    source = pltpu.VMEM(((rows + 2 * REACH) * (cols + 2 * REACH) * TILES, LANES), jnp.float32)
    grad = pltpu.VMEM(((rows + 2) * (cols + 2) * TILES, LANES), jnp.float32)
    result = pltpu.VMEM((cols * TILES, LANES), jnp.float32)
    size = rows * cols * channels
    hidden_grad = vmem_call(
        functools.partial(conv_kernel, rows, len(halo_rows)),
        struct((rows, cols, channels), jnp.bfloat16),
        [pltpu.VMEM((9 * 2 * pitch, LANES), jnp.float32), source, source, grad, grad, result, result,
         pltpu.VMEM((rows, cols, channels), jnp.bfloat16), pltpu.SemaphoreType.DMA((2, pitch // TILES))],
        n_in=2 * len(halo_rows) + 3, flops=2 * size, bytes_accessed=size, vmem_mib=12, out_hbm=True,
    )(*halo_rows, side, *corners, block, conv_weight)
    return hidden_grad[None]


def per_device(queries, attn_keys, attn_values, attn_cotangent, clip_ids, hidden_pre, conv_weight):
    blocked = lax.axis_size("width") == 2 and hidden_pre.shape[0] == 1 and hidden_pre.shape[3] % (2 * LANES) == 0
    pairs = lax.axis_size("height") == 2 and 3 <= lax.axis_size("tm") <= 4 and HEADS % 2 == 0
    if blocked and pairs:
        return paired(queries, attn_keys, attn_values, attn_cotangent, clip_ids, hidden_pre, conv_weight)
    grads = general_attention(queries, attn_keys, attn_values, attn_cotangent, clip_ids)
    if blocked:
        return (*grads, ffn(hidden_pre, conv_weight, halo_arrays(hidden_pre)))
    return (*grads, mixed_ffn(hidden_pre, conv_weight))


def solution(mesh):
    return jax.shard_map(
        per_device,
        mesh=mesh,
        in_specs=(
            P(("group", "tm"), "height", "width", None),
            P(("group", "tm"), "height", "width", None),
            P(("group", "tm"), "height", "width", None),
            P(("group", "tm"), "height", "width", None),
            P("group"),
            P(("group", "tm"), "height", "width", None),
            P(),
        ),
        out_specs=(
            P(("group", "tm"), "height", "width", None),
            P(("group", "tm"), "height", "width", None),
            P(("group", "tm"), "height", "width", None),
            P(("group", "tm"), "height", "width", None),
        ),
        check_vma=False,
    )
```

```python
import functools
from functools import reduce

import jax
import jax.numpy as jnp
from jax import lax
from jax.experimental import pallas as pl
from jax.experimental.pallas import tpu as pltpu
from jax.sharding import PartitionSpec as P

HEAD_DIM = 112
HEADS = 10


EPSILON = 1e-06
TOP_PRECISION = lax.Precision.HIGHEST


def entering(value, axis, join, neutral, backward):
    count, mine = (lax.axis_size(axis), lax.axis_index(axis))
    pieces = jax.tree.map(lambda part: lax.all_gather(part, axis), value)
    if backward:
        pieces = jax.tree.map(lambda part: part[::-1], pieces)
        mine = count - 1 - mine
    so_far = jax.tree.map(
        lambda part, zero: jnp.full_like(part, 0) + jnp.asarray(zero, part.dtype), value, neutral
    )

    def turn(position, so_far):
        longer = join(so_far, jax.tree.map(lambda part: part[position], pieces))
        return jax.tree.map(lambda new, old: jnp.where(position < mine, new, old), longer, so_far)

    return lax.fori_loop(0, count - 1, turn, so_far)


def padded(block, sides, width):
    for axis, dim in sides:
        count = lax.axis_size(axis)
        forward = [(i, i + 1) for i in range(count - 1)]
        backward = [(target, source) for source, target in forward]
        low = lax.ppermute(
            lax.slice_in_dim(block, block.shape[dim] - width, None, axis=dim), axis, forward
        )
        high = lax.ppermute(lax.slice_in_dim(block, 0, width, axis=dim), axis, backward)
        block = jnp.concatenate([low, block, high], axis=dim)
    return block


def carry_on(earlier, later):
    keeping = 1.0 - later[0]
    return (
        jnp.maximum(earlier[0], later[0]),
        later[1] + keeping * earlier[1],
        later[2] + keeping * earlier[2],
    )


def clip_flags(clip_ids):
    frame = lax.axis_index("tm")
    frame_count = lax.axis_size("tm")
    current = lax.dynamic_index_in_dim(clip_ids, frame, 0, keepdims=False)
    before = lax.dynamic_index_in_dim(clip_ids, jnp.maximum(frame - 1, 0), 0, keepdims=False)
    after = lax.dynamic_index_in_dim(
        clip_ids, jnp.minimum(frame + 1, frame_count - 1), 0, keepdims=False
    )
    starts = jnp.where((frame == 0) | (current != before), 1.0, 0.0).astype(jnp.float32)
    ends = jnp.where((frame == frame_count - 1) | (current != after), 1.0, 0.0).astype(jnp.float32)
    return (starts, ends)


def glu_grad(conv_out, split_at):
    value_part = conv_out[..., :split_at]
    gate_part = conv_out[..., split_at:]
    squash = jax.nn.sigmoid(gate_part)
    glu = value_part * gate_part * squash
    value_gradient = glu * gate_part * squash
    gate_grad = glu * value_part * squash * (1.0 + gate_part * (1.0 - squash))
    return jnp.concatenate([value_gradient, gate_grad], axis=-1)


def depthwise(source, weights, start, sign, height_out, width_out):
    terms = []
    for offset_row in (-1, 0, 1):
        for offset_col in (-1, 0, 1):
            tap_index = (offset_row + 1) * 3 + offset_col + 1
            row_start = start + sign * offset_row
            col_start = start + sign * offset_col
            window = source[
                row_start : row_start + height_out, col_start : col_start + width_out
            ].astype(jnp.float32)
            terms.append(weights[tap_index] * window)
    return reduce(lambda first, second: first + second, terms)


def general_attention(queries, attn_keys, attn_values, attn_cotangent, clip_ids):
    token_count = queries.shape[1] * queries.shape[2]
    flat_width = HEADS * HEAD_DIM
    starts, ends = clip_flags(clip_ids)
    zero_flag = jnp.zeros((), jnp.float32)
    feature_keys = jnp.maximum(attn_keys, 0).reshape(token_count, HEADS, HEAD_DIM)
    value_row_block = attn_values.reshape(token_count, HEADS, HEAD_DIM)
    local_kv = jnp.einsum(
        "jrf,jrx->rfx", feature_keys, value_row_block, preferred_element_type=jnp.float32
    ).reshape(flat_width, HEAD_DIM)
    local_norm = jnp.sum(feature_keys.astype(jnp.float32), axis=0).reshape(flat_width)
    share_kv, share_norm = (
        lax.psum_scatter(local_kv, ("height", "width"), scatter_dimension=0, tiled=True),
        lax.psum_scatter(local_norm, ("height", "width"), scatter_dimension=0, tiled=True),
    )
    earlier = entering(
        (starts, share_kv, share_norm),
        "tm",
        carry_on,
        (zero_flag, jnp.zeros_like(share_kv), jnp.zeros_like(share_norm)),
        False,
    )
    part_kv = share_kv + (1.0 - starts) * earlier[1]
    part_norm = share_norm + (1.0 - starts) * earlier[2]
    state_key_value, state_norm = (
        lax.all_gather(part_kv, ("height", "width"), axis=0, tiled=True),
        lax.all_gather(part_norm, ("height", "width"), axis=0, tiled=True),
    )
    state_key_value = state_key_value.reshape(HEADS, HEAD_DIM, HEAD_DIM)
    state_norm = state_norm.reshape(HEADS, HEAD_DIM)
    feature_query = (
        jnp.maximum(queries, 0).reshape(token_count, HEADS, HEAD_DIM).astype(jnp.float32)
    )
    cotangent = attn_cotangent.reshape(token_count, HEADS, HEAD_DIM).astype(jnp.float32)
    ratio_numerator = jnp.einsum(
        "cob,obq->coq", feature_query, state_key_value, precision=TOP_PRECISION
    )
    denominator = (
        jnp.einsum("thk,hk->th", feature_query, state_norm, precision=TOP_PRECISION) + EPSILON
    )
    attended = ratio_numerator / denominator[..., None]
    scaled_gradient = cotangent / denominator[..., None]
    denominator_grad = -jnp.sum(cotangent * attended, axis=-1) / denominator
    query_feature_gradient = jnp.einsum(
        "dla,lja->dlj", scaled_gradient, state_key_value, precision=TOP_PRECISION
    )
    query_feature_gradient = query_feature_gradient + state_norm[None] * denominator_grad[..., None]
    query_grad = (
        jnp.where(feature_query > 0.0, query_feature_gradient, 0.0)
        .reshape(queries.shape)
        .astype(jnp.bfloat16)
    )
    gradient_key_value = jnp.einsum(
        "jrf,jrx->rfx", feature_query, scaled_gradient, precision=TOP_PRECISION
    ).reshape(flat_width, HEAD_DIM)
    grad_norm = jnp.einsum(
        "thk,th->hk", feature_query, denominator_grad, precision=TOP_PRECISION
    ).reshape(flat_width)
    share_grad_kv, share_grad_norm = (
        lax.psum_scatter(gradient_key_value, ("height", "width"), scatter_dimension=0, tiled=True),
        lax.psum_scatter(grad_norm, ("height", "width"), scatter_dimension=0, tiled=True),
    )
    later = entering(
        (ends, share_grad_kv, share_grad_norm),
        "tm",
        carry_on,
        (zero_flag, jnp.zeros_like(share_grad_kv), jnp.zeros_like(share_grad_norm)),
        True,
    )
    part_grad_kv = share_grad_kv + (1.0 - ends) * later[1]
    part_grad_norm = share_grad_norm + (1.0 - ends) * later[2]
    total_key_value, norm_total = (
        lax.all_gather(part_grad_kv, ("height", "width"), axis=0, tiled=True),
        lax.all_gather(part_grad_norm, ("height", "width"), axis=0, tiled=True),
    )
    total_key_value = total_key_value.reshape(HEADS, HEAD_DIM, HEAD_DIM)
    norm_total = norm_total.reshape(HEADS, HEAD_DIM)
    key_feat_grad = (
        jnp.einsum(
            "dla,lja->dlj",
            value_row_block.astype(jnp.float32),
            total_key_value,
            precision=TOP_PRECISION,
        )
        + norm_total[None]
    )
    key_grad = (
        jnp.where(feature_keys > 0, key_feat_grad, 0.0)
        .reshape(attn_keys.shape)
        .astype(jnp.bfloat16)
    )
    value_gradient = jnp.einsum(
        "cob,obq->coq", feature_keys.astype(jnp.float32), total_key_value, precision=TOP_PRECISION
    )
    value_gradient = value_gradient.reshape(attn_values.shape).astype(jnp.bfloat16)
    return (query_grad, key_grad, value_gradient)


LANES = 128


def split_terms(value):
    high = value.astype(jnp.bfloat16)
    low = (value - high.astype(jnp.float32)).astype(jnp.bfloat16)
    return high, low


def dot_tokens(left, right):
    return lax.dot_general(left, right, (((0,), (0,)), ((), ())), preferred_element_type=jnp.float32)


def dot_rows(left, right):
    return lax.dot_general(left, right, (((1,), (0,)), ((), ())), preferred_element_type=jnp.float32)


def dot_columns(left, right):
    return lax.dot_general(left, right, (((1,), (1,)), ((), ())), preferred_element_type=jnp.float32)


def head_slice(ref, head):
    return ref[:, head * HEAD_DIM : (head + 1) * HEAD_DIM]


def tail_block(rows, first):
    column = lax.broadcasted_iota(jnp.int32, (rows, LANES - HEAD_DIM), 1)
    return jnp.where(column == 0, first, 0.0).astype(jnp.bfloat16)


def vmem_call(kernel, out_shape, scratch=(), smem_first=False, n_in=0, flops=0, bytes_accessed=0, vmem_mib=8, in_hbm=False, out_hbm=False, n_given=0):
    vmem = pl.BlockSpec(memory_space=pltpu.VMEM)
    in_specs = [pl.BlockSpec(memory_space=pltpu.HBM) if in_hbm else vmem] * n_in
    in_specs += [pl.BlockSpec(memory_space=pltpu.HBM)] * n_given
    if smem_first:
        in_specs[0] = pl.BlockSpec(memory_space=pltpu.SMEM)
    return pl.pallas_call(
        kernel,
        out_shape=out_shape,
        in_specs=in_specs,
        out_specs=jax.tree.map(lambda _: pl.BlockSpec(memory_space=pltpu.HBM) if out_hbm else vmem, out_shape),
        scratch_shapes=list(scratch),
        input_output_aliases={n_in: 0} if n_given else {},
        cost_estimate=pl.CostEstimate(flops=flops, bytes_accessed=bytes_accessed, transcendentals=0),
        compiler_params=pltpu.CompilerParams(vmem_limit_bytes=vmem_mib << 20),
    )


PARTS = 4


def stage(sources, targets, sems):
    copies = []
    for at, (source, target) in enumerate(zip(sources, targets)):
        rows = source.shape[0] // PARTS
        for part in range(PARTS):
            span = pl.ds(part * rows, rows)
            copies.append(pltpu.make_async_copy(source.at[span], target.at[span], sems.at[at, part]))
    for copy in copies:
        copy.start()
    for copy in copies:
        copy.wait()


def state_kernel(key_hbm, value_hbm, keep_ref, send_ref, halves, key_ref, value_ref, sems):
    stage((key_hbm, value_hbm), (key_ref, value_ref), sems)
    tokens = key_ref.shape[0]
    one = tail_block(tokens, 1.0)
    half = halves.shape[2]
    per_group = HEADS // 2
    column = lax.axis_index("width")
    for group in range(2):
        for place in range(per_group):
            head = group * per_group + place
            feature = jnp.maximum(head_slice(key_ref, head), 0)
            wide = jnp.concatenate([head_slice(value_ref, head), one], axis=1)
            store_rows(halves, group, place * HEAD_DIM, dot_tokens(feature, wide), half)
    keep_ref[...] = halves[column]
    send_ref[...] = halves[1 - column]


def store_rows(halves, group, first, block, half):
    cut = min(max(half - first, 0), HEAD_DIM)
    if cut:
        index = (0, group) if group is not None else (0,)
        halves[(*index, slice(first, first + cut))] = block[:cut]
    if cut < HEAD_DIM:
        index = (1, group) if group is not None else (1,)
        start = first + cut - half
        halves[(*index, slice(start, start + HEAD_DIM - cut))] = block[cut:]


def pick_kernel(keep_ref, came_ref, mine_ref, other_ref):
    row = lax.axis_index("height")
    mine_ref[...] = keep_ref[row] + came_ref[row]
    other_ref[...] = keep_ref[1 - row] + came_ref[1 - row]


def write_masks(clip_ref, out_ref):
    frame = lax.axis_index("tm")
    last = lax.axis_size("tm") - 1
    here = clip_ref[frame]
    line = lax.broadcasted_iota(jnp.int32, out_ref.shape, 0)
    masks = jnp.zeros(out_ref.shape, jnp.float32)
    for at, (step, hop) in enumerate(((1, 1), (1, 2), (-1, 1), (-1, 2))):
        other = frame - step * hop
        inside = (other >= 0) & (other <= last)
        same = inside & (clip_ref[jnp.clip(other, 0, last)] == here)
        masks = jnp.where(line == at, jnp.where(same, 1.0, 0.0), masks)
    out_ref[...] = masks


def heads_kernel(query_hbm, cotangent_hbm, clip_hbm, mine_ref, other_ref, mask_ref, groups, query_ref, cotangent_ref, sems, clip_ref, clip_sem):
    clip_copy = pltpu.make_async_copy(clip_hbm, clip_ref, clip_sem)
    clip_copy.start()
    stage((query_hbm, cotangent_hbm), (query_ref, cotangent_ref), sems)
    clip_copy.wait()
    write_masks(clip_ref, mask_ref)
    none = tail_block(query_ref.shape[0], 0.0)
    per_group = HEADS // 2
    row = lax.axis_index("height")
    for head in range(HEADS):
        group, place = divmod(head, per_group)
        feature = jnp.maximum(head_slice(query_ref, head), 0)
        groups[group, 0, place] = jnp.concatenate([feature, none], axis=1)
        groups[group, 1, place] = jnp.concatenate([head_slice(cotangent_ref, head), none], axis=1)
    mine_ref[...] = groups[row]
    other_ref[...] = groups[1 - row]


def query_kernel(state_ref, came_ref, mine_ref, other_ref, keep_ref, send_ref, own_out, other_out, state, halves):
    column = lax.axis_index("width")
    half = state_ref.shape[0]
    per_group = HEADS // 2
    tokens = mine_ref.shape[2]
    state[column] = state_ref[...]
    state[1 - column] = came_ref[...]
    lane = lax.broadcasted_iota(jnp.int32, (2 * tokens, LANES), 1)
    for place in range(per_group):
        feature = jnp.concatenate([mine_ref[0, place], other_ref[0, place]], axis=0)
        cotangent = jnp.concatenate([mine_ref[1, place], other_ref[1, place]], axis=0).astype(jnp.float32)
        high, low = split_terms(load_rows(state, place * HEAD_DIM, half))
        narrow = feature[:, :HEAD_DIM]
        product = dot_rows(narrow, high) + dot_rows(narrow, low)
        inverse = 1.0 / (product[:, HEAD_DIM : HEAD_DIM + 1] + EPSILON)
        against = jnp.sum(cotangent * product, axis=1, keepdims=True)
        norm_grad = -(against * inverse) * inverse
        scaled = jnp.where(lane == HEAD_DIM, norm_grad, cotangent * inverse)
        scaled_high, scaled_low = split_terms(scaled)
        grad = dot_tokens(narrow, scaled_high) + dot_tokens(narrow, scaled_low)
        store_rows(halves, None, place * HEAD_DIM, grad, half)
        back = dot_columns(scaled_high, high) + dot_columns(scaled_high, low) + dot_columns(scaled_low, high)
        back = jnp.where(narrow > 0, back, 0.0).astype(jnp.bfloat16)
        own_out[place, :, :HEAD_DIM] = back[:tokens]
        other_out[place, :, :HEAD_DIM] = back[tokens:]
    keep_ref[...] = halves[column]
    send_ref[...] = halves[1 - column]


def load_rows(state, first, half):
    cut = min(max(half - first, 0), HEAD_DIM)
    parts = []
    if cut:
        parts.append(state[0, first : first + cut])
    if cut < HEAD_DIM:
        start = first + cut - half
        parts.append(state[1, start : start + HEAD_DIM - cut])
    return parts[0] if len(parts) == 1 else jnp.concatenate(parts, axis=0)


def key_heads(key_ref, value_ref, total, half, group, place, one):
    head = group * (HEADS // 2) + place
    feature = jnp.maximum(head_slice(key_ref, head), 0)
    wide = jnp.concatenate([head_slice(value_ref, head), one], axis=1)
    high, low = split_terms(load_rows(total, place * HEAD_DIM, half))
    grad = dot_columns(wide, high) + dot_columns(wide, low)
    product = dot_rows(feature, high) + dot_rows(feature, low)
    return jnp.where(feature > 0, grad, 0.0).astype(jnp.bfloat16), product[:, :HEAD_DIM].astype(jnp.bfloat16)


def key_kernel(mine, key_ref, value_ref, here_ref, came_ref, *refs):
    column, row = lax.axis_index("width"), lax.axis_index("height")
    half = here_ref.shape[0]
    given, (key_out, value_out, total) = refs[:-3], refs[-3:]
    total[column] = here_ref[...]
    total[1 - column] = came_ref[...]
    one = tail_block(key_ref.shape[0], 1.0)
    for group in range(2):
        @pl.when(row == (group if mine else 1 - group))
        def _():
            for place in range(HEADS // 2):
                grads = key_heads(key_ref, value_ref, total, half, group, place, one)
                for at, out in enumerate((key_out, value_out)):
                    if mine:
                        out[place, :, :HEAD_DIM] = grads[at]
                        continue
                    for which, part in ((group, grads[at]), (1 - group, given[at][place, :, :HEAD_DIM])):
                        first = (which * (HEADS // 2) + place) * HEAD_DIM
                        out[:, first : first + HEAD_DIM] = part


def join_kernel(mine_ref, came_ref, out_ref):
    row = lax.axis_index("height")
    per_group = HEADS // 2
    for place in range(per_group):
        mine, came = mine_ref[place, :, :HEAD_DIM], came_ref[place, :, :HEAD_DIM]
        first = jnp.where(row == 0, mine, came)
        second = jnp.where(row == 0, came, mine)
        out_ref[:, place * HEAD_DIM : (place + 1) * HEAD_DIM] = first
        at = (per_group + place) * HEAD_DIM
        out_ref[:, at : at + HEAD_DIM] = second


def struct(shape, dtype=jnp.float32):
    return jax.ShapeDtypeStruct(shape, dtype)


SWAP = [(0, 1), (1, 0)]


def paired(queries, attn_keys, attn_values, attn_cotangent, clip_ids, hidden_pre, conv_weight):
    tokens = queries.shape[1] * queries.shape[2]
    flat = HEADS * HEAD_DIM
    per_group = HEADS // 2
    half = per_group * HEAD_DIM // 2
    frames = lax.axis_size("tm")
    query, key, value, cotangent = (
        part.reshape(tokens, flat) for part in (queries, attn_keys, attn_values, attn_cotangent)
    )
    share = struct((half, LANES))
    pair = struct((2, half, LANES))

    key_hbm, value_hbm = (
        pltpu.with_memory_space_constraint(part, pltpu.HBM) for part in (key, value)
    )
    staged = [pltpu.VMEM((tokens, flat), jnp.bfloat16)] * 2 + [pltpu.SemaphoreType.DMA((2, PARTS))]
    keep, send = vmem_call(
        state_kernel, (pair, pair), [pltpu.VMEM((2, 2, half, LANES), jnp.float32), *staged], n_in=2, in_hbm=True,
        flops=2 * tokens * flat * LANES, bytes_accessed=4 * tokens * flat + 8 * half * LANES * 2,
    )(key_hbm, value_hbm)
    hidden, send = lax.optimization_barrier((hidden_pre, send))
    edges = row_edges(hidden)
    came = lax.ppermute(send, "width", SWAP)
    came, edges = lax.optimization_barrier((came, edges))
    mine, other = vmem_call(pick_kernel, (share, share), n_in=2, bytes_accessed=24 * half * LANES)(keep, came)
    came = lax.ppermute(other, "height", SWAP)

    packed = struct((2, per_group, tokens, LANES), jnp.bfloat16)
    query, cotangent, hidden, _ = lax.optimization_barrier((query, cotangent, hidden, mine))
    heads_mine, heads_other, masks = vmem_call(
        heads_kernel,
        (packed, packed, struct((8, LANES))),
        [pltpu.VMEM((2, 2, per_group, tokens, LANES), jnp.bfloat16), *staged,
         pltpu.SMEM(clip_ids.shape, jnp.int32), pltpu.SemaphoreType.DMA],
        n_in=3, in_hbm=True, bytes_accessed=12 * tokens * flat,
    )(*(pltpu.with_memory_space_constraint(part, pltpu.HBM) for part in (query, cotangent, clip_ids)))
    side = side_edge(hidden[0])
    edges, _ = lax.optimization_barrier((edges, heads_other))
    halo = halo_arrays(edges, side)
    _, own = lax.optimization_barrier(((heads_other, side), mine + came))
    heads_sent = lax.ppermute(heads_other, "height", SWAP)

    def along_frames(own, step, beside):
        moves = [[(at, at + step * hop) for at in range(frames) if 0 <= at + step * hop < frames] for hop in (1, 2)]
        near = lax.ppermute(own, "tm", moves[0])
        far = lax.ppermute(own, "tm", moves[1])
        near, far, beside = beside(own, near, far)
        at = 0 if step > 0 else 2
        return own + masks[at : at + 1] * near + masks[at + 1 : at + 2] * far, beside

    def fetch(own, near, far):
        return lax.optimization_barrier((near, far, heads_sent))

    state, heads_came = along_frames(own, 1, fetch)
    came = lax.ppermute(state, "width", SWAP)
    back = struct((per_group, tokens, LANES), jnp.bfloat16)
    keep, send, back_mine, back_other = vmem_call(
        query_kernel, (share, share, back, back),
        [pltpu.VMEM((2, half, LANES), jnp.float32), pltpu.VMEM((2, half, LANES), jnp.float32)], n_in=4,
        flops=14 * tokens * flat * LANES, bytes_accessed=8 * tokens * flat,
    )(state, came, heads_mine, heads_came)
    came = lax.ppermute(send, "width", SWAP)
    own, halo = lax.optimization_barrier((keep + came, halo))

    def convolve(own, near, far):
        other, _ = lax.optimization_barrier((back_other, own))
        back_came = lax.ppermute(other, "height", SWAP)
        hidden_grad = ffn(hidden_pre, conv_weight, halo)
        query_grad = vmem_call(
            join_kernel, struct((tokens, flat), jnp.bfloat16), n_in=2, bytes_accessed=4 * tokens * flat
        )(back_mine, back_came)
        near, far, hidden_grad = lax.optimization_barrier((near, far, hidden_grad))
        return near, far, (query_grad, hidden_grad)

    total, (query_grad, hidden_grad) = along_frames(own, -1, convolve)
    far = lax.ppermute(total, "height", SWAP)
    near_came = lax.ppermute(total, "width", SWAP)
    state = [pltpu.VMEM((2, half, LANES), jnp.float32)]
    cost = {"flops": 4 * tokens * flat * LANES, "bytes_accessed": 4 * tokens * flat}
    near_grads = vmem_call(functools.partial(key_kernel, True), (back, back), state, n_in=4, **cost)(
        key, value, total, near_came
    )
    far, query_grad = lax.optimization_barrier((far, query_grad))
    far_came = lax.ppermute(far, "width", SWAP)
    out = struct((tokens, flat), jnp.bfloat16)
    key_grad, value_gradient = vmem_call(functools.partial(key_kernel, False), (out, out), state, n_in=6, **cost)(
        key, value, far, far_came, *near_grads
    )
    grads = tuple(part.reshape(queries.shape) for part in (query_grad, key_grad, value_gradient))
    return (*grads, hidden_grad)


def mixed_ffn(hidden_pre, conv_weight):
    row_count = hidden_pre.shape[1]
    col_count = hidden_pre.shape[2]
    split_at = hidden_pre.shape[3] // 2
    widened = padded(hidden_pre, (("height", 1), ("width", 2)), 2)[0]
    conv_out = depthwise(widened, conv_weight, 1, 1, row_count + 2, col_count + 2)
    row_global = lax.axis_index("height") * row_count + jnp.arange(row_count + 2) - 1
    col_global = lax.axis_index("width") * col_count + jnp.arange(col_count + 2) - 1
    row_inside = (row_global >= 0) & (row_global < row_count * lax.axis_size("height"))
    col_inside = (col_global >= 0) & (col_global < col_count * lax.axis_size("width"))
    inside = (row_inside[:, None] & col_inside[None, :]).astype(jnp.float32)
    conv_grad = glu_grad(conv_out, split_at) * inside[:, :, None]
    hidden_grad = depthwise(conv_grad, conv_weight, 1, -1, row_count, col_count)
    hidden_grad = hidden_grad[None].astype(jnp.bfloat16)
    return hidden_grad


TILES = 8
REACH = 2
UNROLL = 2


def conv_kernel(bases, row_refs, *refs):
    halo_rows, refs = refs[:row_refs], refs[row_refs:]
    side_ref, refs = refs[0], refs[1:]
    corners, refs = refs[:row_refs], refs[row_refs:]
    block_ref, weight_ref = refs[:2]
    out_hbm, taps, value_in, gate_in, value_grad, gate_grad, *results, out_ref, sems = refs[-8 - 2 * UNROLL :]
    rows, cols, channels = block_ref.shape
    lane_tiles = channels // LANES // 2
    pitch = -(-lane_tiles // TILES) * TILES
    row, column = lax.axis_index("height"), lax.axis_index("width")
    first_row, last_row = row == 0, row == lax.axis_size("height") - 1
    wide, tall = cols + 2 * REACH, rows + 2 * REACH
    grad_wide = wide - 2

    for base in bases:
        for tile in range(base, min(base + TILES, lane_tiles)):
            for place, source in ((tile, tile), (pitch + tile, lane_tiles + tile)):
                lanes = slice(source * LANES, (source + 1) * LANES)
                taps[pl.ds(place, 9, stride=2 * pitch), :] = weight_ref[:, lanes]

    def source_at(at_row, at_col):
        return pl.multiple_of((at_row * wide + at_col) * TILES, TILES)

    def grad_at(at_row, at_col):
        return pl.multiple_of((at_row * grad_wide + at_col) * TILES, TILES)

    zero = jnp.zeros((TILES, LANES), jnp.float32)
    low_border = jnp.where(first_row, 0, rows + REACH)
    outer_col = jnp.where(column == 0, 0, cols + REACH)
    side_col = jnp.where(column == 0, cols + REACH, 0)
    grad_outer_col = jnp.where(column == 0, 0, grad_wide - 1)
    start_col = jnp.where(column == 0, REACH, REACH - 1)
    low, high = jnp.where(first_row, REACH, REACH - 1), jnp.where(last_row, rows + REACH, rows + REACH + 1)

    for ref in (value_in, gate_in):
        @pl.loop(0, tall)
        def _(at):
            for extra in range(REACH):
                ref[pl.ds(source_at(at, outer_col + extra), TILES), :] = zero

    for ref in (value_grad, gate_grad):
        @pl.loop(0, rows + 2)
        def _(at):
            ref[pl.ds(grad_at(at, grad_outer_col), TILES), :] = zero

        for edge, at in ((first_row, 0), (last_row, rows + 1)):
            @pl.when(edge)
            def _():
                for col in range(grad_wide):
                    ref[pl.ds(grad_at(at, col), TILES), :] = zero

    copies = []
    for base in bases:
        count = min(TILES, lane_tiles - base)

        def spread(load, at_row, at_col, length):
            for ref, offset in ((value_in, base), (gate_in, lane_tiles + base)):
                for tile in range(count):
                    part = load(slice((offset + tile) * LANES, (offset + tile + 1) * LANES)).astype(jnp.float32)
                    ref[pl.ds(source_at(at_row, at_col) + tile, length, stride=TILES), :] = part

        @pl.loop(0, rows)
        def _(at):
            spread(lambda lanes: block_ref[at, :, lanes], at + REACH, REACH, cols)
            spread(lambda lanes: side_ref[at, :, lanes], at + REACH, side_col, REACH)

        for edge, at, which in ((first_row, 0, 0), (last_row, rows + REACH, row_refs - 1)):
            rows_ref, corner_ref = halo_rows[which], corners[which]
            for extra in range(REACH):
                @pl.when(jnp.logical_not(edge))
                def _():
                    spread(lambda lanes: rows_ref[extra, :, lanes], at + extra, REACH, cols)
                    spread(lambda lanes: corner_ref[extra, :, lanes], at + extra, side_col, REACH)

                @pl.when(edge)
                def _():
                    for ref in (value_in, gate_in):
                        for col in range(wide):
                            ref[pl.ds(source_at(at + extra, col), TILES), :] = zero

        def weights(offset):
            return [taps[2 * pitch * tap + offset + base : 2 * pitch * tap + offset + base + TILES, :] for tap in range(9)]

        value_taps, gate_taps = weights(0), weights(pitch)

        @pl.loop(low, high)
        def _(at):
            cache = {}

            def read(ref, a, col):
                if (id(ref), a, col) not in cache:
                    cache[id(ref), a, col] = ref[pl.ds(source_at(at + a, start_col + col), TILES), :]
                return cache[id(ref), a, col]

            for col in range(cols + 1):
                def conv(ref, kernel):
                    total = None
                    for a in (-1, 0, 1):
                        for b in (-1, 0, 1):
                            term = kernel[3 * (a + 1) + b + 1] * read(ref, a, col + b)
                            total = term if total is None else total + term
                    return total

                value, gate = conv(value_in, value_taps), conv(gate_in, gate_taps)
                squash = jax.nn.sigmoid(gate)
                gated = gate * squash
                glu = value * gated
                place = pl.ds(grad_at(at - 1, start_col + col - 1), TILES)
                value_grad[place, :] = glu * gated
                gate_grad[place, :] = glu * value * (squash + gated * (1.0 - squash))

        def gather(at, results):
            cache = {}

            def read(ref, a, col):
                if (id(ref), a, col) not in cache:
                    cache[id(ref), a, col] = ref[pl.ds(grad_at(at + a, col), TILES), :]
                return cache[id(ref), a, col]

            for col in range(cols):
                for ref, kernel, result in zip((value_grad, gate_grad), (value_taps, gate_taps), results):
                    total = None
                    for a in (-1, 0, 1):
                        for b in (-1, 0, 1):
                            term = kernel[3 * (a + 1) + b + 1] * read(ref, 1 - a, col + 1 - b)
                            total = term if total is None else total + term
                    result[pl.ds(col, TILES, stride=cols), :] = total

        def settle(at, results):
            for result, offset in zip(results, (base, lane_tiles + base)):
                for tile in range(count):
                    lanes = slice((offset + tile) * LANES, (offset + tile + 1) * LANES)
                    out_ref[at, :, lanes] = result[tile * cols : (tile + 1) * cols, :].astype(jnp.bfloat16)

        @pl.loop(0, rows // UNROLL)
        def _(at):
            for step in range(UNROLL):
                gather(at * UNROLL + step, results[2 * step : 2 * step + 2])
                if step:
                    settle(at * UNROLL + step - 1, results[2 * step - 2 : 2 * step])
            settle(at * UNROLL + UNROLL - 1, results[2 * UNROLL - 2 :])

        for at, offset in enumerate((base, lane_tiles + base)):
            lanes = pl.ds(offset * LANES, count * LANES)
            copy = pltpu.make_async_copy(out_ref.at[:, :, lanes], out_hbm.at[:, :, lanes], sems.at[at, base // TILES])
            copy.start()
            copies.append(copy)
    for copy in copies:
        copy.wait()


def edge_slice(block, dim, low_side):
    start = jnp.where(low_side, 0, block.shape[dim] - REACH)
    return lax.dynamic_slice_in_dim(block, start, REACH, axis=dim)


def row_edges(hidden_pre):
    block = hidden_pre[0]
    if lax.axis_size("height") == 2:
        return [edge_slice(block, 0, lax.axis_index("height") == 1)]
    return [block[block.shape[0] - REACH :], block[:REACH]]


def side_edge(block):
    return edge_slice(block, 1, lax.axis_index("width") == 1)


def halo_arrays(edges, side):
    height = lax.axis_size("height")
    if height == 2:
        moves = [SWAP]
    else:
        moves = [[(at, at + 1) for at in range(height - 1)], [(at + 1, at) for at in range(height - 1)]]
    halo_rows = [lax.ppermute(edge, "height", move) for edge, move in zip(edges, moves)]
    side = lax.ppermute(side, "width", SWAP)
    corners = [lax.ppermute(side_edge(part), "width", SWAP) for part in halo_rows]
    return halo_rows, side, corners


def conv_part(bases, halo, block, conv_weight, given=()):
    halo_rows, side, corners = halo
    rows, cols, channels = block.shape
    lane_tiles = channels // LANES // 2
    pitch = -(-lane_tiles // TILES) * TILES
    source = pltpu.VMEM(((rows + 2 * REACH) * (cols + 2 * REACH) * TILES, LANES), jnp.float32)
    grad = pltpu.VMEM(((rows + 2) * (cols + 2) * TILES, LANES), jnp.float32)
    result = pltpu.VMEM((cols * TILES, LANES), jnp.float32)
    size = rows * cols * channels
    return vmem_call(
        functools.partial(conv_kernel, bases, len(halo_rows)),
        struct((rows, cols, channels), jnp.bfloat16),
        [pltpu.VMEM((9 * 2 * pitch, LANES), jnp.float32), source, source, grad, grad, *[result] * (2 * UNROLL),
         pltpu.VMEM((rows, cols, channels), jnp.bfloat16), pltpu.SemaphoreType.DMA((2, pitch // TILES))],
        n_in=2 * len(halo_rows) + 3, n_given=len(given), flops=size * len(bases), bytes_accessed=size, vmem_mib=12,
        out_hbm=True,
    )(*halo_rows, side, *corners, block, conv_weight, *given)


def conv_bases(hidden_pre):
    lane_tiles = hidden_pre.shape[3] // LANES // 2
    return list(range(0, lane_tiles, TILES))


def ffn(hidden_pre, conv_weight, halo):
    return conv_part(conv_bases(hidden_pre), halo, hidden_pre[0], conv_weight)[None]


def per_device(queries, attn_keys, attn_values, attn_cotangent, clip_ids, hidden_pre, conv_weight):
    blocked = lax.axis_size("width") == 2 and hidden_pre.shape[0] == 1 and hidden_pre.shape[3] % (2 * LANES) == 0
    pairs = lax.axis_size("height") == 2 and 3 <= lax.axis_size("tm") <= 4 and HEADS % 2 == 0
    if blocked and pairs:
        return paired(queries, attn_keys, attn_values, attn_cotangent, clip_ids, hidden_pre, conv_weight)
    grads = general_attention(queries, attn_keys, attn_values, attn_cotangent, clip_ids)
    if blocked:
        return (*grads, ffn(hidden_pre, conv_weight, halo_arrays(row_edges(hidden_pre), side_edge(hidden_pre[0]))))
    return (*grads, mixed_ffn(hidden_pre, conv_weight))


def solution(mesh):
    return jax.shard_map(
        per_device,
        mesh=mesh,
        in_specs=(
            P(("group", "tm"), "height", "width", None),
            P(("group", "tm"), "height", "width", None),
            P(("group", "tm"), "height", "width", None),
            P(("group", "tm"), "height", "width", None),
            P("group"),
            P(("group", "tm"), "height", "width", None),
            P(),
        ),
        out_specs=(
            P(("group", "tm"), "height", "width", None),
            P(("group", "tm"), "height", "width", None),
            P(("group", "tm"), "height", "width", None),
            P(("group", "tm"), "height", "width", None),
        ),
        check_vma=False,
    )
```

```python
import functools
from functools import reduce

import jax
import jax.numpy as jnp
from jax import lax
from jax.experimental import pallas as pl
from jax.experimental.pallas import tpu as pltpu
from jax.sharding import PartitionSpec as P

HEAD_DIM = 112
HEADS = 10


EPSILON = 1e-06
TOP_PRECISION = lax.Precision.HIGHEST


def entering(value, axis, join, neutral, backward):
    count, mine = (lax.axis_size(axis), lax.axis_index(axis))
    pieces = jax.tree.map(lambda part: lax.all_gather(part, axis), value)
    if backward:
        pieces = jax.tree.map(lambda part: part[::-1], pieces)
        mine = count - 1 - mine
    so_far = jax.tree.map(
        lambda part, zero: jnp.full_like(part, 0) + jnp.asarray(zero, part.dtype), value, neutral
    )

    def turn(position, so_far):
        longer = join(so_far, jax.tree.map(lambda part: part[position], pieces))
        return jax.tree.map(lambda new, old: jnp.where(position < mine, new, old), longer, so_far)

    return lax.fori_loop(0, count - 1, turn, so_far)


def padded(block, sides, width):
    for axis, dim in sides:
        count = lax.axis_size(axis)
        forward = [(i, i + 1) for i in range(count - 1)]
        backward = [(target, source) for source, target in forward]
        low = lax.ppermute(
            lax.slice_in_dim(block, block.shape[dim] - width, None, axis=dim), axis, forward
        )
        high = lax.ppermute(lax.slice_in_dim(block, 0, width, axis=dim), axis, backward)
        block = jnp.concatenate([low, block, high], axis=dim)
    return block


def carry_on(earlier, later):
    keeping = 1.0 - later[0]
    return (
        jnp.maximum(earlier[0], later[0]),
        later[1] + keeping * earlier[1],
        later[2] + keeping * earlier[2],
    )


def clip_flags(clip_ids):
    frame = lax.axis_index("tm")
    frame_count = lax.axis_size("tm")
    current = lax.dynamic_index_in_dim(clip_ids, frame, 0, keepdims=False)
    before = lax.dynamic_index_in_dim(clip_ids, jnp.maximum(frame - 1, 0), 0, keepdims=False)
    after = lax.dynamic_index_in_dim(
        clip_ids, jnp.minimum(frame + 1, frame_count - 1), 0, keepdims=False
    )
    starts = jnp.where((frame == 0) | (current != before), 1.0, 0.0).astype(jnp.float32)
    ends = jnp.where((frame == frame_count - 1) | (current != after), 1.0, 0.0).astype(jnp.float32)
    return (starts, ends)


def glu_grad(conv_out, split_at):
    value_part = conv_out[..., :split_at]
    gate_part = conv_out[..., split_at:]
    squash = jax.nn.sigmoid(gate_part)
    glu = value_part * gate_part * squash
    value_gradient = glu * gate_part * squash
    gate_grad = glu * value_part * squash * (1.0 + gate_part * (1.0 - squash))
    return jnp.concatenate([value_gradient, gate_grad], axis=-1)


def depthwise(source, weights, start, sign, height_out, width_out):
    terms = []
    for offset_row in (-1, 0, 1):
        for offset_col in (-1, 0, 1):
            tap_index = (offset_row + 1) * 3 + offset_col + 1
            row_start = start + sign * offset_row
            col_start = start + sign * offset_col
            window = source[
                row_start : row_start + height_out, col_start : col_start + width_out
            ].astype(jnp.float32)
            terms.append(weights[tap_index] * window)
    return reduce(lambda first, second: first + second, terms)


def general_attention(queries, attn_keys, attn_values, attn_cotangent, clip_ids):
    token_count = queries.shape[1] * queries.shape[2]
    flat_width = HEADS * HEAD_DIM
    starts, ends = clip_flags(clip_ids)
    zero_flag = jnp.zeros((), jnp.float32)
    feature_keys = jnp.maximum(attn_keys, 0).reshape(token_count, HEADS, HEAD_DIM)
    value_row_block = attn_values.reshape(token_count, HEADS, HEAD_DIM)
    local_kv = jnp.einsum(
        "jrf,jrx->rfx", feature_keys, value_row_block, preferred_element_type=jnp.float32
    ).reshape(flat_width, HEAD_DIM)
    local_norm = jnp.sum(feature_keys.astype(jnp.float32), axis=0).reshape(flat_width)
    share_kv, share_norm = (
        lax.psum_scatter(local_kv, ("height", "width"), scatter_dimension=0, tiled=True),
        lax.psum_scatter(local_norm, ("height", "width"), scatter_dimension=0, tiled=True),
    )
    earlier = entering(
        (starts, share_kv, share_norm),
        "tm",
        carry_on,
        (zero_flag, jnp.zeros_like(share_kv), jnp.zeros_like(share_norm)),
        False,
    )
    part_kv = share_kv + (1.0 - starts) * earlier[1]
    part_norm = share_norm + (1.0 - starts) * earlier[2]
    state_key_value, state_norm = (
        lax.all_gather(part_kv, ("height", "width"), axis=0, tiled=True),
        lax.all_gather(part_norm, ("height", "width"), axis=0, tiled=True),
    )
    state_key_value = state_key_value.reshape(HEADS, HEAD_DIM, HEAD_DIM)
    state_norm = state_norm.reshape(HEADS, HEAD_DIM)
    feature_query = (
        jnp.maximum(queries, 0).reshape(token_count, HEADS, HEAD_DIM).astype(jnp.float32)
    )
    cotangent = attn_cotangent.reshape(token_count, HEADS, HEAD_DIM).astype(jnp.float32)
    ratio_numerator = jnp.einsum(
        "cob,obq->coq", feature_query, state_key_value, precision=TOP_PRECISION
    )
    denominator = (
        jnp.einsum("thk,hk->th", feature_query, state_norm, precision=TOP_PRECISION) + EPSILON
    )
    attended = ratio_numerator / denominator[..., None]
    scaled_gradient = cotangent / denominator[..., None]
    denominator_grad = -jnp.sum(cotangent * attended, axis=-1) / denominator
    query_feature_gradient = jnp.einsum(
        "dla,lja->dlj", scaled_gradient, state_key_value, precision=TOP_PRECISION
    )
    query_feature_gradient = query_feature_gradient + state_norm[None] * denominator_grad[..., None]
    query_grad = (
        jnp.where(feature_query > 0.0, query_feature_gradient, 0.0)
        .reshape(queries.shape)
        .astype(jnp.bfloat16)
    )
    gradient_key_value = jnp.einsum(
        "jrf,jrx->rfx", feature_query, scaled_gradient, precision=TOP_PRECISION
    ).reshape(flat_width, HEAD_DIM)
    grad_norm = jnp.einsum(
        "thk,th->hk", feature_query, denominator_grad, precision=TOP_PRECISION
    ).reshape(flat_width)
    share_grad_kv, share_grad_norm = (
        lax.psum_scatter(gradient_key_value, ("height", "width"), scatter_dimension=0, tiled=True),
        lax.psum_scatter(grad_norm, ("height", "width"), scatter_dimension=0, tiled=True),
    )
    later = entering(
        (ends, share_grad_kv, share_grad_norm),
        "tm",
        carry_on,
        (zero_flag, jnp.zeros_like(share_grad_kv), jnp.zeros_like(share_grad_norm)),
        True,
    )
    part_grad_kv = share_grad_kv + (1.0 - ends) * later[1]
    part_grad_norm = share_grad_norm + (1.0 - ends) * later[2]
    total_key_value, norm_total = (
        lax.all_gather(part_grad_kv, ("height", "width"), axis=0, tiled=True),
        lax.all_gather(part_grad_norm, ("height", "width"), axis=0, tiled=True),
    )
    total_key_value = total_key_value.reshape(HEADS, HEAD_DIM, HEAD_DIM)
    norm_total = norm_total.reshape(HEADS, HEAD_DIM)
    key_feat_grad = (
        jnp.einsum(
            "dla,lja->dlj",
            value_row_block.astype(jnp.float32),
            total_key_value,
            precision=TOP_PRECISION,
        )
        + norm_total[None]
    )
    key_grad = (
        jnp.where(feature_keys > 0, key_feat_grad, 0.0)
        .reshape(attn_keys.shape)
        .astype(jnp.bfloat16)
    )
    value_gradient = jnp.einsum(
        "cob,obq->coq", feature_keys.astype(jnp.float32), total_key_value, precision=TOP_PRECISION
    )
    value_gradient = value_gradient.reshape(attn_values.shape).astype(jnp.bfloat16)
    return (query_grad, key_grad, value_gradient)


LANES = 128


def split_terms(value):
    high = value.astype(jnp.bfloat16)
    low = (value - high.astype(jnp.float32)).astype(jnp.bfloat16)
    return high, low


def dot_tokens(left, right):
    return lax.dot_general(left, right, (((0,), (0,)), ((), ())), preferred_element_type=jnp.float32)


def dot_rows(left, right):
    return lax.dot_general(left, right, (((1,), (0,)), ((), ())), preferred_element_type=jnp.float32)


def dot_columns(left, right):
    return lax.dot_general(left, right, (((1,), (1,)), ((), ())), preferred_element_type=jnp.float32)


def head_slice(ref, head):
    return ref[:, head * HEAD_DIM : (head + 1) * HEAD_DIM]


def tail_block(rows, first):
    column = lax.broadcasted_iota(jnp.int32, (rows, LANES - HEAD_DIM), 1)
    return jnp.where(column == 0, first, 0.0).astype(jnp.bfloat16)


def vmem_call(kernel, out_shape, scratch=(), smem_first=False, n_in=0, flops=0, bytes_accessed=0, vmem_mib=8, in_hbm=False, out_hbm=False, n_given=0):
    vmem = pl.BlockSpec(memory_space=pltpu.VMEM)
    in_specs = [pl.BlockSpec(memory_space=pltpu.HBM) if in_hbm else vmem] * n_in
    in_specs += [pl.BlockSpec(memory_space=pltpu.HBM)] * n_given
    if smem_first:
        in_specs[0] = pl.BlockSpec(memory_space=pltpu.SMEM)
    return pl.pallas_call(
        kernel,
        out_shape=out_shape,
        in_specs=in_specs,
        out_specs=jax.tree.map(lambda _: pl.BlockSpec(memory_space=pltpu.HBM) if out_hbm else vmem, out_shape),
        scratch_shapes=list(scratch),
        input_output_aliases={n_in: 0} if n_given else {},
        cost_estimate=pl.CostEstimate(flops=flops, bytes_accessed=bytes_accessed, transcendentals=0),
        compiler_params=pltpu.CompilerParams(vmem_limit_bytes=vmem_mib << 20),
    )


ROWS = 8
SPARE = LANES - HEAD_DIM
PIECES = HEAD_DIM // SPARE


def packed_tiles(tiles):
    return next(kept for kept in range(tiles + 1) if (tiles - kept) * PIECES - (-tiles // SPARE) <= kept)


def tile_of(at):
    return slice(at * ROWS, (at + 1) * ROWS)


def pack_rows(read, write, tiles):
    kept = packed_tiles(tiles)
    moved = (tiles - kept) * PIECES
    lane = lax.broadcasted_iota(jnp.int32, (ROWS, LANES), 1)
    rows = [read(at) for at in range(tiles)]
    for at in range(kept):
        block = rows[at]
        if at < moved:
            extra, piece = divmod(at, PIECES)
            shifted = pltpu.roll(rows[kept + extra], HEAD_DIM - SPARE * piece, 1)
            block = jnp.where(lane < HEAD_DIM, block, shifted)
        else:
            first = (at - moved) * SPARE
            for step in range(min(SPARE, tiles - first)):
                norm = rows[first + step]
                norm = pltpu.roll(norm, step, 1) if step else norm
                block = jnp.where(lane == HEAD_DIM + step, norm, block)
        write(at, block)


def unpack_rows(read, write, tiles):
    kept = packed_tiles(tiles)
    moved = (tiles - kept) * PIECES
    lane = lax.broadcasted_iota(jnp.int32, (ROWS, LANES), 1)
    rows = [read(at) for at in range(kept)]
    for at in range(tiles):
        if at < kept:
            block = rows[at]
        else:
            for piece in range(PIECES):
                shifted = pltpu.roll(rows[(at - kept) * PIECES + piece], SPARE * (piece + 1), 1)
                block = shifted if piece == 0 else jnp.where(lane < SPARE * piece, block, shifted)
        group, step = divmod(at, SPARE)
        norm = rows[moved + group]
        norm = pltpu.roll(norm, LANES - step, 1) if step else norm
        write(at, jnp.where(lane == HEAD_DIM, norm, block))


def store_into(ref, *index):
    def write(at, block):
        ref[(*index, tile_of(at))] = block

    return write


def unpack_into(state, index, packed):
    unpack_rows(lambda at: packed[tile_of(at)], store_into(state, index), state.shape[1] // ROWS)


PARTS = 4


def stage(sources, targets, sems):
    copies = []
    for at, (source, target) in enumerate(zip(sources, targets)):
        rows = source.shape[0] // PARTS
        for part in range(PARTS):
            span = pl.ds(part * rows, rows)
            copies.append(pltpu.make_async_copy(source.at[span], target.at[span], sems.at[at, part]))
    for copy in copies:
        copy.start()
    for copy in copies:
        copy.wait()


def state_kernel(key_hbm, value_hbm, keep_ref, send_ref, halves, key_ref, value_ref, sems):
    stage((key_hbm, value_hbm), (key_ref, value_ref), sems)
    tokens = key_ref.shape[0]
    one = tail_block(tokens, 1.0)
    half = halves.shape[2]
    per_group = HEADS // 2
    column = lax.axis_index("width")
    blocks = []
    for head in range(HEADS):
        feature = jnp.maximum(head_slice(key_ref, head), 0)
        wide = jnp.concatenate([head_slice(value_ref, head), one], axis=1)
        blocks.append(dot_tokens(feature, wide))
    for head in range(HEADS):
        group, place = divmod(head, per_group)
        store_rows(halves, group, place * HEAD_DIM, blocks[head], half)
    keep_ref[...] = halves[column]
    send_ref[...] = halves[1 - column]


def store_rows(halves, group, first, block, half):
    cut = min(max(half - first, 0), HEAD_DIM)
    if cut:
        index = (0, group) if group is not None else (0,)
        halves[(*index, slice(first, first + cut))] = block[:cut]
    if cut < HEAD_DIM:
        index = (1, group) if group is not None else (1,)
        start = first + cut - half
        halves[(*index, slice(start, start + HEAD_DIM - cut))] = block[cut:]


def pick_kernel(keep_ref, came_ref, mine_ref, other_ref):
    row = lax.axis_index("height")
    tiles = keep_ref.shape[1] // ROWS
    for out, at_row in ((mine_ref, row), (other_ref, 1 - row)):
        pack_rows(lambda at: keep_ref[at_row, tile_of(at)] + came_ref[at_row, tile_of(at)], store_into(out), tiles)


def write_masks(clip_ref, out_ref):
    frame = lax.axis_index("tm")
    last = lax.axis_size("tm") - 1
    here = clip_ref[frame]
    line = lax.broadcasted_iota(jnp.int32, out_ref.shape, 0)
    masks = jnp.zeros(out_ref.shape, jnp.float32)
    for at, (step, hop) in enumerate(((1, 1), (1, 2), (-1, 1), (-1, 2))):
        other = frame - step * hop
        inside = (other >= 0) & (other <= last)
        same = inside & (clip_ref[jnp.clip(other, 0, last)] == here)
        masks = jnp.where(line == at, jnp.where(same, 1.0, 0.0), masks)
    out_ref[...] = masks


def heads_kernel(query_hbm, cotangent_hbm, clip_hbm, mine_ref, other_ref, mask_ref, groups, query_ref, cotangent_ref, sems, clip_ref, clip_sem):
    clip_copy = pltpu.make_async_copy(clip_hbm, clip_ref, clip_sem)
    clip_copy.start()
    stage((query_hbm, cotangent_hbm), (query_ref, cotangent_ref), sems)
    clip_copy.wait()
    write_masks(clip_ref, mask_ref)
    none = tail_block(query_ref.shape[0], 0.0)
    per_group = HEADS // 2
    row = lax.axis_index("height")
    for head in range(HEADS):
        group, place = divmod(head, per_group)
        feature = jnp.maximum(head_slice(query_ref, head), 0)
        groups[group, 0, place] = jnp.concatenate([feature, none], axis=1)
        groups[group, 1, place] = jnp.concatenate([head_slice(cotangent_ref, head), none], axis=1)
    mine_ref[...] = groups[row]
    other_ref[...] = groups[1 - row]


def query_kernel(state_ref, came_ref, mine_ref, other_ref, keep_ref, send_ref, own_out, other_out, state, halves):
    column = lax.axis_index("width")
    half = state.shape[1]
    per_group = HEADS // 2
    tokens = mine_ref.shape[2]
    unpack_into(state, column, state_ref)
    unpack_into(state, 1 - column, came_ref)
    lane = lax.broadcasted_iota(jnp.int32, (2 * tokens, LANES), 1)
    features, cots, highs, lows, products = [], [], [], [], []
    for place in range(per_group):
        features.append(jnp.concatenate([mine_ref[0, place], other_ref[0, place]], axis=0)[:, :HEAD_DIM])
        cots.append(jnp.concatenate([mine_ref[1, place], other_ref[1, place]], axis=0))
        high, low = split_terms(load_rows(state, place * HEAD_DIM, half))
        highs.append(high)
        lows.append(low)
        pad = jnp.zeros((LANES - HEAD_DIM, LANES), jnp.bfloat16)
        full = jnp.concatenate([mine_ref[0, place], other_ref[0, place]], axis=0)
        both = jnp.concatenate([high, pad, low, pad], axis=0)
        products.append(dot_rows(jnp.concatenate([full, full], axis=1), both))
    scaleds = []
    for place in range(per_group):
        cotangent = cots[place].astype(jnp.float32)
        product = products[place]
        inverse = 1.0 / (product[:, HEAD_DIM : HEAD_DIM + 1] + EPSILON)
        against = jnp.sum(cotangent * product, axis=1, keepdims=True)
        norm_grad = -(against * inverse) * inverse
        scaleds.append(split_terms(jnp.where(lane == HEAD_DIM, norm_grad, cotangent * inverse)))
    for place in range(per_group):
        narrow, (scaled_high, scaled_low) = features[place], scaleds[place]
        both = dot_tokens(narrow, jnp.concatenate([scaled_high, scaled_low], axis=1))
        grad = both[:, :LANES] + both[:, LANES:]
        store_rows(halves, None, place * HEAD_DIM, grad, half)
    for place in range(per_group):
        narrow, high, low = features[place], highs[place], lows[place]
        scaled_high, scaled_low = scaleds[place]
        terms = jnp.concatenate([high, low], axis=1)
        back = dot_columns(jnp.concatenate([scaled_high] * 2, axis=1), terms)
        back = back + dot_columns(jnp.concatenate([scaled_low] * 2, axis=1), terms)
        back = jnp.where(narrow > 0, back, 0.0).astype(jnp.bfloat16)
        own_out[place, :, :HEAD_DIM] = back[:tokens]
        other_out[place, :, :HEAD_DIM] = back[tokens:]
    for out, part in ((keep_ref, column), (send_ref, 1 - column)):
        pack_rows(lambda at: halves[part, tile_of(at)], store_into(out), half // ROWS)


def load_rows(state, first, half):
    cut = min(max(half - first, 0), HEAD_DIM)
    parts = []
    if cut:
        parts.append(state[0, first : first + cut])
    if cut < HEAD_DIM:
        start = first + cut - half
        parts.append(state[1, start : start + HEAD_DIM - cut])
    return parts[0] if len(parts) == 1 else jnp.concatenate(parts, axis=0)


def key_heads(key_ref, value_ref, total, half, group, place, one):
    head = group * (HEADS // 2) + place
    feature = jnp.maximum(head_slice(key_ref, head), 0)
    wide = jnp.concatenate([head_slice(value_ref, head), one], axis=1)
    high, low = split_terms(load_rows(total, place * HEAD_DIM, half))
    grad = dot_columns(wide, high) + dot_columns(wide, low)
    product = dot_rows(feature, high) + dot_rows(feature, low)
    return jnp.where(feature > 0, grad, 0.0).astype(jnp.bfloat16), product[:, :HEAD_DIM].astype(jnp.bfloat16)


def key_kernel(mine, key_ref, value_ref, here_ref, came_ref, *refs):
    column, row = lax.axis_index("width"), lax.axis_index("height")
    given, (key_out, value_out, total) = refs[:-3], refs[-3:]
    half = total.shape[1]
    unpack_into(total, column, here_ref)
    unpack_into(total, 1 - column, came_ref)
    one = tail_block(key_ref.shape[0], 1.0)
    for group in range(2):
        @pl.when(row == (group if mine else 1 - group))
        def _():
            places = range(HEADS // 2)
            grads = [key_heads(key_ref, value_ref, total, half, group, place, one) for place in places]
            for place in places:
                for at, out in enumerate((key_out, value_out)):
                    if mine:
                        out[place, :, :HEAD_DIM] = grads[place][at]
                        continue
                    for which, part in ((group, grads[place][at]), (1 - group, given[at][place, :, :HEAD_DIM])):
                        first = (which * (HEADS // 2) + place) * HEAD_DIM
                        out[:, first : first + HEAD_DIM] = part


def join_kernel(mine_ref, came_ref, out_ref):
    row = lax.axis_index("height")
    per_group = HEADS // 2
    for place in range(per_group):
        mine, came = mine_ref[place, :, :HEAD_DIM], came_ref[place, :, :HEAD_DIM]
        first = jnp.where(row == 0, mine, came)
        second = jnp.where(row == 0, came, mine)
        out_ref[:, place * HEAD_DIM : (place + 1) * HEAD_DIM] = first
        at = (per_group + place) * HEAD_DIM
        out_ref[:, at : at + HEAD_DIM] = second


def struct(shape, dtype=jnp.float32):
    return jax.ShapeDtypeStruct(shape, dtype)


SWAP = [(0, 1), (1, 0)]


def paired(queries, attn_keys, attn_values, attn_cotangent, clip_ids, hidden_pre, conv_weight):
    tokens = queries.shape[1] * queries.shape[2]
    flat = HEADS * HEAD_DIM
    per_group = HEADS // 2
    half = per_group * HEAD_DIM // 2
    frames = lax.axis_size("tm")
    query, key, value, cotangent = (
        part.reshape(tokens, flat) for part in (queries, attn_keys, attn_values, attn_cotangent)
    )
    share = struct((packed_tiles(half // ROWS) * ROWS, LANES))
    pair = struct((2, half, LANES))

    key_hbm, value_hbm = (
        pltpu.with_memory_space_constraint(part, pltpu.HBM) for part in (key, value)
    )
    staged = [pltpu.VMEM((tokens, flat), jnp.bfloat16)] * 2 + [pltpu.SemaphoreType.DMA((2, PARTS))]
    keep, send = vmem_call(
        state_kernel, (pair, pair), [pltpu.VMEM((2, 2, half, LANES), jnp.float32), *staged], n_in=2, in_hbm=True,
        flops=2 * tokens * flat * LANES, bytes_accessed=4 * tokens * flat + 8 * half * LANES * 2,
    )(key_hbm, value_hbm)
    hidden, send = lax.optimization_barrier((hidden_pre, send))
    edges = row_edges(hidden)
    came = lax.ppermute(send, "width", SWAP)
    came, edges = lax.optimization_barrier((came, edges))
    mine, other = vmem_call(pick_kernel, (share, share), n_in=2, bytes_accessed=24 * half * LANES)(keep, came)
    came = lax.ppermute(other, "height", SWAP)

    packed = struct((2, per_group, tokens, LANES), jnp.bfloat16)
    query, cotangent, hidden, _ = lax.optimization_barrier((query, cotangent, hidden, mine))
    heads_mine, heads_other, masks = vmem_call(
        heads_kernel,
        (packed, packed, struct((8, LANES))),
        [pltpu.VMEM((2, 2, per_group, tokens, LANES), jnp.bfloat16), *staged,
         pltpu.SMEM(clip_ids.shape, jnp.int32), pltpu.SemaphoreType.DMA],
        n_in=3, in_hbm=True, bytes_accessed=12 * tokens * flat,
    )(*(pltpu.with_memory_space_constraint(part, pltpu.HBM) for part in (query, cotangent, clip_ids)))
    side = side_edge(hidden[0])
    edges, _ = lax.optimization_barrier((edges, heads_other))
    halo = halo_arrays(edges, side)
    _, own = lax.optimization_barrier(((heads_other, side), mine + came))
    heads_sent = lax.ppermute(heads_other, "height", SWAP)

    def along_frames(own, step, beside):
        moves = [[(at, at + step * hop) for at in range(frames) if 0 <= at + step * hop < frames] for hop in (1, 2)]
        near = lax.ppermute(own, "tm", moves[0])
        far = lax.ppermute(own, "tm", moves[1])
        near, far, beside = beside(own, near, far)
        at = 0 if step > 0 else 2
        return own + masks[at : at + 1] * near + masks[at + 1 : at + 2] * far, beside

    def fetch(own, near, far):
        return lax.optimization_barrier((near, far, heads_sent))

    state, heads_came = along_frames(own, 1, fetch)
    came = lax.ppermute(state, "width", SWAP)
    back = struct((per_group, tokens, LANES), jnp.bfloat16)
    keep, send, back_mine, back_other = vmem_call(
        query_kernel, (share, share, back, back),
        [pltpu.VMEM((2, half, LANES), jnp.float32), pltpu.VMEM((2, half, LANES), jnp.float32)], n_in=4,
        flops=14 * tokens * flat * LANES, bytes_accessed=8 * tokens * flat,
    )(state, came, heads_mine, heads_came)
    came = lax.ppermute(send, "width", SWAP)
    own, halo = lax.optimization_barrier((keep + came, halo))

    def convolve(own, near, far):
        other, _ = lax.optimization_barrier((back_other, own))
        back_came = lax.ppermute(other, "height", SWAP)
        hidden_grad = ffn(hidden_pre, conv_weight, halo)
        query_grad = vmem_call(
            join_kernel, struct((tokens, flat), jnp.bfloat16), n_in=2, bytes_accessed=4 * tokens * flat
        )(back_mine, back_came)
        near, far, hidden_grad = lax.optimization_barrier((near, far, hidden_grad))
        return near, far, (query_grad, hidden_grad)

    total, (query_grad, hidden_grad) = along_frames(own, -1, convolve)
    far = lax.ppermute(total, "height", SWAP)
    near_came = lax.ppermute(total, "width", SWAP)
    state = [pltpu.VMEM((2, half, LANES), jnp.float32)]
    cost = {"flops": 4 * tokens * flat * LANES, "bytes_accessed": 4 * tokens * flat}
    near_grads = vmem_call(functools.partial(key_kernel, True), (back, back), state, n_in=4, **cost)(
        key, value, total, near_came
    )
    far, query_grad = lax.optimization_barrier((far, query_grad))
    far_came = lax.ppermute(far, "width", SWAP)
    out = struct((tokens, flat), jnp.bfloat16)
    key_grad, value_gradient = vmem_call(functools.partial(key_kernel, False), (out, out), state, n_in=6, **cost)(
        key, value, far, far_came, *near_grads
    )
    grads = tuple(part.reshape(queries.shape) for part in (query_grad, key_grad, value_gradient))
    return (*grads, hidden_grad)


def mixed_ffn(hidden_pre, conv_weight):
    row_count = hidden_pre.shape[1]
    col_count = hidden_pre.shape[2]
    split_at = hidden_pre.shape[3] // 2
    widened = padded(hidden_pre, (("height", 1), ("width", 2)), 2)[0]
    conv_out = depthwise(widened, conv_weight, 1, 1, row_count + 2, col_count + 2)
    row_global = lax.axis_index("height") * row_count + jnp.arange(row_count + 2) - 1
    col_global = lax.axis_index("width") * col_count + jnp.arange(col_count + 2) - 1
    row_inside = (row_global >= 0) & (row_global < row_count * lax.axis_size("height"))
    col_inside = (col_global >= 0) & (col_global < col_count * lax.axis_size("width"))
    inside = (row_inside[:, None] & col_inside[None, :]).astype(jnp.float32)
    conv_grad = glu_grad(conv_out, split_at) * inside[:, :, None]
    hidden_grad = depthwise(conv_grad, conv_weight, 1, -1, row_count, col_count)
    hidden_grad = hidden_grad[None].astype(jnp.bfloat16)
    return hidden_grad


TILES = 8
REACH = 2
UNROLL = 2


def conv_kernel(bases, row_refs, *refs):
    halo_rows, refs = refs[:row_refs], refs[row_refs:]
    side_ref, refs = refs[0], refs[1:]
    corners, refs = refs[:row_refs], refs[row_refs:]
    block_ref, weight_ref = refs[:2]
    out_hbm, taps, value_in, gate_in, value_grad, gate_grad, *results, out_ref, sems = refs[-8 - 2 * UNROLL :]
    rows, cols, channels = block_ref.shape
    lane_tiles = channels // LANES // 2
    pitch = -(-lane_tiles // TILES) * TILES
    row, column = lax.axis_index("height"), lax.axis_index("width")
    first_row, last_row = row == 0, row == lax.axis_size("height") - 1
    wide, tall = cols + 2 * REACH, rows + 2 * REACH
    grad_wide = wide - 2

    for base in bases:
        for tile in range(base, min(base + TILES, lane_tiles)):
            for place, source in ((tile, tile), (pitch + tile, lane_tiles + tile)):
                lanes = slice(source * LANES, (source + 1) * LANES)
                taps[pl.ds(place, 9, stride=2 * pitch), :] = weight_ref[:, lanes]

    def source_at(at_row, at_col):
        return pl.multiple_of((at_row * wide + at_col) * TILES, TILES)

    def grad_at(at_row, at_col):
        return pl.multiple_of((at_row * grad_wide + at_col) * TILES, TILES)

    zero = jnp.zeros((TILES, LANES), jnp.float32)
    low_border = jnp.where(first_row, 0, rows + REACH)
    outer_col = jnp.where(column == 0, 0, cols + REACH)
    side_col = jnp.where(column == 0, cols + REACH, 0)
    grad_outer_col = jnp.where(column == 0, 0, grad_wide - 1)
    start_col = jnp.where(column == 0, REACH, REACH - 1)
    low, high = jnp.where(first_row, REACH, REACH - 1), jnp.where(last_row, rows + REACH, rows + REACH + 1)

    for ref in (value_in, gate_in):
        @pl.loop(0, tall)
        def _(at):
            for extra in range(REACH):
                ref[pl.ds(source_at(at, outer_col + extra), TILES), :] = zero

    for ref in (value_grad, gate_grad):
        @pl.loop(0, rows + 2)
        def _(at):
            ref[pl.ds(grad_at(at, grad_outer_col), TILES), :] = zero

        for edge, at in ((first_row, 0), (last_row, rows + 1)):
            @pl.when(edge)
            def _():
                for col in range(grad_wide):
                    ref[pl.ds(grad_at(at, col), TILES), :] = zero

    copies = []
    for base in bases:
        count = min(TILES, lane_tiles - base)

        def spread(load, at_row, at_col, length):
            for ref, offset in ((value_in, base), (gate_in, lane_tiles + base)):
                for tile in range(count):
                    part = load(slice((offset + tile) * LANES, (offset + tile + 1) * LANES)).astype(jnp.float32)
                    ref[pl.ds(source_at(at_row, at_col) + tile, length, stride=TILES), :] = part

        @pl.loop(0, rows)
        def _(at):
            spread(lambda lanes: block_ref[at, :, lanes], at + REACH, REACH, cols)
            spread(lambda lanes: side_ref[at, :, lanes], at + REACH, side_col, REACH)

        for edge, at, which in ((first_row, 0, 0), (last_row, rows + REACH, row_refs - 1)):
            rows_ref, corner_ref = halo_rows[which], corners[which]
            for extra in range(REACH):
                @pl.when(jnp.logical_not(edge))
                def _():
                    spread(lambda lanes: rows_ref[extra, :, lanes], at + extra, REACH, cols)
                    spread(lambda lanes: corner_ref[extra, :, lanes], at + extra, side_col, REACH)

                @pl.when(edge)
                def _():
                    for ref in (value_in, gate_in):
                        for col in range(wide):
                            ref[pl.ds(source_at(at + extra, col), TILES), :] = zero

        def weights(offset):
            return [taps[2 * pitch * tap + offset + base : 2 * pitch * tap + offset + base + TILES, :] for tap in range(9)]

        value_taps, gate_taps = weights(0), weights(pitch)

        @pl.loop(low, high)
        def _(at):
            cache = {}

            def read(ref, a, col):
                if (id(ref), a, col) not in cache:
                    cache[id(ref), a, col] = ref[pl.ds(source_at(at + a, start_col + col), TILES), :]
                return cache[id(ref), a, col]

            for col in range(cols + 1):
                def conv(ref, kernel):
                    total = None
                    for a in (-1, 0, 1):
                        for b in (-1, 0, 1):
                            term = kernel[3 * (a + 1) + b + 1] * read(ref, a, col + b)
                            total = term if total is None else total + term
                    return total

                value, gate = conv(value_in, value_taps), conv(gate_in, gate_taps)
                squash = jax.nn.sigmoid(gate)
                gated = gate * squash
                glu = value * gated
                place = pl.ds(grad_at(at - 1, start_col + col - 1), TILES)
                value_grad[place, :] = glu * gated
                gate_grad[place, :] = glu * value * (squash + gated * (1.0 - squash))

        def gather(at, results):
            cache = {}

            def read(ref, a, col):
                if (id(ref), a, col) not in cache:
                    cache[id(ref), a, col] = ref[pl.ds(grad_at(at + a, col), TILES), :]
                return cache[id(ref), a, col]

            for col in range(cols):
                for ref, kernel, result in zip((value_grad, gate_grad), (value_taps, gate_taps), results):
                    total = None
                    for a in (-1, 0, 1):
                        for b in (-1, 0, 1):
                            term = kernel[3 * (a + 1) + b + 1] * read(ref, 1 - a, col + 1 - b)
                            total = term if total is None else total + term
                    result[pl.ds(col, TILES, stride=cols), :] = total

        def settle(at, results):
            for result, offset in zip(results, (base, lane_tiles + base)):
                for tile in range(count):
                    lanes = slice((offset + tile) * LANES, (offset + tile + 1) * LANES)
                    out_ref[at, :, lanes] = result[tile * cols : (tile + 1) * cols, :].astype(jnp.bfloat16)

        @pl.loop(0, rows // UNROLL)
        def _(at):
            for step in range(UNROLL):
                gather(at * UNROLL + step, results[2 * step : 2 * step + 2])
                if step:
                    settle(at * UNROLL + step - 1, results[2 * step - 2 : 2 * step])
            settle(at * UNROLL + UNROLL - 1, results[2 * UNROLL - 2 :])

        for at, offset in enumerate((base, lane_tiles + base)):
            lanes = pl.ds(offset * LANES, count * LANES)
            copy = pltpu.make_async_copy(out_ref.at[:, :, lanes], out_hbm.at[:, :, lanes], sems.at[at, base // TILES])
            copy.start()
            copies.append(copy)
    for copy in copies:
        copy.wait()


def edge_slice(block, dim, low_side):
    start = jnp.where(low_side, 0, block.shape[dim] - REACH)
    return lax.dynamic_slice_in_dim(block, start, REACH, axis=dim)


def row_edges(hidden_pre):
    block = hidden_pre[0]
    if lax.axis_size("height") == 2:
        return [edge_slice(block, 0, lax.axis_index("height") == 1)]
    return [block[block.shape[0] - REACH :], block[:REACH]]


def side_edge(block):
    return edge_slice(block, 1, lax.axis_index("width") == 1)


def halo_arrays(edges, side):
    height = lax.axis_size("height")
    if height == 2:
        moves = [SWAP]
    else:
        moves = [[(at, at + 1) for at in range(height - 1)], [(at + 1, at) for at in range(height - 1)]]
    halo_rows = [lax.ppermute(edge, "height", move) for edge, move in zip(edges, moves)]
    side = lax.ppermute(side, "width", SWAP)
    corners = [lax.ppermute(side_edge(part), "width", SWAP) for part in halo_rows]
    return halo_rows, side, corners


def conv_part(bases, halo, block, conv_weight, given=()):
    halo_rows, side, corners = halo
    rows, cols, channels = block.shape
    lane_tiles = channels // LANES // 2
    pitch = -(-lane_tiles // TILES) * TILES
    source = pltpu.VMEM(((rows + 2 * REACH) * (cols + 2 * REACH) * TILES, LANES), jnp.float32)
    grad = pltpu.VMEM(((rows + 2) * (cols + 2) * TILES, LANES), jnp.float32)
    result = pltpu.VMEM((cols * TILES, LANES), jnp.float32)
    size = rows * cols * channels
    return vmem_call(
        functools.partial(conv_kernel, bases, len(halo_rows)),
        struct((rows, cols, channels), jnp.bfloat16),
        [pltpu.VMEM((9 * 2 * pitch, LANES), jnp.float32), source, source, grad, grad, *[result] * (2 * UNROLL),
         pltpu.VMEM((rows, cols, channels), jnp.bfloat16), pltpu.SemaphoreType.DMA((2, pitch // TILES))],
        n_in=2 * len(halo_rows) + 3, n_given=len(given), flops=size * len(bases), bytes_accessed=size, vmem_mib=12,
        out_hbm=True,
    )(*halo_rows, side, *corners, block, conv_weight, *given)


def conv_bases(hidden_pre):
    lane_tiles = hidden_pre.shape[3] // LANES // 2
    return list(range(0, lane_tiles, TILES))


def ffn(hidden_pre, conv_weight, halo):
    return conv_part(conv_bases(hidden_pre), halo, hidden_pre[0], conv_weight)[None]


def per_device(queries, attn_keys, attn_values, attn_cotangent, clip_ids, hidden_pre, conv_weight):
    blocked = lax.axis_size("width") == 2 and hidden_pre.shape[0] == 1 and hidden_pre.shape[3] % (2 * LANES) == 0
    pairs = lax.axis_size("height") == 2 and 3 <= lax.axis_size("tm") <= 4 and HEADS % 2 == 0
    if blocked and pairs:
        return paired(queries, attn_keys, attn_values, attn_cotangent, clip_ids, hidden_pre, conv_weight)
    grads = general_attention(queries, attn_keys, attn_values, attn_cotangent, clip_ids)
    if blocked:
        return (*grads, ffn(hidden_pre, conv_weight, halo_arrays(row_edges(hidden_pre), side_edge(hidden_pre[0]))))
    return (*grads, mixed_ffn(hidden_pre, conv_weight))


def solution(mesh):
    return jax.shard_map(
        per_device,
        mesh=mesh,
        in_specs=(
            P(("group", "tm"), "height", "width", None),
            P(("group", "tm"), "height", "width", None),
            P(("group", "tm"), "height", "width", None),
            P(("group", "tm"), "height", "width", None),
            P("group"),
            P(("group", "tm"), "height", "width", None),
            P(),
        ),
        out_specs=(
            P(("group", "tm"), "height", "width", None),
            P(("group", "tm"), "height", "width", None),
            P(("group", "tm"), "height", "width", None),
            P(("group", "tm"), "height", "width", None),
        ),
        check_vma=False,
    )
```

```python
import functools
from functools import reduce

import jax
import jax.numpy as jnp
from jax import lax
from jax.experimental import pallas as pl
from jax.experimental.pallas import tpu as pltpu
from jax.sharding import PartitionSpec as P

HEAD_DIM = 112
HEADS = 10


EPSILON = 1e-06
TOP_PRECISION = lax.Precision.HIGHEST


def entering(value, axis, join, neutral, backward):
    count, mine = (lax.axis_size(axis), lax.axis_index(axis))
    pieces = jax.tree.map(lambda part: lax.all_gather(part, axis), value)
    if backward:
        pieces = jax.tree.map(lambda part: part[::-1], pieces)
        mine = count - 1 - mine
    so_far = jax.tree.map(
        lambda part, zero: jnp.full_like(part, 0) + jnp.asarray(zero, part.dtype), value, neutral
    )

    def turn(position, so_far):
        longer = join(so_far, jax.tree.map(lambda part: part[position], pieces))
        return jax.tree.map(lambda new, old: jnp.where(position < mine, new, old), longer, so_far)

    return lax.fori_loop(0, count - 1, turn, so_far)


def padded(block, sides, width):
    for axis, dim in sides:
        count = lax.axis_size(axis)
        forward = [(i, i + 1) for i in range(count - 1)]
        backward = [(target, source) for source, target in forward]
        low = lax.ppermute(
            lax.slice_in_dim(block, block.shape[dim] - width, None, axis=dim), axis, forward
        )
        high = lax.ppermute(lax.slice_in_dim(block, 0, width, axis=dim), axis, backward)
        block = jnp.concatenate([low, block, high], axis=dim)
    return block


def carry_on(earlier, later):
    keeping = 1.0 - later[0]
    return (
        jnp.maximum(earlier[0], later[0]),
        later[1] + keeping * earlier[1],
        later[2] + keeping * earlier[2],
    )


def clip_flags(clip_ids):
    frame = lax.axis_index("tm")
    frame_count = lax.axis_size("tm")
    current = lax.dynamic_index_in_dim(clip_ids, frame, 0, keepdims=False)
    before = lax.dynamic_index_in_dim(clip_ids, jnp.maximum(frame - 1, 0), 0, keepdims=False)
    after = lax.dynamic_index_in_dim(
        clip_ids, jnp.minimum(frame + 1, frame_count - 1), 0, keepdims=False
    )
    starts = jnp.where((frame == 0) | (current != before), 1.0, 0.0).astype(jnp.float32)
    ends = jnp.where((frame == frame_count - 1) | (current != after), 1.0, 0.0).astype(jnp.float32)
    return (starts, ends)


def glu_grad(conv_out, split_at):
    value_part = conv_out[..., :split_at]
    gate_part = conv_out[..., split_at:]
    squash = jax.nn.sigmoid(gate_part)
    glu = value_part * gate_part * squash
    value_gradient = glu * gate_part * squash
    gate_grad = glu * value_part * squash * (1.0 + gate_part * (1.0 - squash))
    return jnp.concatenate([value_gradient, gate_grad], axis=-1)


def depthwise(source, weights, start, sign, height_out, width_out):
    terms = []
    for offset_row in (-1, 0, 1):
        for offset_col in (-1, 0, 1):
            tap_index = (offset_row + 1) * 3 + offset_col + 1
            row_start = start + sign * offset_row
            col_start = start + sign * offset_col
            window = source[
                row_start : row_start + height_out, col_start : col_start + width_out
            ].astype(jnp.float32)
            terms.append(weights[tap_index] * window)
    return reduce(lambda first, second: first + second, terms)


def general_attention(queries, attn_keys, attn_values, attn_cotangent, clip_ids):
    token_count = queries.shape[1] * queries.shape[2]
    flat_width = HEADS * HEAD_DIM
    starts, ends = clip_flags(clip_ids)
    zero_flag = jnp.zeros((), jnp.float32)
    feature_keys = jnp.maximum(attn_keys, 0).reshape(token_count, HEADS, HEAD_DIM)
    value_row_block = attn_values.reshape(token_count, HEADS, HEAD_DIM)
    local_kv = jnp.einsum(
        "jrf,jrx->rfx", feature_keys, value_row_block, preferred_element_type=jnp.float32
    ).reshape(flat_width, HEAD_DIM)
    local_norm = jnp.sum(feature_keys.astype(jnp.float32), axis=0).reshape(flat_width)
    share_kv, share_norm = (
        lax.psum_scatter(local_kv, ("height", "width"), scatter_dimension=0, tiled=True),
        lax.psum_scatter(local_norm, ("height", "width"), scatter_dimension=0, tiled=True),
    )
    earlier = entering(
        (starts, share_kv, share_norm),
        "tm",
        carry_on,
        (zero_flag, jnp.zeros_like(share_kv), jnp.zeros_like(share_norm)),
        False,
    )
    part_kv = share_kv + (1.0 - starts) * earlier[1]
    part_norm = share_norm + (1.0 - starts) * earlier[2]
    state_key_value, state_norm = (
        lax.all_gather(part_kv, ("height", "width"), axis=0, tiled=True),
        lax.all_gather(part_norm, ("height", "width"), axis=0, tiled=True),
    )
    state_key_value = state_key_value.reshape(HEADS, HEAD_DIM, HEAD_DIM)
    state_norm = state_norm.reshape(HEADS, HEAD_DIM)
    feature_query = (
        jnp.maximum(queries, 0).reshape(token_count, HEADS, HEAD_DIM).astype(jnp.float32)
    )
    cotangent = attn_cotangent.reshape(token_count, HEADS, HEAD_DIM).astype(jnp.float32)
    ratio_numerator = jnp.einsum(
        "cob,obq->coq", feature_query, state_key_value, precision=TOP_PRECISION
    )
    denominator = (
        jnp.einsum("thk,hk->th", feature_query, state_norm, precision=TOP_PRECISION) + EPSILON
    )
    attended = ratio_numerator / denominator[..., None]
    scaled_gradient = cotangent / denominator[..., None]
    denominator_grad = -jnp.sum(cotangent * attended, axis=-1) / denominator
    query_feature_gradient = jnp.einsum(
        "dla,lja->dlj", scaled_gradient, state_key_value, precision=TOP_PRECISION
    )
    query_feature_gradient = query_feature_gradient + state_norm[None] * denominator_grad[..., None]
    query_grad = (
        jnp.where(feature_query > 0.0, query_feature_gradient, 0.0)
        .reshape(queries.shape)
        .astype(jnp.bfloat16)
    )
    gradient_key_value = jnp.einsum(
        "jrf,jrx->rfx", feature_query, scaled_gradient, precision=TOP_PRECISION
    ).reshape(flat_width, HEAD_DIM)
    grad_norm = jnp.einsum(
        "thk,th->hk", feature_query, denominator_grad, precision=TOP_PRECISION
    ).reshape(flat_width)
    share_grad_kv, share_grad_norm = (
        lax.psum_scatter(gradient_key_value, ("height", "width"), scatter_dimension=0, tiled=True),
        lax.psum_scatter(grad_norm, ("height", "width"), scatter_dimension=0, tiled=True),
    )
    later = entering(
        (ends, share_grad_kv, share_grad_norm),
        "tm",
        carry_on,
        (zero_flag, jnp.zeros_like(share_grad_kv), jnp.zeros_like(share_grad_norm)),
        True,
    )
    part_grad_kv = share_grad_kv + (1.0 - ends) * later[1]
    part_grad_norm = share_grad_norm + (1.0 - ends) * later[2]
    total_key_value, norm_total = (
        lax.all_gather(part_grad_kv, ("height", "width"), axis=0, tiled=True),
        lax.all_gather(part_grad_norm, ("height", "width"), axis=0, tiled=True),
    )
    total_key_value = total_key_value.reshape(HEADS, HEAD_DIM, HEAD_DIM)
    norm_total = norm_total.reshape(HEADS, HEAD_DIM)
    key_feat_grad = (
        jnp.einsum(
            "dla,lja->dlj",
            value_row_block.astype(jnp.float32),
            total_key_value,
            precision=TOP_PRECISION,
        )
        + norm_total[None]
    )
    key_grad = (
        jnp.where(feature_keys > 0, key_feat_grad, 0.0)
        .reshape(attn_keys.shape)
        .astype(jnp.bfloat16)
    )
    value_gradient = jnp.einsum(
        "cob,obq->coq", feature_keys.astype(jnp.float32), total_key_value, precision=TOP_PRECISION
    )
    value_gradient = value_gradient.reshape(attn_values.shape).astype(jnp.bfloat16)
    return (query_grad, key_grad, value_gradient)


LANES = 128


def split_terms(value, count=2):
    terms = []
    for _ in range(count):
        terms.append(value.astype(jnp.bfloat16))
        value = value - terms[-1].astype(jnp.float32)
    return terms


def beside(*parts):
    return jnp.concatenate(parts, axis=1)


def dot_tokens(left, right):
    return lax.dot_general(left, right, (((0,), (0,)), ((), ())), preferred_element_type=jnp.float32)


def dot_rows(left, right):
    return lax.dot_general(left, right, (((1,), (0,)), ((), ())), preferred_element_type=jnp.float32)


def dot_columns(left, right):
    return lax.dot_general(left, right, (((1,), (1,)), ((), ())), preferred_element_type=jnp.float32)


def head_slice(ref, head):
    return ref[:, head * HEAD_DIM : (head + 1) * HEAD_DIM]


def tail_block(rows, first):
    column = lax.broadcasted_iota(jnp.int32, (rows, LANES - HEAD_DIM), 1)
    return jnp.where(column == 0, first, 0.0).astype(jnp.bfloat16)


def vmem_call(kernel, out_shape, scratch=(), smem_first=False, n_in=0, flops=0, bytes_accessed=0, vmem_mib=8, in_hbm=False, out_hbm=False, n_given=0):
    vmem = pl.BlockSpec(memory_space=pltpu.VMEM)
    in_specs = [pl.BlockSpec(memory_space=pltpu.HBM) if in_hbm else vmem] * n_in
    in_specs += [pl.BlockSpec(memory_space=pltpu.HBM)] * n_given
    if smem_first:
        in_specs[0] = pl.BlockSpec(memory_space=pltpu.SMEM)
    return pl.pallas_call(
        kernel,
        out_shape=out_shape,
        in_specs=in_specs,
        out_specs=jax.tree.map(lambda _: pl.BlockSpec(memory_space=pltpu.HBM) if out_hbm else vmem, out_shape),
        scratch_shapes=list(scratch),
        input_output_aliases={n_in: 0} if n_given else {},
        cost_estimate=pl.CostEstimate(flops=flops, bytes_accessed=bytes_accessed, transcendentals=0),
        compiler_params=pltpu.CompilerParams(vmem_limit_bytes=vmem_mib << 20),
    )


ROWS = 8
SPARE = LANES - HEAD_DIM
PIECES = HEAD_DIM // SPARE


def packed_tiles(tiles):
    return next(kept for kept in range(tiles + 1) if (tiles - kept) * PIECES - (-tiles // SPARE) <= kept)


def tile_of(at):
    return slice(at * ROWS, (at + 1) * ROWS)


def pack_rows(read, write, tiles):
    kept = packed_tiles(tiles)
    moved = (tiles - kept) * PIECES
    lane = lax.broadcasted_iota(jnp.int32, (ROWS, LANES), 1)
    rows = [read(at) for at in range(tiles)]
    for at in range(kept):
        block = rows[at]
        if at < moved:
            extra, piece = divmod(at, PIECES)
            shifted = pltpu.roll(rows[kept + extra], HEAD_DIM - SPARE * piece, 1)
            block = jnp.where(lane < HEAD_DIM, block, shifted)
        else:
            first = (at - moved) * SPARE
            for step in range(min(SPARE, tiles - first)):
                norm = rows[first + step]
                norm = pltpu.roll(norm, step, 1) if step else norm
                block = jnp.where(lane == HEAD_DIM + step, norm, block)
        write(at, block)


def unpack_rows(read, write, tiles):
    kept = packed_tiles(tiles)
    moved = (tiles - kept) * PIECES
    lane = lax.broadcasted_iota(jnp.int32, (ROWS, LANES), 1)
    rows = [read(at) for at in range(kept)]
    for at in range(tiles):
        if at < kept:
            block = rows[at]
        else:
            for piece in range(PIECES):
                shifted = pltpu.roll(rows[(at - kept) * PIECES + piece], SPARE * (piece + 1), 1)
                block = shifted if piece == 0 else jnp.where(lane < SPARE * piece, block, shifted)
        group, step = divmod(at, SPARE)
        norm = rows[moved + group]
        norm = pltpu.roll(norm, LANES - step, 1) if step else norm
        write(at, jnp.where(lane == HEAD_DIM, norm, block))


def store_into(ref, *index):
    def write(at, block):
        ref[(*index, tile_of(at))] = block

    return write


def unpack_into(state, index, packed):
    unpack_rows(lambda at: packed[tile_of(at)], store_into(state, index), state.shape[1] // ROWS)


PARTS = 4


def stage(sources, targets, sems):
    copies = []
    for at, (source, target) in enumerate(zip(sources, targets)):
        rows = source.shape[0] // PARTS
        for part in range(PARTS):
            span = pl.ds(part * rows, rows)
            copies.append(pltpu.make_async_copy(source.at[span], target.at[span], sems.at[at, part]))
    for copy in copies:
        copy.start()
    for copy in copies:
        copy.wait()


def state_kernel(key_hbm, value_hbm, keep_ref, send_ref, halves, key_ref, value_ref, sems):
    stage((key_hbm, value_hbm), (key_ref, value_ref), sems)
    tokens = key_ref.shape[0]
    one = tail_block(tokens, 1.0)
    half = halves.shape[2]
    per_group = HEADS // 2
    column = lax.axis_index("width")
    blocks = []
    for head in range(HEADS):
        feature = jnp.maximum(head_slice(key_ref, head), 0)
        wide = jnp.concatenate([head_slice(value_ref, head), one], axis=1)
        blocks.append(dot_tokens(feature, wide))
    for head in range(HEADS):
        group, place = divmod(head, per_group)
        store_rows(halves, group, place * HEAD_DIM, blocks[head], half)
    keep_ref[...] = halves[column]
    send_ref[...] = halves[1 - column]


def store_rows(halves, group, first, block, half):
    cut = min(max(half - first, 0), HEAD_DIM)
    if cut:
        index = (0, group) if group is not None else (0,)
        halves[(*index, slice(first, first + cut))] = block[:cut]
    if cut < HEAD_DIM:
        index = (1, group) if group is not None else (1,)
        start = first + cut - half
        halves[(*index, slice(start, start + HEAD_DIM - cut))] = block[cut:]


def pick_kernel(keep_ref, came_ref, mine_ref, other_ref):
    row = lax.axis_index("height")
    tiles = keep_ref.shape[1] // ROWS
    for out, at_row in ((mine_ref, row), (other_ref, 1 - row)):
        pack_rows(lambda at: keep_ref[at_row, tile_of(at)] + came_ref[at_row, tile_of(at)], store_into(out), tiles)


def write_masks(clip_ref, out_ref):
    frame = lax.axis_index("tm")
    last = lax.axis_size("tm") - 1
    here = clip_ref[frame]
    line = lax.broadcasted_iota(jnp.int32, out_ref.shape, 0)
    masks = jnp.zeros(out_ref.shape, jnp.float32)
    for at, (step, hop) in enumerate(((1, 1), (1, 2), (-1, 1), (-1, 2))):
        other = frame - step * hop
        inside = (other >= 0) & (other <= last)
        same = inside & (clip_ref[jnp.clip(other, 0, last)] == here)
        masks = jnp.where(line == at, jnp.where(same, 1.0, 0.0), masks)
    out_ref[...] = masks


def heads_kernel(query_hbm, cotangent_hbm, clip_hbm, mine_ref, other_ref, mask_ref, groups, query_ref, cotangent_ref, sems, clip_ref, clip_sem):
    clip_copy = pltpu.make_async_copy(clip_hbm, clip_ref, clip_sem)
    clip_copy.start()
    stage((query_hbm, cotangent_hbm), (query_ref, cotangent_ref), sems)
    clip_copy.wait()
    write_masks(clip_ref, mask_ref)
    none = tail_block(query_ref.shape[0], 0.0)
    per_group = HEADS // 2
    row = lax.axis_index("height")
    for head in range(HEADS):
        group, place = divmod(head, per_group)
        feature = jnp.maximum(head_slice(query_ref, head), 0)
        groups[group, 0, place] = jnp.concatenate([feature, none], axis=1)
        groups[group, 1, place] = jnp.concatenate([head_slice(cotangent_ref, head), none], axis=1)
    mine_ref[...] = groups[row]
    other_ref[...] = groups[1 - row]


def query_kernel(state_ref, came_ref, mine_ref, other_ref, keep_ref, send_ref, own_out, other_out, state, halves):
    column = lax.axis_index("width")
    half = state.shape[1]
    per_group = HEADS // 2
    tokens = mine_ref.shape[2]
    unpack_into(state, column, state_ref)
    unpack_into(state, 1 - column, came_ref)
    lane = lax.broadcasted_iota(jnp.int32, (2 * tokens, LANES), 1)
    places = range(per_group)
    features, cots, states, products = [], [], [], []
    pad = jnp.zeros((LANES - HEAD_DIM, LANES), jnp.bfloat16)
    for place in places:
        full = jnp.concatenate([mine_ref[0, place], other_ref[0, place]], axis=0)
        features.append(full[:, :HEAD_DIM])
        cots.append(jnp.concatenate([mine_ref[1, place], other_ref[1, place]], axis=0))
        high, low, rest = split_terms(load_rows(state, place * HEAD_DIM, half), 3)
        states.append((high, low, rest))
        product = dot_rows(beside(full, full), jnp.concatenate([high, pad, low, pad], axis=0))
        products.append(product + dot_rows(features[-1], rest))
    scaleds = []
    for place in places:
        cotangent = cots[place].astype(jnp.float32)
        product = products[place]
        inverse = 1.0 / (product[:, HEAD_DIM : HEAD_DIM + 1] + EPSILON)
        against = jnp.sum(cotangent * product, axis=1, keepdims=True)
        norm_grad = -(against * inverse) * inverse
        scaleds.append(split_terms(jnp.where(lane == HEAD_DIM, norm_grad, cotangent * inverse), 3))
    for place in places:
        both = dot_tokens(features[place], beside(*scaleds[place][:2]))
        store_rows(halves, None, place * HEAD_DIM, both[:, :LANES] + both[:, LANES:], half)
    for place in places:
        narrow, (high, low, rest) = features[place], states[place]
        first, second, third = scaleds[place]
        back = dot_columns(beside(first, third), beside(rest, high))
        back = back + dot_columns(beside(second, second), beside(high, low))
        back = back + dot_columns(beside(first, first), beside(high, low))
        back = jnp.where(narrow > 0, back, 0.0).astype(jnp.bfloat16)
        own_out[place, :, :HEAD_DIM] = back[:tokens]
        other_out[place, :, :HEAD_DIM] = back[tokens:]
    for out, part in ((keep_ref, column), (send_ref, 1 - column)):
        pack_rows(lambda at: halves[part, tile_of(at)], store_into(out), half // ROWS)


def load_rows(state, first, half):
    cut = min(max(half - first, 0), HEAD_DIM)
    parts = []
    if cut:
        parts.append(state[0, first : first + cut])
    if cut < HEAD_DIM:
        start = first + cut - half
        parts.append(state[1, start : start + HEAD_DIM - cut])
    return parts[0] if len(parts) == 1 else jnp.concatenate(parts, axis=0)


def key_heads(key_ref, value_ref, total, half, group, place, one):
    head = group * (HEADS // 2) + place
    feature = jnp.maximum(head_slice(key_ref, head), 0)
    wide = jnp.concatenate([head_slice(value_ref, head), one], axis=1)
    high, low = split_terms(load_rows(total, place * HEAD_DIM, half))
    grad = dot_columns(beside(wide, wide), beside(high, low))
    product = dot_rows(feature, high) + dot_rows(feature, low)
    return jnp.where(feature > 0, grad, 0.0).astype(jnp.bfloat16), product[:, :HEAD_DIM].astype(jnp.bfloat16)


def key_kernel(mine, key_ref, value_ref, here_ref, came_ref, *refs):
    column, row = lax.axis_index("width"), lax.axis_index("height")
    given, (key_out, value_out, total) = refs[:-3], refs[-3:]
    half = total.shape[1]
    unpack_into(total, column, here_ref)
    unpack_into(total, 1 - column, came_ref)
    one = tail_block(key_ref.shape[0], 1.0)
    for group in range(2):
        @pl.when(row == (group if mine else 1 - group))
        def _():
            places = range(HEADS // 2)
            grads = [key_heads(key_ref, value_ref, total, half, group, place, one) for place in places]
            for place in places:
                for at, out in enumerate((key_out, value_out)):
                    if mine:
                        out[place, :, :HEAD_DIM] = grads[place][at]
                        continue
                    for which, part in ((group, grads[place][at]), (1 - group, given[at][place, :, :HEAD_DIM])):
                        first = (which * (HEADS // 2) + place) * HEAD_DIM
                        out[:, first : first + HEAD_DIM] = part


def join_kernel(mine_ref, came_ref, out_ref):
    row = lax.axis_index("height")
    per_group = HEADS // 2
    for place in range(per_group):
        mine, came = mine_ref[place, :, :HEAD_DIM], came_ref[place, :, :HEAD_DIM]
        first = jnp.where(row == 0, mine, came)
        second = jnp.where(row == 0, came, mine)
        out_ref[:, place * HEAD_DIM : (place + 1) * HEAD_DIM] = first
        at = (per_group + place) * HEAD_DIM
        out_ref[:, at : at + HEAD_DIM] = second


def struct(shape, dtype=jnp.float32):
    return jax.ShapeDtypeStruct(shape, dtype)


SWAP = [(0, 1), (1, 0)]


def paired(queries, attn_keys, attn_values, attn_cotangent, clip_ids, hidden_pre, conv_weight):
    tokens = queries.shape[1] * queries.shape[2]
    flat = HEADS * HEAD_DIM
    per_group = HEADS // 2
    half = per_group * HEAD_DIM // 2
    frames = lax.axis_size("tm")
    query, key, value, cotangent = (
        part.reshape(tokens, flat) for part in (queries, attn_keys, attn_values, attn_cotangent)
    )
    share = struct((packed_tiles(half // ROWS) * ROWS, LANES))
    pair = struct((2, half, LANES))

    key_hbm, value_hbm = (
        pltpu.with_memory_space_constraint(part, pltpu.HBM) for part in (key, value)
    )
    staged = [pltpu.VMEM((tokens, flat), jnp.bfloat16)] * 2 + [pltpu.SemaphoreType.DMA((2, PARTS))]
    keep, send = vmem_call(
        state_kernel, (pair, pair), [pltpu.VMEM((2, 2, half, LANES), jnp.float32), *staged], n_in=2, in_hbm=True,
        flops=2 * tokens * flat * LANES, bytes_accessed=4 * tokens * flat + 8 * half * LANES * 2,
    )(key_hbm, value_hbm)
    hidden, send = lax.optimization_barrier((hidden_pre, send))
    edges = row_edges(hidden)
    came = lax.ppermute(send, "width", SWAP)
    came, edges = lax.optimization_barrier((came, edges))
    mine, other = vmem_call(pick_kernel, (share, share), n_in=2, bytes_accessed=24 * half * LANES)(keep, came)
    came = lax.ppermute(other, "height", SWAP)

    packed = struct((2, per_group, tokens, LANES), jnp.bfloat16)
    query, cotangent, hidden, _ = lax.optimization_barrier((query, cotangent, hidden, mine))
    heads_mine, heads_other, masks = vmem_call(
        heads_kernel,
        (packed, packed, struct((8, LANES))),
        [pltpu.VMEM((2, 2, per_group, tokens, LANES), jnp.bfloat16), *staged,
         pltpu.SMEM(clip_ids.shape, jnp.int32), pltpu.SemaphoreType.DMA],
        n_in=3, in_hbm=True, bytes_accessed=12 * tokens * flat,
    )(*(pltpu.with_memory_space_constraint(part, pltpu.HBM) for part in (query, cotangent, clip_ids)))
    side = side_edge(hidden[0])
    edges, _ = lax.optimization_barrier((edges, heads_other))
    halo = halo_arrays(edges, side)
    _, own = lax.optimization_barrier(((heads_other, side), mine + came))
    heads_sent = lax.ppermute(heads_other, "height", SWAP)

    def along_frames(own, step, meanwhile):
        moves = [[(at, at + step * hop) for at in range(frames) if 0 <= at + step * hop < frames] for hop in (1, 2)]
        near = lax.ppermute(own, "tm", moves[0])
        far = lax.ppermute(own, "tm", moves[1])
        near, far, others = meanwhile(own, near, far)
        at = 0 if step > 0 else 2
        return own + masks[at : at + 1] * near + masks[at + 1 : at + 2] * far, others

    def fetch(own, near, far):
        return lax.optimization_barrier((near, far, heads_sent))

    state, heads_came = along_frames(own, 1, fetch)
    came = lax.ppermute(state, "width", SWAP)
    back = struct((per_group, tokens, LANES), jnp.bfloat16)
    keep, send, back_mine, back_other = vmem_call(
        query_kernel, (share, share, back, back),
        [pltpu.VMEM((2, half, LANES), jnp.float32), pltpu.VMEM((2, half, LANES), jnp.float32)], n_in=4,
        flops=14 * tokens * flat * LANES, bytes_accessed=8 * tokens * flat,
    )(state, came, heads_mine, heads_came)
    came = lax.ppermute(send, "width", SWAP)
    own, halo = lax.optimization_barrier((keep + came, halo))

    def convolve(own, near, far):
        other, _ = lax.optimization_barrier((back_other, own))
        back_came = lax.ppermute(other, "height", SWAP)
        hidden_grad = ffn(hidden_pre, conv_weight, halo)
        query_grad = vmem_call(
            join_kernel, struct((tokens, flat), jnp.bfloat16), n_in=2, bytes_accessed=4 * tokens * flat
        )(back_mine, back_came)
        near, far, hidden_grad = lax.optimization_barrier((near, far, hidden_grad))
        return near, far, (query_grad, hidden_grad)

    total, (query_grad, hidden_grad) = along_frames(own, -1, convolve)
    far = lax.ppermute(total, "height", SWAP)
    near_came = lax.ppermute(total, "width", SWAP)
    state = [pltpu.VMEM((2, half, LANES), jnp.float32)]
    cost = {"flops": 4 * tokens * flat * LANES, "bytes_accessed": 4 * tokens * flat}
    near_grads = vmem_call(functools.partial(key_kernel, True), (back, back), state, n_in=4, **cost)(
        key, value, total, near_came
    )
    far, query_grad = lax.optimization_barrier((far, query_grad))
    far_came = lax.ppermute(far, "width", SWAP)
    out = struct((tokens, flat), jnp.bfloat16)
    key_grad, value_gradient = vmem_call(functools.partial(key_kernel, False), (out, out), state, n_in=6, **cost)(
        key, value, far, far_came, *near_grads
    )
    grads = tuple(part.reshape(queries.shape) for part in (query_grad, key_grad, value_gradient))
    return (*grads, hidden_grad)


def mixed_ffn(hidden_pre, conv_weight):
    row_count = hidden_pre.shape[1]
    col_count = hidden_pre.shape[2]
    split_at = hidden_pre.shape[3] // 2
    widened = padded(hidden_pre, (("height", 1), ("width", 2)), 2)[0]
    conv_out = depthwise(widened, conv_weight, 1, 1, row_count + 2, col_count + 2)
    row_global = lax.axis_index("height") * row_count + jnp.arange(row_count + 2) - 1
    col_global = lax.axis_index("width") * col_count + jnp.arange(col_count + 2) - 1
    row_inside = (row_global >= 0) & (row_global < row_count * lax.axis_size("height"))
    col_inside = (col_global >= 0) & (col_global < col_count * lax.axis_size("width"))
    inside = (row_inside[:, None] & col_inside[None, :]).astype(jnp.float32)
    conv_grad = glu_grad(conv_out, split_at) * inside[:, :, None]
    hidden_grad = depthwise(conv_grad, conv_weight, 1, -1, row_count, col_count)
    hidden_grad = hidden_grad[None].astype(jnp.bfloat16)
    return hidden_grad


TILES = 8
REACH = 2
UNROLL = 8


def conv_kernel(bases, row_refs, *refs):
    halo_rows, refs = refs[:row_refs], refs[row_refs:]
    side_ref, refs = refs[0], refs[1:]
    corners, refs = refs[:row_refs], refs[row_refs:]
    block_ref, weight_ref = refs[:2]
    out_hbm, taps, value_in, gate_in, value_grad, gate_grad, *results, out_ref, sems = refs[-8 - 2 * UNROLL :]
    rows, cols, channels = block_ref.shape
    lane_tiles = channels // LANES // 2
    pitch = -(-lane_tiles // TILES) * TILES
    row, column = lax.axis_index("height"), lax.axis_index("width")
    first_row, last_row = row == 0, row == lax.axis_size("height") - 1
    wide, tall = cols + 2 * REACH, rows + 2 * REACH
    grad_wide = wide - 2

    for base in bases:
        for tile in range(base, min(base + TILES, lane_tiles)):
            for place, source in ((tile, tile), (pitch + tile, lane_tiles + tile)):
                lanes = slice(source * LANES, (source + 1) * LANES)
                taps[pl.ds(place, 9, stride=2 * pitch), :] = weight_ref[:, lanes]

    def source_at(at_row, at_col):
        return pl.multiple_of((at_row * wide + at_col) * TILES, TILES)

    def grad_at(at_row, at_col):
        return pl.multiple_of((at_row * grad_wide + at_col) * TILES, TILES)

    zero = jnp.zeros((TILES, LANES), jnp.float32)
    low_border = jnp.where(first_row, 0, rows + REACH)
    outer_col = jnp.where(column == 0, 0, cols + REACH)
    side_col = jnp.where(column == 0, cols + REACH, 0)
    grad_outer_col = jnp.where(column == 0, 0, grad_wide - 1)
    start_col = jnp.where(column == 0, REACH, REACH - 1)
    low, high = jnp.where(first_row, REACH, REACH - 1), jnp.where(last_row, rows + REACH, rows + REACH + 1)

    for ref in (value_in, gate_in):
        @pl.loop(0, tall)
        def _(at):
            for extra in range(REACH):
                ref[pl.ds(source_at(at, outer_col + extra), TILES), :] = zero

    for ref in (value_grad, gate_grad):
        @pl.loop(0, rows + 2)
        def _(at):
            ref[pl.ds(grad_at(at, grad_outer_col), TILES), :] = zero

        for edge, at in ((first_row, 0), (last_row, rows + 1)):
            @pl.when(edge)
            def _():
                for col in range(grad_wide):
                    ref[pl.ds(grad_at(at, col), TILES), :] = zero

    copies = []
    for base in bases:
        count = min(TILES, lane_tiles - base)

        def spread(load, at_row, at_col, length):
            for ref, offset in ((value_in, base), (gate_in, lane_tiles + base)):
                for tile in range(count):
                    part = load(slice((offset + tile) * LANES, (offset + tile + 1) * LANES)).astype(jnp.float32)
                    ref[pl.ds(source_at(at_row, at_col) + tile, length, stride=TILES), :] = part

        @pl.loop(0, rows)
        def _(at):
            spread(lambda lanes: block_ref[at, :, lanes], at + REACH, REACH, cols)
            spread(lambda lanes: side_ref[at, :, lanes], at + REACH, side_col, REACH)

        for edge, at, which in ((first_row, 0, 0), (last_row, rows + REACH, row_refs - 1)):
            rows_ref, corner_ref = halo_rows[which], corners[which]
            for extra in range(REACH):
                @pl.when(jnp.logical_not(edge))
                def _():
                    spread(lambda lanes: rows_ref[extra, :, lanes], at + extra, REACH, cols)
                    spread(lambda lanes: corner_ref[extra, :, lanes], at + extra, side_col, REACH)

                @pl.when(edge)
                def _():
                    for ref in (value_in, gate_in):
                        for col in range(wide):
                            ref[pl.ds(source_at(at + extra, col), TILES), :] = zero

        def weights(offset):
            return [taps[2 * pitch * tap + offset + base : 2 * pitch * tap + offset + base + TILES, :] for tap in range(9)]

        value_taps, gate_taps = weights(0), weights(pitch)

        @pl.loop(low, high)
        def _(at):
            cache = {}

            def read(ref, a, col):
                if (id(ref), a, col) not in cache:
                    cache[id(ref), a, col] = ref[pl.ds(source_at(at + a, start_col + col), TILES), :]
                return cache[id(ref), a, col]

            for col in range(cols + 1):
                def conv(ref, kernel):
                    total = None
                    for a in (-1, 0, 1):
                        for b in (-1, 0, 1):
                            term = kernel[3 * (a + 1) + b + 1] * read(ref, a, col + b)
                            total = term if total is None else total + term
                    return total

                value, gate = conv(value_in, value_taps), conv(gate_in, gate_taps)
                squash = jax.nn.sigmoid(gate)
                gated = gate * squash
                glu = value * gated
                place = pl.ds(grad_at(at - 1, start_col + col - 1), TILES)
                value_grad[place, :] = glu * gated
                gate_grad[place, :] = glu * value * (squash + gated * (1.0 - squash))

        def gather(at, results):
            cache = {}

            def read(ref, a, col):
                if (id(ref), a, col) not in cache:
                    cache[id(ref), a, col] = ref[pl.ds(grad_at(at + a, col), TILES), :]
                return cache[id(ref), a, col]

            for col in range(cols):
                for ref, kernel, result in zip((value_grad, gate_grad), (value_taps, gate_taps), results):
                    total = None
                    for a in (-1, 0, 1):
                        for b in (-1, 0, 1):
                            term = kernel[3 * (a + 1) + b + 1] * read(ref, 1 - a, col + 1 - b)
                            total = term if total is None else total + term
                    result[pl.ds(col, TILES, stride=cols), :] = total

        def settle(at, results):
            for result, offset in zip(results, (base, lane_tiles + base)):
                for tile in range(count):
                    lanes = slice((offset + tile) * LANES, (offset + tile + 1) * LANES)
                    out_ref[at, :, lanes] = result[tile * cols : (tile + 1) * cols, :].astype(jnp.bfloat16)

        @pl.loop(0, rows // UNROLL)
        def _(at):
            for step in range(UNROLL):
                gather(at * UNROLL + step, results[2 * step : 2 * step + 2])
                if step:
                    settle(at * UNROLL + step - 1, results[2 * step - 2 : 2 * step])
            settle(at * UNROLL + UNROLL - 1, results[2 * UNROLL - 2 :])

        for at, offset in enumerate((base, lane_tiles + base)):
            lanes = pl.ds(offset * LANES, count * LANES)
            copy = pltpu.make_async_copy(out_ref.at[:, :, lanes], out_hbm.at[:, :, lanes], sems.at[at, base // TILES])
            copy.start()
            copies.append(copy)
    for copy in copies:
        copy.wait()


def edge_slice(block, dim, low_side):
    start = jnp.where(low_side, 0, block.shape[dim] - REACH)
    return lax.dynamic_slice_in_dim(block, start, REACH, axis=dim)


def row_edges(hidden_pre):
    block = hidden_pre[0]
    if lax.axis_size("height") == 2:
        return [edge_slice(block, 0, lax.axis_index("height") == 1)]
    return [block[block.shape[0] - REACH :], block[:REACH]]


def side_edge(block):
    return edge_slice(block, 1, lax.axis_index("width") == 1)


def halo_arrays(edges, side):
    height = lax.axis_size("height")
    if height == 2:
        moves = [SWAP]
    else:
        moves = [[(at, at + 1) for at in range(height - 1)], [(at + 1, at) for at in range(height - 1)]]
    halo_rows = [lax.ppermute(edge, "height", move) for edge, move in zip(edges, moves)]
    side = lax.ppermute(side, "width", SWAP)
    corners = [lax.ppermute(side_edge(part), "width", SWAP) for part in halo_rows]
    return halo_rows, side, corners


def conv_part(bases, halo, block, conv_weight, given=()):
    halo_rows, side, corners = halo
    rows, cols, channels = block.shape
    lane_tiles = channels // LANES // 2
    pitch = -(-lane_tiles // TILES) * TILES
    source = pltpu.VMEM(((rows + 2 * REACH) * (cols + 2 * REACH) * TILES, LANES), jnp.float32)
    grad = pltpu.VMEM(((rows + 2) * (cols + 2) * TILES, LANES), jnp.float32)
    result = pltpu.VMEM((cols * TILES, LANES), jnp.float32)
    size = rows * cols * channels
    return vmem_call(
        functools.partial(conv_kernel, bases, len(halo_rows)),
        struct((rows, cols, channels), jnp.bfloat16),
        [pltpu.VMEM((9 * 2 * pitch, LANES), jnp.float32), source, source, grad, grad, *[result] * (2 * UNROLL),
         pltpu.VMEM((rows, cols, channels), jnp.bfloat16), pltpu.SemaphoreType.DMA((2, pitch // TILES))],
        n_in=2 * len(halo_rows) + 3, n_given=len(given), flops=size * len(bases), bytes_accessed=size, vmem_mib=12,
        out_hbm=True,
    )(*halo_rows, side, *corners, block, conv_weight, *given)


def conv_bases(hidden_pre):
    lane_tiles = hidden_pre.shape[3] // LANES // 2
    return list(range(0, lane_tiles, TILES))


def ffn(hidden_pre, conv_weight, halo):
    return conv_part(conv_bases(hidden_pre), halo, hidden_pre[0], conv_weight)[None]


def per_device(queries, attn_keys, attn_values, attn_cotangent, clip_ids, hidden_pre, conv_weight):
    blocked = lax.axis_size("width") == 2 and hidden_pre.shape[0] == 1 and hidden_pre.shape[3] % (2 * LANES) == 0
    pairs = lax.axis_size("height") == 2 and 3 <= lax.axis_size("tm") <= 4 and HEADS % 2 == 0
    if blocked and pairs:
        return paired(queries, attn_keys, attn_values, attn_cotangent, clip_ids, hidden_pre, conv_weight)
    grads = general_attention(queries, attn_keys, attn_values, attn_cotangent, clip_ids)
    if blocked:
        return (*grads, ffn(hidden_pre, conv_weight, halo_arrays(row_edges(hidden_pre), side_edge(hidden_pre[0]))))
    return (*grads, mixed_ffn(hidden_pre, conv_weight))


def solution(mesh):
    return jax.shard_map(
        per_device,
        mesh=mesh,
        in_specs=(
            P(("group", "tm"), "height", "width", None),
            P(("group", "tm"), "height", "width", None),
            P(("group", "tm"), "height", "width", None),
            P(("group", "tm"), "height", "width", None),
            P("group"),
            P(("group", "tm"), "height", "width", None),
            P(),
        ),
        out_specs=(
            P(("group", "tm"), "height", "width", None),
            P(("group", "tm"), "height", "width", None),
            P(("group", "tm"), "height", "width", None),
            P(("group", "tm"), "height", "width", None),
        ),
        check_vma=False,
    )
```

```python
import functools
from functools import reduce

import jax
import jax.numpy as jnp
from jax import lax
from jax.experimental import pallas as pl
from jax.experimental.pallas import tpu as pltpu
from jax.sharding import PartitionSpec as P

HEAD_DIM = 112
HEADS = 10


EPSILON = 1e-06
TOP_PRECISION = lax.Precision.HIGHEST


def entering(value, axis, join, neutral, backward):
    count, mine = (lax.axis_size(axis), lax.axis_index(axis))
    pieces = jax.tree.map(lambda part: lax.all_gather(part, axis), value)
    if backward:
        pieces = jax.tree.map(lambda part: part[::-1], pieces)
        mine = count - 1 - mine
    so_far = jax.tree.map(
        lambda part, zero: jnp.full_like(part, 0) + jnp.asarray(zero, part.dtype), value, neutral
    )

    def turn(position, so_far):
        longer = join(so_far, jax.tree.map(lambda part: part[position], pieces))
        return jax.tree.map(lambda new, old: jnp.where(position < mine, new, old), longer, so_far)

    return lax.fori_loop(0, count - 1, turn, so_far)


def padded(block, sides, width):
    for axis, dim in sides:
        count = lax.axis_size(axis)
        forward = [(i, i + 1) for i in range(count - 1)]
        backward = [(target, source) for source, target in forward]
        low = lax.ppermute(
            lax.slice_in_dim(block, block.shape[dim] - width, None, axis=dim), axis, forward
        )
        high = lax.ppermute(lax.slice_in_dim(block, 0, width, axis=dim), axis, backward)
        block = jnp.concatenate([low, block, high], axis=dim)
    return block


def carry_on(earlier, later):
    keeping = 1.0 - later[0]
    return (
        jnp.maximum(earlier[0], later[0]),
        later[1] + keeping * earlier[1],
        later[2] + keeping * earlier[2],
    )


def clip_flags(clip_ids):
    frame = lax.axis_index("tm")
    frame_count = lax.axis_size("tm")
    current = lax.dynamic_index_in_dim(clip_ids, frame, 0, keepdims=False)
    before = lax.dynamic_index_in_dim(clip_ids, jnp.maximum(frame - 1, 0), 0, keepdims=False)
    after = lax.dynamic_index_in_dim(
        clip_ids, jnp.minimum(frame + 1, frame_count - 1), 0, keepdims=False
    )
    starts = jnp.where((frame == 0) | (current != before), 1.0, 0.0).astype(jnp.float32)
    ends = jnp.where((frame == frame_count - 1) | (current != after), 1.0, 0.0).astype(jnp.float32)
    return (starts, ends)


def glu_grad(conv_out, split_at):
    value_part = conv_out[..., :split_at]
    gate_part = conv_out[..., split_at:]
    squash = jax.nn.sigmoid(gate_part)
    glu = value_part * gate_part * squash
    value_gradient = glu * gate_part * squash
    gate_grad = glu * value_part * squash * (1.0 + gate_part * (1.0 - squash))
    return jnp.concatenate([value_gradient, gate_grad], axis=-1)


def depthwise(source, weights, start, sign, height_out, width_out):
    terms = []
    for offset_row in (-1, 0, 1):
        for offset_col in (-1, 0, 1):
            tap_index = (offset_row + 1) * 3 + offset_col + 1
            row_start = start + sign * offset_row
            col_start = start + sign * offset_col
            window = source[
                row_start : row_start + height_out, col_start : col_start + width_out
            ].astype(jnp.float32)
            terms.append(weights[tap_index] * window)
    return reduce(lambda first, second: first + second, terms)


def general_attention(queries, attn_keys, attn_values, attn_cotangent, clip_ids):
    token_count = queries.shape[1] * queries.shape[2]
    flat_width = HEADS * HEAD_DIM
    starts, ends = clip_flags(clip_ids)
    zero_flag = jnp.zeros((), jnp.float32)
    feature_keys = jnp.maximum(attn_keys, 0).reshape(token_count, HEADS, HEAD_DIM)
    value_row_block = attn_values.reshape(token_count, HEADS, HEAD_DIM)
    local_kv = jnp.einsum(
        "jrf,jrx->rfx", feature_keys, value_row_block, preferred_element_type=jnp.float32
    ).reshape(flat_width, HEAD_DIM)
    local_norm = jnp.sum(feature_keys.astype(jnp.float32), axis=0).reshape(flat_width)
    share_kv, share_norm = (
        lax.psum_scatter(local_kv, ("height", "width"), scatter_dimension=0, tiled=True),
        lax.psum_scatter(local_norm, ("height", "width"), scatter_dimension=0, tiled=True),
    )
    earlier = entering(
        (starts, share_kv, share_norm),
        "tm",
        carry_on,
        (zero_flag, jnp.zeros_like(share_kv), jnp.zeros_like(share_norm)),
        False,
    )
    part_kv = share_kv + (1.0 - starts) * earlier[1]
    part_norm = share_norm + (1.0 - starts) * earlier[2]
    state_key_value, state_norm = (
        lax.all_gather(part_kv, ("height", "width"), axis=0, tiled=True),
        lax.all_gather(part_norm, ("height", "width"), axis=0, tiled=True),
    )
    state_key_value = state_key_value.reshape(HEADS, HEAD_DIM, HEAD_DIM)
    state_norm = state_norm.reshape(HEADS, HEAD_DIM)
    feature_query = (
        jnp.maximum(queries, 0).reshape(token_count, HEADS, HEAD_DIM).astype(jnp.float32)
    )
    cotangent = attn_cotangent.reshape(token_count, HEADS, HEAD_DIM).astype(jnp.float32)
    ratio_numerator = jnp.einsum(
        "cob,obq->coq", feature_query, state_key_value, precision=TOP_PRECISION
    )
    denominator = (
        jnp.einsum("thk,hk->th", feature_query, state_norm, precision=TOP_PRECISION) + EPSILON
    )
    attended = ratio_numerator / denominator[..., None]
    scaled_gradient = cotangent / denominator[..., None]
    denominator_grad = -jnp.sum(cotangent * attended, axis=-1) / denominator
    query_feature_gradient = jnp.einsum(
        "dla,lja->dlj", scaled_gradient, state_key_value, precision=TOP_PRECISION
    )
    query_feature_gradient = query_feature_gradient + state_norm[None] * denominator_grad[..., None]
    query_grad = (
        jnp.where(feature_query > 0.0, query_feature_gradient, 0.0)
        .reshape(queries.shape)
        .astype(jnp.bfloat16)
    )
    gradient_key_value = jnp.einsum(
        "jrf,jrx->rfx", feature_query, scaled_gradient, precision=TOP_PRECISION
    ).reshape(flat_width, HEAD_DIM)
    grad_norm = jnp.einsum(
        "thk,th->hk", feature_query, denominator_grad, precision=TOP_PRECISION
    ).reshape(flat_width)
    share_grad_kv, share_grad_norm = (
        lax.psum_scatter(gradient_key_value, ("height", "width"), scatter_dimension=0, tiled=True),
        lax.psum_scatter(grad_norm, ("height", "width"), scatter_dimension=0, tiled=True),
    )
    later = entering(
        (ends, share_grad_kv, share_grad_norm),
        "tm",
        carry_on,
        (zero_flag, jnp.zeros_like(share_grad_kv), jnp.zeros_like(share_grad_norm)),
        True,
    )
    part_grad_kv = share_grad_kv + (1.0 - ends) * later[1]
    part_grad_norm = share_grad_norm + (1.0 - ends) * later[2]
    total_key_value, norm_total = (
        lax.all_gather(part_grad_kv, ("height", "width"), axis=0, tiled=True),
        lax.all_gather(part_grad_norm, ("height", "width"), axis=0, tiled=True),
    )
    total_key_value = total_key_value.reshape(HEADS, HEAD_DIM, HEAD_DIM)
    norm_total = norm_total.reshape(HEADS, HEAD_DIM)
    key_feat_grad = (
        jnp.einsum(
            "dla,lja->dlj",
            value_row_block.astype(jnp.float32),
            total_key_value,
            precision=TOP_PRECISION,
        )
        + norm_total[None]
    )
    key_grad = (
        jnp.where(feature_keys > 0, key_feat_grad, 0.0)
        .reshape(attn_keys.shape)
        .astype(jnp.bfloat16)
    )
    value_gradient = jnp.einsum(
        "cob,obq->coq", feature_keys.astype(jnp.float32), total_key_value, precision=TOP_PRECISION
    )
    value_gradient = value_gradient.reshape(attn_values.shape).astype(jnp.bfloat16)
    return (query_grad, key_grad, value_gradient)


LANES = 128


def split_terms(value, count=2):
    terms = []
    for _ in range(count):
        terms.append(value.astype(jnp.bfloat16))
        value = value - terms[-1].astype(jnp.float32)
    return terms


def beside(*parts):
    return jnp.concatenate(parts, axis=1)


def dot_tokens(left, right):
    return lax.dot_general(left, right, (((0,), (0,)), ((), ())), preferred_element_type=jnp.float32)


def dot_rows(left, right):
    return lax.dot_general(left, right, (((1,), (0,)), ((), ())), preferred_element_type=jnp.float32)


def dot_columns(left, right):
    return lax.dot_general(left, right, (((1,), (1,)), ((), ())), preferred_element_type=jnp.float32)


def head_slice(ref, head):
    return ref[:, head * HEAD_DIM : (head + 1) * HEAD_DIM]


def tail_block(rows, first):
    column = lax.broadcasted_iota(jnp.int32, (rows, LANES - HEAD_DIM), 1)
    return jnp.where(column == 0, first, 0.0).astype(jnp.bfloat16)


def vmem_call(kernel, out_shape, scratch=(), smem_first=False, n_in=0, flops=0, bytes_accessed=0, vmem_mib=8, in_hbm=False, out_hbm=False, n_given=0):
    vmem = pl.BlockSpec(memory_space=pltpu.VMEM)
    in_specs = [pl.BlockSpec(memory_space=pltpu.HBM) if in_hbm else vmem] * n_in
    in_specs += [pl.BlockSpec(memory_space=pltpu.HBM)] * n_given
    if smem_first:
        in_specs[0] = pl.BlockSpec(memory_space=pltpu.SMEM)
    return pl.pallas_call(
        kernel,
        out_shape=out_shape,
        in_specs=in_specs,
        out_specs=jax.tree.map(lambda _: pl.BlockSpec(memory_space=pltpu.HBM) if out_hbm else vmem, out_shape),
        scratch_shapes=list(scratch),
        input_output_aliases={n_in: 0} if n_given else {},
        cost_estimate=pl.CostEstimate(flops=flops, bytes_accessed=bytes_accessed, transcendentals=0),
        compiler_params=pltpu.CompilerParams(vmem_limit_bytes=vmem_mib << 20),
    )


ROWS = 8
SPARE = LANES - HEAD_DIM
PIECES = HEAD_DIM // SPARE


def packed_tiles(tiles):
    return next(kept for kept in range(tiles + 1) if (tiles - kept) * PIECES - (-tiles // SPARE) <= kept)


def tile_of(at):
    return slice(at * ROWS, (at + 1) * ROWS)


def pack_rows(read, write, tiles):
    kept = packed_tiles(tiles)
    moved = (tiles - kept) * PIECES
    lane = lax.broadcasted_iota(jnp.int32, (ROWS, LANES), 1)
    rows = [read(at) for at in range(tiles)]
    for at in range(kept):
        block = rows[at]
        if at < moved:
            extra, piece = divmod(at, PIECES)
            shifted = pltpu.roll(rows[kept + extra], HEAD_DIM - SPARE * piece, 1)
            block = jnp.where(lane < HEAD_DIM, block, shifted)
        else:
            first = (at - moved) * SPARE
            for step in range(min(SPARE, tiles - first)):
                norm = rows[first + step]
                norm = pltpu.roll(norm, step, 1) if step else norm
                block = jnp.where(lane == HEAD_DIM + step, norm, block)
        write(at, block)


def unpack_rows(read, write, tiles):
    kept = packed_tiles(tiles)
    moved = (tiles - kept) * PIECES
    lane = lax.broadcasted_iota(jnp.int32, (ROWS, LANES), 1)
    rows = [read(at) for at in range(kept)]
    for at in range(tiles):
        if at < kept:
            block = rows[at]
        else:
            for piece in range(PIECES):
                shifted = pltpu.roll(rows[(at - kept) * PIECES + piece], SPARE * (piece + 1), 1)
                block = shifted if piece == 0 else jnp.where(lane < SPARE * piece, block, shifted)
        group, step = divmod(at, SPARE)
        norm = rows[moved + group]
        norm = pltpu.roll(norm, LANES - step, 1) if step else norm
        write(at, jnp.where(lane == HEAD_DIM, norm, block))


def store_into(ref, *index):
    def write(at, block):
        ref[(*index, tile_of(at))] = block

    return write


def unpack_into(state, index, packed):
    unpack_rows(lambda at: packed[tile_of(at)], store_into(state, index), state.shape[1] // ROWS)


PARTS = 4


def stage(sources, targets, sems):
    copies = []
    for at, (source, target) in enumerate(zip(sources, targets)):
        rows = source.shape[0] // PARTS
        for part in range(PARTS):
            span = pl.ds(part * rows, rows)
            copies.append(pltpu.make_async_copy(source.at[span], target.at[span], sems.at[at, part]))
    for copy in copies:
        copy.start()
    for copy in copies:
        copy.wait()


def state_kernel(key_hbm, value_hbm, keep_ref, send_ref, halves, key_ref, value_ref, sems):
    stage((key_hbm, value_hbm), (key_ref, value_ref), sems)
    tokens = key_ref.shape[0]
    one = tail_block(tokens, 1.0)
    half = halves.shape[2]
    per_group = HEADS // 2
    column = lax.axis_index("width")
    blocks = []
    for head in range(HEADS):
        feature = jnp.maximum(head_slice(key_ref, head), 0)
        wide = jnp.concatenate([head_slice(value_ref, head), one], axis=1)
        blocks.append(dot_tokens(feature, wide))
    for head in range(HEADS):
        group, place = divmod(head, per_group)
        store_rows(halves, group, place * HEAD_DIM, blocks[head], half)
    keep_ref[...] = halves[column]
    send_ref[...] = halves[1 - column]


def store_rows(halves, group, first, block, half):
    cut = min(max(half - first, 0), HEAD_DIM)
    if cut:
        index = (0, group) if group is not None else (0,)
        halves[(*index, slice(first, first + cut))] = block[:cut]
    if cut < HEAD_DIM:
        index = (1, group) if group is not None else (1,)
        start = first + cut - half
        halves[(*index, slice(start, start + HEAD_DIM - cut))] = block[cut:]


def pick_kernel(keep_ref, came_ref, mine_ref, other_ref):
    row = lax.axis_index("height")
    tiles = keep_ref.shape[1] // ROWS
    for out, at_row in ((mine_ref, row), (other_ref, 1 - row)):
        pack_rows(lambda at: keep_ref[at_row, tile_of(at)] + came_ref[at_row, tile_of(at)], store_into(out), tiles)


def write_masks(clip_ref, out_ref):
    frame = lax.axis_index("tm")
    last = lax.axis_size("tm") - 1
    here = clip_ref[frame]
    line = lax.broadcasted_iota(jnp.int32, out_ref.shape, 0)
    masks = jnp.zeros(out_ref.shape, jnp.float32)
    for at, (step, hop) in enumerate(((1, 1), (1, 2), (-1, 1), (-1, 2))):
        other = frame - step * hop
        inside = (other >= 0) & (other <= last)
        same = inside & (clip_ref[jnp.clip(other, 0, last)] == here)
        masks = jnp.where(line == at, jnp.where(same, 1.0, 0.0), masks)
    out_ref[...] = masks


def heads_kernel(query_hbm, cotangent_hbm, clip_hbm, mine_ref, other_ref, mask_ref, groups, query_ref, cotangent_ref, sems, clip_ref, clip_sem):
    clip_copy = pltpu.make_async_copy(clip_hbm, clip_ref, clip_sem)
    clip_copy.start()
    stage((query_hbm, cotangent_hbm), (query_ref, cotangent_ref), sems)
    clip_copy.wait()
    write_masks(clip_ref, mask_ref)
    none = tail_block(query_ref.shape[0], 0.0)
    per_group = HEADS // 2
    row = lax.axis_index("height")
    for head in range(HEADS):
        group, place = divmod(head, per_group)
        feature = jnp.maximum(head_slice(query_ref, head), 0)
        groups[group, 0, place] = jnp.concatenate([feature, none], axis=1)
        groups[group, 1, place] = jnp.concatenate([head_slice(cotangent_ref, head), none], axis=1)
    mine_ref[...] = groups[row]
    other_ref[...] = groups[1 - row]


def query_kernel(state_ref, came_ref, mine_ref, other_ref, keep_ref, send_ref, own_out, other_out, state, halves):
    column = lax.axis_index("width")
    half = state.shape[1]
    per_group = HEADS // 2
    tokens = mine_ref.shape[2]
    unpack_into(state, column, state_ref)
    unpack_into(state, 1 - column, came_ref)
    lane = lax.broadcasted_iota(jnp.int32, (2 * tokens, LANES), 1)
    places = range(per_group)
    features, cots, states, products = [], [], [], []
    pad = jnp.zeros((LANES - HEAD_DIM, LANES), jnp.bfloat16)
    for place in places:
        full = jnp.concatenate([mine_ref[0, place], other_ref[0, place]], axis=0)
        features.append(full[:, :HEAD_DIM])
        cots.append(jnp.concatenate([mine_ref[1, place], other_ref[1, place]], axis=0))
        high, low, rest = split_terms(load_rows(state, place * HEAD_DIM, half), 3)
        states.append((high, low, rest))
        product = dot_rows(beside(full, full), jnp.concatenate([high, pad, low, pad], axis=0))
        products.append(product + dot_rows(features[-1], rest))
    scaleds = []
    for place in places:
        cotangent = cots[place].astype(jnp.float32)
        product = products[place]
        inverse = 1.0 / (product[:, HEAD_DIM : HEAD_DIM + 1] + EPSILON)
        against = jnp.sum(cotangent * product, axis=1, keepdims=True)
        norm_grad = -(against * inverse) * inverse
        scaleds.append(split_terms(jnp.where(lane == HEAD_DIM, norm_grad, cotangent * inverse), 3))
    for place in places:
        both = dot_tokens(features[place], beside(*scaleds[place][:2]))
        store_rows(halves, None, place * HEAD_DIM, both[:, :LANES] + both[:, LANES:], half)
    for place in places:
        narrow, (high, low, rest) = features[place], states[place]
        first, second, third = scaleds[place]
        back = dot_columns(beside(first, third), beside(rest, high))
        back = back + dot_columns(beside(second, second), beside(high, low))
        back = back + dot_columns(beside(first, first), beside(high, low))
        back = jnp.where(narrow > 0, back, 0.0).astype(jnp.bfloat16)
        own_out[place, :, :HEAD_DIM] = back[:tokens]
        other_out[place, :, :HEAD_DIM] = back[tokens:]
    for out, part in ((keep_ref, column), (send_ref, 1 - column)):
        pack_rows(lambda at: halves[part, tile_of(at)], store_into(out), half // ROWS)


def load_rows(state, first, half):
    cut = min(max(half - first, 0), HEAD_DIM)
    parts = []
    if cut:
        parts.append(state[0, first : first + cut])
    if cut < HEAD_DIM:
        start = first + cut - half
        parts.append(state[1, start : start + HEAD_DIM - cut])
    return parts[0] if len(parts) == 1 else jnp.concatenate(parts, axis=0)


def key_heads(key_ref, value_ref, total, half, group, place, one):
    head = group * (HEADS // 2) + place
    feature = jnp.maximum(head_slice(key_ref, head), 0)
    wide = jnp.concatenate([head_slice(value_ref, head), one], axis=1)
    high, low = split_terms(load_rows(total, place * HEAD_DIM, half))
    grad = dot_columns(beside(wide, wide), beside(high, low))
    product = dot_rows(feature, high) + dot_rows(feature, low)
    return jnp.where(feature > 0, grad, 0.0).astype(jnp.bfloat16), product[:, :HEAD_DIM].astype(jnp.bfloat16)


def key_kernel(mine, key_ref, value_ref, here_ref, came_ref, *refs):
    column, row = lax.axis_index("width"), lax.axis_index("height")
    given, (key_out, value_out, total) = refs[:-3], refs[-3:]
    half = total.shape[1]
    unpack_into(total, column, here_ref)
    unpack_into(total, 1 - column, came_ref)
    one = tail_block(key_ref.shape[0], 1.0)
    for group in range(2):
        @pl.when(row == (group if mine else 1 - group))
        def _():
            places = range(HEADS // 2)
            grads = [key_heads(key_ref, value_ref, total, half, group, place, one) for place in places]
            for place in places:
                for at, out in enumerate((key_out, value_out)):
                    if mine:
                        out[place, :, :HEAD_DIM] = grads[place][at]
                        continue
                    for which, part in ((group, grads[place][at]), (1 - group, given[at][place, :, :HEAD_DIM])):
                        first = (which * (HEADS // 2) + place) * HEAD_DIM
                        out[:, first : first + HEAD_DIM] = part


def join_kernel(mine_ref, came_ref, out_ref):
    row = lax.axis_index("height")
    per_group = HEADS // 2
    for place in range(per_group):
        mine, came = mine_ref[place, :, :HEAD_DIM], came_ref[place, :, :HEAD_DIM]
        first = jnp.where(row == 0, mine, came)
        second = jnp.where(row == 0, came, mine)
        out_ref[:, place * HEAD_DIM : (place + 1) * HEAD_DIM] = first
        at = (per_group + place) * HEAD_DIM
        out_ref[:, at : at + HEAD_DIM] = second


def struct(shape, dtype=jnp.float32):
    return jax.ShapeDtypeStruct(shape, dtype)


SWAP = [(0, 1), (1, 0)]


def paired(queries, attn_keys, attn_values, attn_cotangent, clip_ids, hidden_pre, conv_weight):
    tokens = queries.shape[1] * queries.shape[2]
    flat = HEADS * HEAD_DIM
    per_group = HEADS // 2
    half = per_group * HEAD_DIM // 2
    frames = lax.axis_size("tm")
    query, key, value, cotangent = (
        part.reshape(tokens, flat) for part in (queries, attn_keys, attn_values, attn_cotangent)
    )
    share = struct((packed_tiles(half // ROWS) * ROWS, LANES))
    pair = struct((2, half, LANES))

    key_hbm, value_hbm = (
        pltpu.with_memory_space_constraint(part, pltpu.HBM) for part in (key, value)
    )
    staged = [pltpu.VMEM((tokens, flat), jnp.bfloat16)] * 2 + [pltpu.SemaphoreType.DMA((2, PARTS))]
    keep, send = vmem_call(
        state_kernel, (pair, pair), [pltpu.VMEM((2, 2, half, LANES), jnp.float32), *staged], n_in=2, in_hbm=True,
        flops=2 * tokens * flat * LANES, bytes_accessed=4 * tokens * flat + 8 * half * LANES * 2,
    )(key_hbm, value_hbm)
    hidden, send = lax.optimization_barrier((hidden_pre, send))
    edges = row_edges(hidden)
    came = lax.ppermute(send, "width", SWAP)
    came, edges = lax.optimization_barrier((came, edges))
    mine, other = vmem_call(pick_kernel, (share, share), n_in=2, bytes_accessed=24 * half * LANES)(keep, came)
    came = lax.ppermute(other, "height", SWAP)

    packed = struct((2, per_group, tokens, LANES), jnp.bfloat16)
    query, cotangent, hidden, _ = lax.optimization_barrier((query, cotangent, hidden, mine))
    heads_mine, heads_other, masks = vmem_call(
        heads_kernel,
        (packed, packed, struct((8, LANES))),
        [pltpu.VMEM((2, 2, per_group, tokens, LANES), jnp.bfloat16), *staged,
         pltpu.SMEM(clip_ids.shape, jnp.int32), pltpu.SemaphoreType.DMA],
        n_in=3, in_hbm=True, bytes_accessed=12 * tokens * flat,
    )(*(pltpu.with_memory_space_constraint(part, pltpu.HBM) for part in (query, cotangent, clip_ids)))
    side = side_edge(hidden[0])
    edges, _ = lax.optimization_barrier((edges, heads_other))
    halo = halo_arrays(edges, side)
    _, own = lax.optimization_barrier(((heads_other, side), mine + came))
    heads_sent = lax.ppermute(heads_other, "height", SWAP)

    def along_frames(own, step, meanwhile):
        moves = [[(at, at + step * hop) for at in range(frames) if 0 <= at + step * hop < frames] for hop in (1, 2)]
        hops = (1, 2) if step > 0 else (2, 1)
        sent = {hop: lax.ppermute(own, "tm", moves[hop - 1]) for hop in hops}
        near, far = sent[1], sent[2]
        near, far, others = meanwhile(own, near, far)
        at = 0 if step > 0 else 2
        return own + masks[at : at + 1] * near + masks[at + 1 : at + 2] * far, others

    def fetch(own, near, far):
        block, _ = lax.optimization_barrier((hidden_pre[0], own))
        near, far, kept = lax.optimization_barrier((near, far, (heads_sent, spread_block(block, conv_weight))))
        return near, far, kept

    state, (heads_came, spread_out) = along_frames(own, 1, fetch)
    came = lax.ppermute(state, "width", SWAP)
    back = struct((per_group, tokens, LANES), jnp.bfloat16)
    keep, send, back_mine, back_other = vmem_call(
        query_kernel, (share, share, back, back),
        [pltpu.VMEM((2, half, LANES), jnp.float32), pltpu.VMEM((2, half, LANES), jnp.float32)], n_in=4,
        flops=14 * tokens * flat * LANES, bytes_accessed=8 * tokens * flat,
    )(state, came, heads_mine, heads_came)
    came = lax.ppermute(send, "width", SWAP)
    own, halo = lax.optimization_barrier((keep + came, halo))

    def convolve(own, near, far):
        other, _ = lax.optimization_barrier((back_other, own))
        back_came = lax.ppermute(other, "height", SWAP)
        hidden_grad = ffn(hidden_pre, halo, spread_out)
        query_grad = vmem_call(
            join_kernel, struct((tokens, flat), jnp.bfloat16), n_in=2, bytes_accessed=4 * tokens * flat
        )(back_mine, back_came)
        far, near, hidden_grad = lax.optimization_barrier((far, near, hidden_grad))
        return near, far, (query_grad, hidden_grad)

    total, (query_grad, hidden_grad) = along_frames(own, -1, convolve)
    far = lax.ppermute(total, "height", SWAP)
    near_came = lax.ppermute(total, "width", SWAP)
    state = [pltpu.VMEM((2, half, LANES), jnp.float32)]
    cost = {"flops": 4 * tokens * flat * LANES, "bytes_accessed": 4 * tokens * flat}
    near_grads = vmem_call(functools.partial(key_kernel, True), (back, back), state, n_in=4, **cost)(
        key, value, total, near_came
    )
    far, query_grad = lax.optimization_barrier((far, query_grad))
    far_came = lax.ppermute(far, "width", SWAP)
    out = struct((tokens, flat), jnp.bfloat16)
    key_grad, value_gradient = vmem_call(functools.partial(key_kernel, False), (out, out), state, n_in=6, **cost)(
        key, value, far, far_came, *near_grads
    )
    grads = tuple(part.reshape(queries.shape) for part in (query_grad, key_grad, value_gradient))
    return (*grads, hidden_grad)


def mixed_ffn(hidden_pre, conv_weight):
    row_count = hidden_pre.shape[1]
    col_count = hidden_pre.shape[2]
    split_at = hidden_pre.shape[3] // 2
    widened = padded(hidden_pre, (("height", 1), ("width", 2)), 2)[0]
    conv_out = depthwise(widened, conv_weight, 1, 1, row_count + 2, col_count + 2)
    row_global = lax.axis_index("height") * row_count + jnp.arange(row_count + 2) - 1
    col_global = lax.axis_index("width") * col_count + jnp.arange(col_count + 2) - 1
    row_inside = (row_global >= 0) & (row_global < row_count * lax.axis_size("height"))
    col_inside = (col_global >= 0) & (col_global < col_count * lax.axis_size("width"))
    inside = (row_inside[:, None] & col_inside[None, :]).astype(jnp.float32)
    conv_grad = glu_grad(conv_out, split_at) * inside[:, :, None]
    hidden_grad = depthwise(conv_grad, conv_weight, 1, -1, row_count, col_count)
    hidden_grad = hidden_grad[None].astype(jnp.bfloat16)
    return hidden_grad


TILES = 8
REACH = 2
UNROLL = 8


def spread(load, refs, offsets, count, start, length):
    for ref, offset in zip(refs, offsets):
        for tile in range(count):
            part = load(slice((offset + tile) * LANES, (offset + tile + 1) * LANES)).astype(jnp.float32)
            ref[pl.ds(start + tile, length, stride=TILES), :] = part


def spread_kernel(block_ref, weight_ref, source, taps):
    rows, cols, channels = block_ref.shape
    lane_tiles = channels // LANES // 2
    pitch = -(-lane_tiles // TILES) * TILES
    wide = cols + 2 * REACH
    for tile in range(lane_tiles):
        for place, at in ((tile, tile), (pitch + tile, lane_tiles + tile)):
            taps[pl.ds(place, 9, stride=2 * pitch), :] = weight_ref[:, at * LANES : (at + 1) * LANES]

    @pl.loop(0, rows)
    def _(at):
        start = pl.multiple_of(((at + REACH) * wide + REACH) * TILES, TILES)
        for base in range(0, lane_tiles, TILES):
            refs = source.at[base // TILES, 0], source.at[base // TILES, 1]
            count = min(TILES, lane_tiles - base)
            spread(lambda lanes: block_ref[at, :, lanes], refs, (base, lane_tiles + base), count, start, cols)


def conv_kernel(row_refs, *refs):
    halo_rows, refs = refs[:row_refs], refs[row_refs:]
    side_ref, refs = refs[0], refs[1:]
    corners, refs = refs[:row_refs], refs[row_refs:]
    _, taps, out_hbm, source, value_grad, gate_grad, *results, out_ref, sems = refs
    rows, cols, channels = out_ref.shape
    lane_tiles = channels // LANES // 2
    pitch = -(-lane_tiles // TILES) * TILES
    row, column = lax.axis_index("height"), lax.axis_index("width")
    first_row, last_row = row == 0, row == lax.axis_size("height") - 1
    wide, tall = cols + 2 * REACH, rows + 2 * REACH
    grad_wide = wide - 2

    def source_at(at_row, at_col):
        return pl.multiple_of((at_row * wide + at_col) * TILES, TILES)

    def grad_at(at_row, at_col):
        return pl.multiple_of((at_row * grad_wide + at_col) * TILES, TILES)

    zero = jnp.zeros((TILES, LANES), jnp.float32)
    outer_col = jnp.where(column == 0, 0, cols + REACH)
    side_col = jnp.where(column == 0, cols + REACH, 0)
    grad_outer_col = jnp.where(column == 0, 0, grad_wide - 1)
    start_col = jnp.where(column == 0, REACH, REACH - 1)
    low, high = jnp.where(first_row, REACH, REACH - 1), jnp.where(last_row, rows + REACH, rows + REACH + 1)

    for ref in (value_grad, gate_grad):
        @pl.loop(0, rows + 2)
        def _(at):
            ref[pl.ds(grad_at(at, grad_outer_col), TILES), :] = zero

        for edge, at in ((first_row, 0), (last_row, rows + 1)):
            @pl.when(edge)
            def _():
                for col in range(grad_wide):
                    ref[pl.ds(grad_at(at, col), TILES), :] = zero

    copies = []
    for base in range(0, lane_tiles, TILES):
        count = min(TILES, lane_tiles - base)
        value_in, gate_in = source.at[base // TILES, 0], source.at[base // TILES, 1]
        offsets = base, lane_tiles + base

        @pl.loop(0, rows)
        def _(at):
            spread(
                lambda lanes: side_ref[at, :, lanes], (value_in, gate_in), offsets, count,
                source_at(at + REACH, side_col), REACH,
            )
            for ref in (value_in, gate_in):
                for extra in range(REACH):
                    ref[pl.ds(source_at(at + REACH, outer_col + extra), TILES), :] = zero

        for edge, at, which in ((first_row, 0, 0), (last_row, rows + REACH, row_refs - 1)):
            rows_ref, corner_ref = halo_rows[which], corners[which]
            for extra in range(REACH):
                @pl.when(jnp.logical_not(edge))
                def _():
                    for ref, col, length in ((rows_ref, REACH, cols), (corner_ref, side_col, REACH)):
                        spread(
                            lambda lanes: ref[extra, :, lanes], (value_in, gate_in), offsets, count,
                            source_at(at + extra, col), length,
                        )
                    for ref in (value_in, gate_in):
                        for side in range(REACH):
                            ref[pl.ds(source_at(at + extra, outer_col + side), TILES), :] = zero

                @pl.when(edge)
                def _():
                    for ref in (value_in, gate_in):
                        for col in range(wide):
                            ref[pl.ds(source_at(at + extra, col), TILES), :] = zero

        def weights(offset):
            return [taps[2 * pitch * tap + offset + base : 2 * pitch * tap + offset + base + TILES, :] for tap in range(9)]

        value_taps, gate_taps = weights(0), weights(pitch)

        @pl.loop(low, high)
        def _(at):
            cache = {}

            def read(ref, a, col):
                if (id(ref), a, col) not in cache:
                    cache[id(ref), a, col] = ref[pl.ds(source_at(at + a, start_col + col), TILES), :]
                return cache[id(ref), a, col]

            for col in range(cols + 1):
                def conv(ref, kernel):
                    total = None
                    for a in (-1, 0, 1):
                        for b in (-1, 0, 1):
                            term = kernel[3 * (a + 1) + b + 1] * read(ref, a, col + b)
                            total = term if total is None else total + term
                    return total

                value, gate = conv(value_in, value_taps), conv(gate_in, gate_taps)
                squash = jax.nn.sigmoid(gate)
                gated = gate * squash
                glu = value * gated
                place = pl.ds(grad_at(at - 1, start_col + col - 1), TILES)
                value_grad[place, :] = glu * gated
                gate_grad[place, :] = glu * value * (squash + gated * (1.0 - squash))

        def gather(at, results):
            cache = {}

            def read(ref, a, col):
                if (id(ref), a, col) not in cache:
                    cache[id(ref), a, col] = ref[pl.ds(grad_at(at + a, col), TILES), :]
                return cache[id(ref), a, col]

            for col in range(cols):
                for ref, kernel, result in zip((value_grad, gate_grad), (value_taps, gate_taps), results):
                    total = None
                    for a in (-1, 0, 1):
                        for b in (-1, 0, 1):
                            term = kernel[3 * (a + 1) + b + 1] * read(ref, 1 - a, col + 1 - b)
                            total = term if total is None else total + term
                    result[pl.ds(col, TILES, stride=cols), :] = total

        def settle(at, results):
            for result, offset in zip(results, (base, lane_tiles + base)):
                for tile in range(count):
                    lanes = slice((offset + tile) * LANES, (offset + tile + 1) * LANES)
                    out_ref[at, :, lanes] = result[tile * cols : (tile + 1) * cols, :].astype(jnp.bfloat16)

        @pl.loop(0, rows // UNROLL)
        def _(at):
            for step in range(UNROLL):
                gather(at * UNROLL + step, results[2 * step : 2 * step + 2])
                if step:
                    settle(at * UNROLL + step - 1, results[2 * step - 2 : 2 * step])
            settle(at * UNROLL + UNROLL - 1, results[2 * UNROLL - 2 :])

        for at, offset in enumerate((base, lane_tiles + base)):
            lanes = pl.ds(offset * LANES, count * LANES)
            copy = pltpu.make_async_copy(out_ref.at[:, :, lanes], out_hbm.at[:, :, lanes], sems.at[at, base // TILES])
            copy.start()
            copies.append(copy)
    for copy in copies:
        copy.wait()


def edge_slice(block, dim, low_side):
    start = jnp.where(low_side, 0, block.shape[dim] - REACH)
    return lax.dynamic_slice_in_dim(block, start, REACH, axis=dim)


def row_edges(hidden_pre):
    block = hidden_pre[0]
    if lax.axis_size("height") == 2:
        return [edge_slice(block, 0, lax.axis_index("height") == 1)]
    return [block[block.shape[0] - REACH :], block[:REACH]]


def side_edge(block):
    return edge_slice(block, 1, lax.axis_index("width") == 1)


def halo_arrays(edges, side):
    height = lax.axis_size("height")
    if height == 2:
        moves = [SWAP]
    else:
        moves = [[(at, at + 1) for at in range(height - 1)], [(at + 1, at) for at in range(height - 1)]]
    halo_rows = [lax.ppermute(edge, "height", move) for edge, move in zip(edges, moves)]
    side = lax.ppermute(side, "width", SWAP)
    corners = [lax.ppermute(side_edge(part), "width", SWAP) for part in halo_rows]
    return halo_rows, side, corners


def spread_block(block, conv_weight):
    rows, cols, channels = block.shape
    chunks = -(-channels // LANES // 2 // TILES)
    size = (rows + 2 * REACH) * (cols + 2 * REACH) * TILES
    return vmem_call(
        spread_kernel,
        (struct((chunks, 2, size, LANES)), struct((9 * 2 * chunks * TILES, LANES))),
        n_in=2, flops=rows * cols * channels, bytes_accessed=rows * cols * channels,
    )(block, conv_weight)


def ffn(hidden_pre, halo, spread_out):
    halo_rows, side, corners = halo
    rows, cols, channels = hidden_pre.shape[1:]
    source, taps = spread_out
    chunks = source.shape[0]
    vmem, hbm = pl.BlockSpec(memory_space=pltpu.VMEM), pl.BlockSpec(memory_space=pltpu.HBM)
    grad = pltpu.VMEM(((rows + 2) * (cols + 2) * TILES, LANES), jnp.float32)
    result = pltpu.VMEM((cols * TILES, LANES), jnp.float32)
    size = rows * cols * channels
    hidden_grad, _ = pl.pallas_call(
        functools.partial(conv_kernel, len(halo_rows)),
        out_shape=(struct((rows, cols, channels), jnp.bfloat16), struct(source.shape)),
        in_specs=[vmem] * (2 * len(halo_rows) + 3),
        out_specs=(hbm, vmem),
        scratch_shapes=[
            grad, grad, *[result] * (2 * UNROLL),
            pltpu.VMEM((rows, cols, channels), jnp.bfloat16), pltpu.SemaphoreType.DMA((2, chunks)),
        ],
        input_output_aliases={2 * len(halo_rows) + 1: 1},
        cost_estimate=pl.CostEstimate(flops=2 * size, bytes_accessed=size, transcendentals=0),
        compiler_params=pltpu.CompilerParams(vmem_limit_bytes=8 << 20),
    )(*halo_rows, side, *corners, source, taps)
    return hidden_grad[None]


def per_device(queries, attn_keys, attn_values, attn_cotangent, clip_ids, hidden_pre, conv_weight):
    blocked = lax.axis_size("width") == 2 and hidden_pre.shape[0] == 1 and hidden_pre.shape[3] % (2 * LANES) == 0
    pairs = lax.axis_size("height") == 2 and 3 <= lax.axis_size("tm") <= 4 and HEADS % 2 == 0
    if blocked and pairs:
        return paired(queries, attn_keys, attn_values, attn_cotangent, clip_ids, hidden_pre, conv_weight)
    grads = general_attention(queries, attn_keys, attn_values, attn_cotangent, clip_ids)
    if blocked:
        halo = halo_arrays(row_edges(hidden_pre), side_edge(hidden_pre[0]))
        return (*grads, ffn(hidden_pre, halo, spread_block(hidden_pre[0], conv_weight)))
    return (*grads, mixed_ffn(hidden_pre, conv_weight))


def solution(mesh):
    return jax.shard_map(
        per_device,
        mesh=mesh,
        in_specs=(
            P(("group", "tm"), "height", "width", None),
            P(("group", "tm"), "height", "width", None),
            P(("group", "tm"), "height", "width", None),
            P(("group", "tm"), "height", "width", None),
            P("group"),
            P(("group", "tm"), "height", "width", None),
            P(),
        ),
        out_specs=(
            P(("group", "tm"), "height", "width", None),
            P(("group", "tm"), "height", "width", None),
            P(("group", "tm"), "height", "width", None),
            P(("group", "tm"), "height", "width", None),
        ),
        check_vma=False,
    )
```

```python
import functools
from functools import reduce

import jax
import jax.numpy as jnp
from jax import lax
from jax.experimental import pallas as pl
from jax.experimental.pallas import tpu as pltpu
from jax.sharding import PartitionSpec as P

HEAD_DIM = 112
HEADS = 10


EPSILON = 1e-06
TOP_PRECISION = lax.Precision.HIGHEST


def entering(value, axis, join, neutral, backward):
    count, mine = (lax.axis_size(axis), lax.axis_index(axis))
    pieces = jax.tree.map(lambda part: lax.all_gather(part, axis), value)
    if backward:
        pieces = jax.tree.map(lambda part: part[::-1], pieces)
        mine = count - 1 - mine
    so_far = jax.tree.map(
        lambda part, zero: jnp.full_like(part, 0) + jnp.asarray(zero, part.dtype), value, neutral
    )

    def turn(position, so_far):
        longer = join(so_far, jax.tree.map(lambda part: part[position], pieces))
        return jax.tree.map(lambda new, old: jnp.where(position < mine, new, old), longer, so_far)

    return lax.fori_loop(0, count - 1, turn, so_far)


def padded(block, sides, width):
    for axis, dim in sides:
        count = lax.axis_size(axis)
        forward = [(i, i + 1) for i in range(count - 1)]
        backward = [(target, source) for source, target in forward]
        low = lax.ppermute(
            lax.slice_in_dim(block, block.shape[dim] - width, None, axis=dim), axis, forward
        )
        high = lax.ppermute(lax.slice_in_dim(block, 0, width, axis=dim), axis, backward)
        block = jnp.concatenate([low, block, high], axis=dim)
    return block


def carry_on(earlier, later):
    keeping = 1.0 - later[0]
    return (
        jnp.maximum(earlier[0], later[0]),
        later[1] + keeping * earlier[1],
        later[2] + keeping * earlier[2],
    )


def clip_flags(clip_ids):
    frame = lax.axis_index("tm")
    frame_count = lax.axis_size("tm")
    current = lax.dynamic_index_in_dim(clip_ids, frame, 0, keepdims=False)
    before = lax.dynamic_index_in_dim(clip_ids, jnp.maximum(frame - 1, 0), 0, keepdims=False)
    after = lax.dynamic_index_in_dim(
        clip_ids, jnp.minimum(frame + 1, frame_count - 1), 0, keepdims=False
    )
    starts = jnp.where((frame == 0) | (current != before), 1.0, 0.0).astype(jnp.float32)
    ends = jnp.where((frame == frame_count - 1) | (current != after), 1.0, 0.0).astype(jnp.float32)
    return (starts, ends)


def glu_grad(conv_out, split_at):
    value_part = conv_out[..., :split_at]
    gate_part = conv_out[..., split_at:]
    squash = jax.nn.sigmoid(gate_part)
    glu = value_part * gate_part * squash
    value_gradient = glu * gate_part * squash
    gate_grad = glu * value_part * squash * (1.0 + gate_part * (1.0 - squash))
    return jnp.concatenate([value_gradient, gate_grad], axis=-1)


def depthwise(source, weights, start, sign, height_out, width_out):
    terms = []
    for offset_row in (-1, 0, 1):
        for offset_col in (-1, 0, 1):
            tap_index = (offset_row + 1) * 3 + offset_col + 1
            row_start = start + sign * offset_row
            col_start = start + sign * offset_col
            window = source[
                row_start : row_start + height_out, col_start : col_start + width_out
            ].astype(jnp.float32)
            terms.append(weights[tap_index] * window)
    return reduce(lambda first, second: first + second, terms)


def general_attention(queries, attn_keys, attn_values, attn_cotangent, clip_ids):
    token_count = queries.shape[1] * queries.shape[2]
    flat_width = HEADS * HEAD_DIM
    starts, ends = clip_flags(clip_ids)
    zero_flag = jnp.zeros((), jnp.float32)
    feature_keys = jnp.maximum(attn_keys, 0).reshape(token_count, HEADS, HEAD_DIM)
    value_row_block = attn_values.reshape(token_count, HEADS, HEAD_DIM)
    local_kv = jnp.einsum(
        "jrf,jrx->rfx", feature_keys, value_row_block, preferred_element_type=jnp.float32
    ).reshape(flat_width, HEAD_DIM)
    local_norm = jnp.sum(feature_keys.astype(jnp.float32), axis=0).reshape(flat_width)
    share_kv, share_norm = (
        lax.psum_scatter(local_kv, ("height", "width"), scatter_dimension=0, tiled=True),
        lax.psum_scatter(local_norm, ("height", "width"), scatter_dimension=0, tiled=True),
    )
    earlier = entering(
        (starts, share_kv, share_norm),
        "tm",
        carry_on,
        (zero_flag, jnp.zeros_like(share_kv), jnp.zeros_like(share_norm)),
        False,
    )
    part_kv = share_kv + (1.0 - starts) * earlier[1]
    part_norm = share_norm + (1.0 - starts) * earlier[2]
    state_key_value, state_norm = (
        lax.all_gather(part_kv, ("height", "width"), axis=0, tiled=True),
        lax.all_gather(part_norm, ("height", "width"), axis=0, tiled=True),
    )
    state_key_value = state_key_value.reshape(HEADS, HEAD_DIM, HEAD_DIM)
    state_norm = state_norm.reshape(HEADS, HEAD_DIM)
    feature_query = (
        jnp.maximum(queries, 0).reshape(token_count, HEADS, HEAD_DIM).astype(jnp.float32)
    )
    cotangent = attn_cotangent.reshape(token_count, HEADS, HEAD_DIM).astype(jnp.float32)
    ratio_numerator = jnp.einsum(
        "cob,obq->coq", feature_query, state_key_value, precision=TOP_PRECISION
    )
    denominator = (
        jnp.einsum("thk,hk->th", feature_query, state_norm, precision=TOP_PRECISION) + EPSILON
    )
    attended = ratio_numerator / denominator[..., None]
    scaled_gradient = cotangent / denominator[..., None]
    denominator_grad = -jnp.sum(cotangent * attended, axis=-1) / denominator
    query_feature_gradient = jnp.einsum(
        "dla,lja->dlj", scaled_gradient, state_key_value, precision=TOP_PRECISION
    )
    query_feature_gradient = query_feature_gradient + state_norm[None] * denominator_grad[..., None]
    query_grad = (
        jnp.where(feature_query > 0.0, query_feature_gradient, 0.0)
        .reshape(queries.shape)
        .astype(jnp.bfloat16)
    )
    gradient_key_value = jnp.einsum(
        "jrf,jrx->rfx", feature_query, scaled_gradient, precision=TOP_PRECISION
    ).reshape(flat_width, HEAD_DIM)
    grad_norm = jnp.einsum(
        "thk,th->hk", feature_query, denominator_grad, precision=TOP_PRECISION
    ).reshape(flat_width)
    share_grad_kv, share_grad_norm = (
        lax.psum_scatter(gradient_key_value, ("height", "width"), scatter_dimension=0, tiled=True),
        lax.psum_scatter(grad_norm, ("height", "width"), scatter_dimension=0, tiled=True),
    )
    later = entering(
        (ends, share_grad_kv, share_grad_norm),
        "tm",
        carry_on,
        (zero_flag, jnp.zeros_like(share_grad_kv), jnp.zeros_like(share_grad_norm)),
        True,
    )
    part_grad_kv = share_grad_kv + (1.0 - ends) * later[1]
    part_grad_norm = share_grad_norm + (1.0 - ends) * later[2]
    total_key_value, norm_total = (
        lax.all_gather(part_grad_kv, ("height", "width"), axis=0, tiled=True),
        lax.all_gather(part_grad_norm, ("height", "width"), axis=0, tiled=True),
    )
    total_key_value = total_key_value.reshape(HEADS, HEAD_DIM, HEAD_DIM)
    norm_total = norm_total.reshape(HEADS, HEAD_DIM)
    key_feat_grad = (
        jnp.einsum(
            "dla,lja->dlj",
            value_row_block.astype(jnp.float32),
            total_key_value,
            precision=TOP_PRECISION,
        )
        + norm_total[None]
    )
    key_grad = (
        jnp.where(feature_keys > 0, key_feat_grad, 0.0)
        .reshape(attn_keys.shape)
        .astype(jnp.bfloat16)
    )
    value_gradient = jnp.einsum(
        "cob,obq->coq", feature_keys.astype(jnp.float32), total_key_value, precision=TOP_PRECISION
    )
    value_gradient = value_gradient.reshape(attn_values.shape).astype(jnp.bfloat16)
    return (query_grad, key_grad, value_gradient)


LANES = 128


def split_terms(value, count=2):
    terms = []
    for _ in range(count):
        terms.append(value.astype(jnp.bfloat16))
        value = value - terms[-1].astype(jnp.float32)
    return terms


def beside(*parts):
    return jnp.concatenate(parts, axis=1)


def dot_tokens(left, right):
    return lax.dot_general(left, right, (((0,), (0,)), ((), ())), preferred_element_type=jnp.float32)


def dot_rows(left, right):
    return lax.dot_general(left, right, (((1,), (0,)), ((), ())), preferred_element_type=jnp.float32)


def dot_columns(left, right):
    return lax.dot_general(left, right, (((1,), (1,)), ((), ())), preferred_element_type=jnp.float32)


def head_slice(ref, head):
    return ref[:, head * HEAD_DIM : (head + 1) * HEAD_DIM]


def tail_block(rows, first):
    column = lax.broadcasted_iota(jnp.int32, (rows, LANES - HEAD_DIM), 1)
    return jnp.where(column == 0, first, 0.0).astype(jnp.bfloat16)


def vmem_call(kernel, out_shape, scratch=(), smem_first=False, n_in=0, flops=0, bytes_accessed=0, vmem_mib=8, in_hbm=False, out_hbm=False, n_given=0):
    vmem = pl.BlockSpec(memory_space=pltpu.VMEM)
    in_specs = [pl.BlockSpec(memory_space=pltpu.HBM) if in_hbm else vmem] * n_in
    in_specs += [pl.BlockSpec(memory_space=pltpu.HBM)] * n_given
    if smem_first:
        in_specs[0] = pl.BlockSpec(memory_space=pltpu.SMEM)
    return pl.pallas_call(
        kernel,
        out_shape=out_shape,
        in_specs=in_specs,
        out_specs=jax.tree.map(lambda _: pl.BlockSpec(memory_space=pltpu.HBM) if out_hbm else vmem, out_shape),
        scratch_shapes=list(scratch),
        input_output_aliases={n_in: 0} if n_given else {},
        cost_estimate=pl.CostEstimate(flops=flops, bytes_accessed=bytes_accessed, transcendentals=0),
        compiler_params=pltpu.CompilerParams(vmem_limit_bytes=vmem_mib << 20),
    )


ROWS = 8
SPARE = LANES - HEAD_DIM
PIECES = HEAD_DIM // SPARE


def packed_tiles(tiles):
    return next(kept for kept in range(tiles + 1) if (tiles - kept) * PIECES - (-tiles // SPARE) <= kept)


def tile_of(at):
    return slice(at * ROWS, (at + 1) * ROWS)


def pack_rows(read, write, tiles):
    kept = packed_tiles(tiles)
    moved = (tiles - kept) * PIECES
    lane = lax.broadcasted_iota(jnp.int32, (ROWS, LANES), 1)
    rows = [read(at) for at in range(tiles)]
    for at in range(kept):
        block = rows[at]
        if at < moved:
            extra, piece = divmod(at, PIECES)
            shifted = pltpu.roll(rows[kept + extra], HEAD_DIM - SPARE * piece, 1)
            block = jnp.where(lane < HEAD_DIM, block, shifted)
        else:
            first = (at - moved) * SPARE
            for step in range(min(SPARE, tiles - first)):
                norm = rows[first + step]
                norm = pltpu.roll(norm, step, 1) if step else norm
                block = jnp.where(lane == HEAD_DIM + step, norm, block)
        write(at, block)


def unpack_rows(read, write, tiles):
    kept = packed_tiles(tiles)
    moved = (tiles - kept) * PIECES
    lane = lax.broadcasted_iota(jnp.int32, (ROWS, LANES), 1)
    rows = [read(at) for at in range(kept)]
    for at in range(tiles):
        if at < kept:
            block = rows[at]
        else:
            for piece in range(PIECES):
                shifted = pltpu.roll(rows[(at - kept) * PIECES + piece], SPARE * (piece + 1), 1)
                block = shifted if piece == 0 else jnp.where(lane < SPARE * piece, block, shifted)
        group, step = divmod(at, SPARE)
        norm = rows[moved + group]
        norm = pltpu.roll(norm, LANES - step, 1) if step else norm
        write(at, jnp.where(lane == HEAD_DIM, norm, block))


def store_into(ref, *index):
    def write(at, block):
        ref[(*index, tile_of(at))] = block

    return write


def unpack_into(state, index, packed):
    unpack_rows(lambda at: packed[tile_of(at)], store_into(state, index), state.shape[1] // ROWS)


PARTS = 4


def stage(sources, targets, sems):
    copies = []
    for at, (source, target) in enumerate(zip(sources, targets)):
        rows = source.shape[0] // PARTS
        for part in range(PARTS):
            span = pl.ds(part * rows, rows)
            copies.append(pltpu.make_async_copy(source.at[span], target.at[span], sems.at[at, part]))
    for copy in copies:
        copy.start()
    for copy in copies:
        copy.wait()


def state_kernel(key_hbm, value_hbm, keep_ref, send_ref, halves, key_ref, value_ref, sems):
    stage((key_hbm, value_hbm), (key_ref, value_ref), sems)
    tokens = key_ref.shape[0]
    one = tail_block(tokens, 1.0)
    half = halves.shape[2]
    per_group = HEADS // 2
    column = lax.axis_index("width")
    blocks = []
    for head in range(HEADS):
        feature = jnp.maximum(head_slice(key_ref, head), 0)
        wide = jnp.concatenate([head_slice(value_ref, head), one], axis=1)
        blocks.append(dot_tokens(feature, wide))
    for head in range(HEADS):
        group, place = divmod(head, per_group)
        store_rows(halves, group, place * HEAD_DIM, blocks[head], half)
    keep_ref[...] = halves[column]
    send_ref[...] = halves[1 - column]


def store_rows(halves, group, first, block, half):
    cut = min(max(half - first, 0), HEAD_DIM)
    if cut:
        index = (0, group) if group is not None else (0,)
        halves[(*index, slice(first, first + cut))] = block[:cut]
    if cut < HEAD_DIM:
        index = (1, group) if group is not None else (1,)
        start = first + cut - half
        halves[(*index, slice(start, start + HEAD_DIM - cut))] = block[cut:]


def pick_kernel(keep_ref, came_ref, mine_ref, other_ref):
    row = lax.axis_index("height")
    tiles = keep_ref.shape[1] // ROWS
    for out, at_row in ((mine_ref, row), (other_ref, 1 - row)):
        pack_rows(lambda at: keep_ref[at_row, tile_of(at)] + came_ref[at_row, tile_of(at)], store_into(out), tiles)


def write_masks(clip_ref, out_ref):
    frame = lax.axis_index("tm")
    last = lax.axis_size("tm") - 1
    here = clip_ref[frame]
    line = lax.broadcasted_iota(jnp.int32, out_ref.shape, 0)
    masks = jnp.zeros(out_ref.shape, jnp.float32)
    for at, (step, hop) in enumerate(((1, 1), (1, 2), (-1, 1), (-1, 2))):
        other = frame - step * hop
        inside = (other >= 0) & (other <= last)
        same = inside & (clip_ref[jnp.clip(other, 0, last)] == here)
        masks = jnp.where(line == at, jnp.where(same, 1.0, 0.0), masks)
    out_ref[...] = masks


def heads_kernel(query_hbm, cotangent_hbm, clip_hbm, mine_ref, other_ref, mask_ref, groups, query_ref, cotangent_ref, sems, clip_ref, clip_sem):
    clip_copy = pltpu.make_async_copy(clip_hbm, clip_ref, clip_sem)
    clip_copy.start()
    stage((query_hbm, cotangent_hbm), (query_ref, cotangent_ref), sems)
    clip_copy.wait()
    write_masks(clip_ref, mask_ref)
    none = tail_block(query_ref.shape[0], 0.0)
    per_group = HEADS // 2
    row = lax.axis_index("height")
    for head in range(HEADS):
        group, place = divmod(head, per_group)
        feature = jnp.maximum(head_slice(query_ref, head), 0)
        groups[group, 0, place] = jnp.concatenate([feature, none], axis=1)
        groups[group, 1, place] = jnp.concatenate([head_slice(cotangent_ref, head), none], axis=1)
    mine_ref[...] = groups[row]
    other_ref[...] = groups[1 - row]


def query_kernel(state_ref, came_ref, mine_ref, other_ref, keep_ref, send_ref, own_out, other_out, state, halves):
    column = lax.axis_index("width")
    half = state.shape[1]
    per_group = HEADS // 2
    tokens = mine_ref.shape[2]
    unpack_into(state, column, state_ref)
    unpack_into(state, 1 - column, came_ref)
    lane = lax.broadcasted_iota(jnp.int32, (2 * tokens, LANES), 1)
    places = range(per_group)
    features, cots, states, products = [], [], [], []
    pad = jnp.zeros((LANES - HEAD_DIM, LANES), jnp.bfloat16)
    for place in places:
        full = jnp.concatenate([mine_ref[0, place], other_ref[0, place]], axis=0)
        features.append(full[:, :HEAD_DIM])
        cots.append(jnp.concatenate([mine_ref[1, place], other_ref[1, place]], axis=0))
        high, low, rest = split_terms(load_rows(state, place * HEAD_DIM, half), 3)
        states.append((high, low, rest))
        product = dot_rows(beside(full, full), jnp.concatenate([high, pad, low, pad], axis=0))
        products.append(product + dot_rows(features[-1], rest))
    scaleds = []
    for place in places:
        cotangent = cots[place].astype(jnp.float32)
        product = products[place]
        inverse = 1.0 / (product[:, HEAD_DIM : HEAD_DIM + 1] + EPSILON)
        against = jnp.sum(cotangent * product, axis=1, keepdims=True)
        norm_grad = -(against * inverse) * inverse
        scaleds.append(split_terms(jnp.where(lane == HEAD_DIM, norm_grad, cotangent * inverse), 3))
    for place in places:
        both = dot_tokens(features[place], beside(*scaleds[place][:2]))
        store_rows(halves, None, place * HEAD_DIM, both[:, :LANES] + both[:, LANES:], half)
    for place in places:
        narrow, (high, low, rest) = features[place], states[place]
        first, second, third = scaleds[place]
        back = dot_columns(beside(first, third), beside(rest, high))
        back = back + dot_columns(beside(second, second), beside(high, low))
        back = back + dot_columns(beside(first, first), beside(high, low))
        back = jnp.where(narrow > 0, back, 0.0).astype(jnp.bfloat16)
        own_out[place, :, :HEAD_DIM] = back[:tokens]
        other_out[place, :, :HEAD_DIM] = back[tokens:]
    for out, part in ((keep_ref, column), (send_ref, 1 - column)):
        pack_rows(lambda at: halves[part, tile_of(at)], store_into(out), half // ROWS)


def load_rows(state, first, half):
    cut = min(max(half - first, 0), HEAD_DIM)
    parts = []
    if cut:
        parts.append(state[0, first : first + cut])
    if cut < HEAD_DIM:
        start = first + cut - half
        parts.append(state[1, start : start + HEAD_DIM - cut])
    return parts[0] if len(parts) == 1 else jnp.concatenate(parts, axis=0)


def key_heads(key_ref, value_ref, total, half, group, place, one):
    head = group * (HEADS // 2) + place
    feature = jnp.maximum(head_slice(key_ref, head), 0)
    wide = jnp.concatenate([head_slice(value_ref, head), one], axis=1)
    high, low = split_terms(load_rows(total, place * HEAD_DIM, half))
    grad = dot_columns(beside(wide, wide), beside(high, low))
    product = dot_rows(feature, high) + dot_rows(feature, low)
    return jnp.where(feature > 0, grad, 0.0).astype(jnp.bfloat16), product[:, :HEAD_DIM].astype(jnp.bfloat16)


def key_kernel(mine, key_ref, value_ref, here_ref, came_ref, *refs):
    column, row = lax.axis_index("width"), lax.axis_index("height")
    given, (key_out, value_out, total) = refs[:-3], refs[-3:]
    half = total.shape[1]
    unpack_into(total, column, here_ref)
    unpack_into(total, 1 - column, came_ref)
    one = tail_block(key_ref.shape[0], 1.0)
    for group in range(2):
        @pl.when(row == (group if mine else 1 - group))
        def _():
            places = range(HEADS // 2)
            grads = [key_heads(key_ref, value_ref, total, half, group, place, one) for place in places]
            for place in places:
                for at, out in enumerate((key_out, value_out)):
                    if mine:
                        out[place, :, :HEAD_DIM] = grads[place][at]
                        continue
                    for which, part in ((group, grads[place][at]), (1 - group, given[at][place, :, :HEAD_DIM])):
                        first = (which * (HEADS // 2) + place) * HEAD_DIM
                        out[:, first : first + HEAD_DIM] = part


def join_kernel(mine_ref, came_ref, out_ref):
    row = lax.axis_index("height")
    per_group = HEADS // 2
    for place in range(per_group):
        mine, came = mine_ref[place, :, :HEAD_DIM], came_ref[place, :, :HEAD_DIM]
        first = jnp.where(row == 0, mine, came)
        second = jnp.where(row == 0, came, mine)
        out_ref[:, place * HEAD_DIM : (place + 1) * HEAD_DIM] = first
        at = (per_group + place) * HEAD_DIM
        out_ref[:, at : at + HEAD_DIM] = second


def struct(shape, dtype=jnp.float32):
    return jax.ShapeDtypeStruct(shape, dtype)


SWAP = [(0, 1), (1, 0)]


def paired(queries, attn_keys, attn_values, attn_cotangent, clip_ids, hidden_pre, conv_weight):
    tokens = queries.shape[1] * queries.shape[2]
    flat = HEADS * HEAD_DIM
    per_group = HEADS // 2
    half = per_group * HEAD_DIM // 2
    frames = lax.axis_size("tm")
    query, key, value, cotangent = (
        part.reshape(tokens, flat) for part in (queries, attn_keys, attn_values, attn_cotangent)
    )
    share = struct((packed_tiles(half // ROWS) * ROWS, LANES))
    pair = struct((2, half, LANES))

    key_hbm, value_hbm = (
        pltpu.with_memory_space_constraint(part, pltpu.HBM) for part in (key, value)
    )
    staged = [pltpu.VMEM((tokens, flat), jnp.bfloat16)] * 2 + [pltpu.SemaphoreType.DMA((2, PARTS))]
    keep, send = vmem_call(
        state_kernel, (pair, pair), [pltpu.VMEM((2, 2, half, LANES), jnp.float32), *staged], n_in=2, in_hbm=True,
        flops=2 * tokens * flat * LANES, bytes_accessed=4 * tokens * flat + 8 * half * LANES * 2,
    )(key_hbm, value_hbm)
    hidden, send = lax.optimization_barrier((hidden_pre, send))
    edges = row_edges(hidden)
    came = lax.ppermute(send, "width", SWAP)
    came, edges = lax.optimization_barrier((came, edges))
    mine, other = vmem_call(pick_kernel, (share, share), n_in=2, bytes_accessed=24 * half * LANES)(keep, came)
    came = lax.ppermute(other, "height", SWAP)

    packed = struct((2, per_group, tokens, LANES), jnp.bfloat16)
    query, cotangent, hidden, _ = lax.optimization_barrier((query, cotangent, hidden, mine))
    heads_mine, heads_other, masks = vmem_call(
        heads_kernel,
        (packed, packed, struct((8, LANES))),
        [pltpu.VMEM((2, 2, per_group, tokens, LANES), jnp.bfloat16), *staged,
         pltpu.SMEM(clip_ids.shape, jnp.int32), pltpu.SemaphoreType.DMA],
        n_in=3, in_hbm=True, bytes_accessed=12 * tokens * flat,
    )(*(pltpu.with_memory_space_constraint(part, pltpu.HBM) for part in (query, cotangent, clip_ids)))
    side = side_edge(hidden[0])
    edges, _ = lax.optimization_barrier((edges, heads_other))
    halo = halo_arrays(edges, side)
    _, own = lax.optimization_barrier(((heads_other, side), mine + came))
    heads_sent = lax.ppermute(heads_other, "height", SWAP)

    def along_frames(own, step, meanwhile):
        moves = [[(at, at + step * hop) for at in range(frames) if 0 <= at + step * hop < frames] for hop in (1, 2)]
        hops = (1, 2) if step > 0 else (2, 1)
        sent = {hop: lax.ppermute(own, "tm", moves[hop - 1]) for hop in hops}
        near, far = sent[1], sent[2]
        near, far, others = meanwhile(own, near, far)
        at = 0 if step > 0 else 2
        return own + masks[at : at + 1] * near + masks[at + 1 : at + 2] * far, others

    def fetch(own, near, far):
        block, _ = lax.optimization_barrier((hidden_pre[0], own))
        near, far, kept = lax.optimization_barrier((near, far, (heads_sent, spread_block(block, conv_weight))))
        return near, far, kept

    state, (heads_came, spread_out) = along_frames(own, 1, fetch)
    came = lax.ppermute(state, "width", SWAP)
    back = struct((per_group, tokens, LANES), jnp.bfloat16)
    keep, send, back_mine, back_other = vmem_call(
        query_kernel, (share, share, back, back),
        [pltpu.VMEM((2, half, LANES), jnp.float32), pltpu.VMEM((2, half, LANES), jnp.float32)], n_in=4,
        flops=14 * tokens * flat * LANES, bytes_accessed=8 * tokens * flat,
    )(state, came, heads_mine, heads_came)
    came = lax.ppermute(send, "width", SWAP)
    own, halo = lax.optimization_barrier((keep + came, halo))

    def convolve(own, near, far):
        other, _ = lax.optimization_barrier((back_other, own))
        back_came = lax.ppermute(other, "height", SWAP)
        hidden_grad = ffn(hidden_pre, halo, spread_out)
        query_grad = vmem_call(
            join_kernel, struct((tokens, flat), jnp.bfloat16), n_in=2, bytes_accessed=4 * tokens * flat
        )(back_mine, back_came)
        far, near, hidden_grad = lax.optimization_barrier((far, near, hidden_grad))
        return near, far, (query_grad, hidden_grad)

    total, (query_grad, hidden_grad) = along_frames(own, -1, convolve)
    far = lax.ppermute(total, "height", SWAP)
    near_came = lax.ppermute(total, "width", SWAP)
    state = [pltpu.VMEM((2, half, LANES), jnp.float32)]
    cost = {"flops": 4 * tokens * flat * LANES, "bytes_accessed": 4 * tokens * flat}
    near_grads = vmem_call(functools.partial(key_kernel, True), (back, back), state, n_in=4, **cost)(
        key, value, total, near_came
    )
    far, query_grad = lax.optimization_barrier((far, query_grad))
    far_came = lax.ppermute(far, "width", SWAP)
    out = struct((tokens, flat), jnp.bfloat16)
    key_grad, value_gradient = vmem_call(functools.partial(key_kernel, False), (out, out), state, n_in=6, **cost)(
        key, value, far, far_came, *near_grads
    )
    grads = tuple(part.reshape(queries.shape) for part in (query_grad, key_grad, value_gradient))
    return (*grads, hidden_grad)


def mixed_ffn(hidden_pre, conv_weight):
    row_count = hidden_pre.shape[1]
    col_count = hidden_pre.shape[2]
    split_at = hidden_pre.shape[3] // 2
    widened = padded(hidden_pre, (("height", 1), ("width", 2)), 2)[0]
    conv_out = depthwise(widened, conv_weight, 1, 1, row_count + 2, col_count + 2)
    row_global = lax.axis_index("height") * row_count + jnp.arange(row_count + 2) - 1
    col_global = lax.axis_index("width") * col_count + jnp.arange(col_count + 2) - 1
    row_inside = (row_global >= 0) & (row_global < row_count * lax.axis_size("height"))
    col_inside = (col_global >= 0) & (col_global < col_count * lax.axis_size("width"))
    inside = (row_inside[:, None] & col_inside[None, :]).astype(jnp.float32)
    conv_grad = glu_grad(conv_out, split_at) * inside[:, :, None]
    hidden_grad = depthwise(conv_grad, conv_weight, 1, -1, row_count, col_count)
    hidden_grad = hidden_grad[None].astype(jnp.bfloat16)
    return hidden_grad


TILES = 8
REACH = 2
UNROLL = 8


def spread(load, refs, offsets, count, start, length):
    for ref, offset in zip(refs, offsets):
        for tile in range(count):
            part = load(slice((offset + tile) * LANES, (offset + tile + 1) * LANES)).astype(jnp.float32)
            ref[pl.ds(start + tile, length, stride=TILES), :] = part


def spread_kernel(block_ref, weight_ref, source, taps):
    rows, cols, channels = block_ref.shape
    lane_tiles = channels // LANES // 2
    pitch = -(-lane_tiles // TILES) * TILES
    wide = cols + 2 * REACH
    for tile in range(lane_tiles):
        for place, at in ((tile, tile), (pitch + tile, lane_tiles + tile)):
            taps[pl.ds(place, 9, stride=2 * pitch), :] = weight_ref[:, at * LANES : (at + 1) * LANES]

    @pl.loop(0, rows)
    def _(at):
        start = pl.multiple_of(((at + REACH) * wide + REACH) * TILES, TILES)
        for base in range(0, lane_tiles, TILES):
            refs = source.at[base // TILES, 0], source.at[base // TILES, 1]
            count = min(TILES, lane_tiles - base)
            spread(lambda lanes: block_ref[at, :, lanes], refs, (base, lane_tiles + base), count, start, cols)


def conv_kernel(row_refs, *refs):
    halo_rows, refs = refs[:row_refs], refs[row_refs:]
    side_ref, refs = refs[0], refs[1:]
    corners, refs = refs[:row_refs], refs[row_refs:]
    _, taps, out_hbm, source, value_grad, gate_grad, *results, out_ref, sems = refs
    rows, cols, channels = out_ref.shape
    lane_tiles = channels // LANES // 2
    pitch = -(-lane_tiles // TILES) * TILES
    row, column = lax.axis_index("height"), lax.axis_index("width")
    first_row, last_row = row == 0, row == lax.axis_size("height") - 1
    wide, tall = cols + 2 * REACH, rows + 2 * REACH
    grad_wide = wide - 2

    def source_at(at_row, at_col):
        return pl.multiple_of((at_row * wide + at_col) * TILES, TILES)

    def grad_at(at_row, at_col):
        return pl.multiple_of((at_row * grad_wide + at_col) * TILES, TILES)

    zero = jnp.zeros((TILES, LANES), jnp.float32)
    outer_col = jnp.where(column == 0, 0, cols + REACH)
    side_col = jnp.where(column == 0, cols + REACH, 0)
    grad_outer_col = jnp.where(column == 0, 0, grad_wide - 1)
    start_col = jnp.where(column == 0, REACH, REACH - 1)
    low, high = jnp.where(first_row, REACH, REACH - 1), jnp.where(last_row, rows + REACH, rows + REACH + 1)

    for ref in (value_grad, gate_grad):
        @pl.loop(0, rows + 2)
        def _(at):
            ref[pl.ds(grad_at(at, grad_outer_col), TILES), :] = zero

        for edge, at in ((first_row, 0), (last_row, rows + 1)):
            @pl.when(edge)
            def _():
                for col in range(grad_wide):
                    ref[pl.ds(grad_at(at, col), TILES), :] = zero

    copies = []
    for base in range(0, lane_tiles, TILES):
        count = min(TILES, lane_tiles - base)
        value_in, gate_in = source.at[base // TILES, 0], source.at[base // TILES, 1]
        offsets = base, lane_tiles + base

        @pl.loop(0, rows)
        def _(at):
            spread(
                lambda lanes: side_ref[at, :, lanes], (value_in, gate_in), offsets, count,
                source_at(at + REACH, side_col), REACH,
            )
            for ref in (value_in, gate_in):
                for extra in range(REACH):
                    ref[pl.ds(source_at(at + REACH, outer_col + extra), TILES), :] = zero

        for edge, at, which in ((first_row, 0, 0), (last_row, rows + REACH, row_refs - 1)):
            rows_ref, corner_ref = halo_rows[which], corners[which]
            for extra in range(REACH):
                @pl.when(jnp.logical_not(edge))
                def _():
                    for ref, col, length in ((rows_ref, REACH, cols), (corner_ref, side_col, REACH)):
                        spread(
                            lambda lanes: ref[extra, :, lanes], (value_in, gate_in), offsets, count,
                            source_at(at + extra, col), length,
                        )
                    for ref in (value_in, gate_in):
                        for side in range(REACH):
                            ref[pl.ds(source_at(at + extra, outer_col + side), TILES), :] = zero

                @pl.when(edge)
                def _():
                    for ref in (value_in, gate_in):
                        for col in range(wide):
                            ref[pl.ds(source_at(at + extra, col), TILES), :] = zero

        def weights(offset):
            return [taps[2 * pitch * tap + offset + base : 2 * pitch * tap + offset + base + TILES, :] for tap in range(9)]

        value_taps, gate_taps = weights(0), weights(pitch)

        def conv_row(at):
            cache = {}

            def read(ref, a, col):
                if (id(ref), a, col) not in cache:
                    cache[id(ref), a, col] = ref[pl.ds(source_at(at + a, start_col + col), TILES), :]
                return cache[id(ref), a, col]

            for col in range(cols + 1):
                def conv(ref, kernel):
                    total = None
                    for a in (-1, 0, 1):
                        for b in (-1, 0, 1):
                            term = kernel[3 * (a + 1) + b + 1] * read(ref, a, col + b)
                            total = term if total is None else total + term
                    return total

                value, gate = conv(value_in, value_taps), conv(gate_in, gate_taps)
                squash = jax.nn.sigmoid(gate)
                gated = gate * squash
                glu = value * gated
                place = pl.ds(grad_at(at - 1, start_col + col - 1), TILES)
                value_grad[place, :] = glu * gated
                gate_grad[place, :] = glu * value * (squash + gated * (1.0 - squash))

        steps = 3 if lax.axis_size("height") == 2 and (rows + 1) % 3 == 0 else 1

        @pl.loop(0, (rows + 1) // 3 if steps == 3 else high - low)
        def _(trip):
            for step in range(steps):
                conv_row(low + trip * steps + step)

        def gather(at, results):
            cache = {}

            def read(ref, a, col):
                if (id(ref), a, col) not in cache:
                    cache[id(ref), a, col] = ref[pl.ds(grad_at(at + a, col), TILES), :]
                return cache[id(ref), a, col]

            for col in range(cols):
                for ref, kernel, result in zip((value_grad, gate_grad), (value_taps, gate_taps), results):
                    total = None
                    for a in (-1, 0, 1):
                        for b in (-1, 0, 1):
                            term = kernel[3 * (a + 1) + b + 1] * read(ref, 1 - a, col + 1 - b)
                            total = term if total is None else total + term
                    result[pl.ds(col, TILES, stride=cols), :] = total

        def settle(at, results):
            for result, offset in zip(results, (base, lane_tiles + base)):
                for tile in range(count):
                    lanes = slice((offset + tile) * LANES, (offset + tile + 1) * LANES)
                    out_ref[at, :, lanes] = result[tile * cols : (tile + 1) * cols, :].astype(jnp.bfloat16)

        @pl.loop(0, rows // UNROLL)
        def _(at):
            for step in range(UNROLL):
                gather(at * UNROLL + step, results[2 * step : 2 * step + 2])
                if step:
                    settle(at * UNROLL + step - 1, results[2 * step - 2 : 2 * step])
            settle(at * UNROLL + UNROLL - 1, results[2 * UNROLL - 2 :])

        for at, offset in enumerate((base, lane_tiles + base)):
            lanes = pl.ds(offset * LANES, count * LANES)
            copy = pltpu.make_async_copy(out_ref.at[:, :, lanes], out_hbm.at[:, :, lanes], sems.at[at, base // TILES])
            copy.start()
            copies.append(copy)
    for copy in copies:
        copy.wait()


def edge_slice(block, dim, low_side):
    start = jnp.where(low_side, 0, block.shape[dim] - REACH)
    return lax.dynamic_slice_in_dim(block, start, REACH, axis=dim)


def row_edges(hidden_pre):
    block = hidden_pre[0]
    if lax.axis_size("height") == 2:
        return [edge_slice(block, 0, lax.axis_index("height") == 1)]
    return [block[block.shape[0] - REACH :], block[:REACH]]


def side_edge(block):
    return edge_slice(block, 1, lax.axis_index("width") == 1)


def halo_arrays(edges, side):
    height = lax.axis_size("height")
    if height == 2:
        moves = [SWAP]
    else:
        moves = [[(at, at + 1) for at in range(height - 1)], [(at + 1, at) for at in range(height - 1)]]
    halo_rows = [lax.ppermute(edge, "height", move) for edge, move in zip(edges, moves)]
    side = lax.ppermute(side, "width", SWAP)
    corners = [lax.ppermute(side_edge(part), "width", SWAP) for part in halo_rows]
    return halo_rows, side, corners


def spread_block(block, conv_weight):
    rows, cols, channels = block.shape
    chunks = -(-channels // LANES // 2 // TILES)
    size = (rows + 2 * REACH) * (cols + 2 * REACH) * TILES
    return vmem_call(
        spread_kernel,
        (struct((chunks, 2, size, LANES)), struct((9 * 2 * chunks * TILES, LANES))),
        n_in=2, flops=rows * cols * channels, bytes_accessed=rows * cols * channels,
    )(block, conv_weight)


def ffn(hidden_pre, halo, spread_out):
    halo_rows, side, corners = halo
    rows, cols, channels = hidden_pre.shape[1:]
    source, taps = spread_out
    chunks = source.shape[0]
    vmem, hbm = pl.BlockSpec(memory_space=pltpu.VMEM), pl.BlockSpec(memory_space=pltpu.HBM)
    grad = pltpu.VMEM(((rows + 2) * (cols + 2) * TILES, LANES), jnp.float32)
    result = pltpu.VMEM((cols * TILES, LANES), jnp.float32)
    size = rows * cols * channels
    hidden_grad, _ = pl.pallas_call(
        functools.partial(conv_kernel, len(halo_rows)),
        out_shape=(struct((rows, cols, channels), jnp.bfloat16), struct(source.shape)),
        in_specs=[vmem] * (2 * len(halo_rows) + 3),
        out_specs=(hbm, vmem),
        scratch_shapes=[
            grad, grad, *[result] * (2 * UNROLL),
            pltpu.VMEM((rows, cols, channels), jnp.bfloat16), pltpu.SemaphoreType.DMA((2, chunks)),
        ],
        input_output_aliases={2 * len(halo_rows) + 1: 1},
        cost_estimate=pl.CostEstimate(flops=2 * size, bytes_accessed=size, transcendentals=0),
        compiler_params=pltpu.CompilerParams(vmem_limit_bytes=8 << 20),
    )(*halo_rows, side, *corners, source, taps)
    return hidden_grad[None]


def per_device(queries, attn_keys, attn_values, attn_cotangent, clip_ids, hidden_pre, conv_weight):
    blocked = lax.axis_size("width") == 2 and hidden_pre.shape[0] == 1 and hidden_pre.shape[3] % (2 * LANES) == 0
    pairs = lax.axis_size("height") == 2 and 3 <= lax.axis_size("tm") <= 4 and HEADS % 2 == 0
    if blocked and pairs:
        return paired(queries, attn_keys, attn_values, attn_cotangent, clip_ids, hidden_pre, conv_weight)
    grads = general_attention(queries, attn_keys, attn_values, attn_cotangent, clip_ids)
    if blocked:
        halo = halo_arrays(row_edges(hidden_pre), side_edge(hidden_pre[0]))
        return (*grads, ffn(hidden_pre, halo, spread_block(hidden_pre[0], conv_weight)))
    return (*grads, mixed_ffn(hidden_pre, conv_weight))


def solution(mesh):
    return jax.shard_map(
        per_device,
        mesh=mesh,
        in_specs=(
            P(("group", "tm"), "height", "width", None),
            P(("group", "tm"), "height", "width", None),
            P(("group", "tm"), "height", "width", None),
            P(("group", "tm"), "height", "width", None),
            P("group"),
            P(("group", "tm"), "height", "width", None),
            P(),
        ),
        out_specs=(
            P(("group", "tm"), "height", "width", None),
            P(("group", "tm"), "height", "width", None),
            P(("group", "tm"), "height", "width", None),
            P(("group", "tm"), "height", "width", None),
        ),
        check_vma=False,
    )
```
